32 devices in a mesh: dp: 8 (over z, core), fsdp: 4 (over y, x).
Axes of the slice: x: 2, y: 2, z: 4, core: 2. Of those that a mesh axis runs over, the one named last changes fastest.
Arguments:
- hidden_in: bfloat16 [32, 256, 2048], P(('dp', 'fsdp')), may hold values from -48 to 48
- segment_ids: int32 [32, 256], P(('dp', 'fsdp')), may hold values from 0 to 2, never falling along the last dimension, each value on 1 to 128 neighbouring positions
- valid_mask: int32 [32, 256], P(('dp', 'fsdp')), may hold values from 0 to 1, as said below
- cotangent: bfloat16 [32, 256, 2048], P(('dp', 'fsdp')), may hold values from -6 to 6
- norm_attn: bfloat16 [2048], P('fsdp'), may hold values from 0.099609375 to 1.8984375
- w_query: bfloat16 [2048, 2048], P('fsdp'), may hold values from -0.4375 to 0.4375
- w_key: bfloat16 [2048, 512], P('fsdp'), may hold values from -0.4375 to 0.4375
- w_value: bfloat16 [2048, 512], P('fsdp'), may hold values from -0.125 to 0.125
- w_output: bfloat16 [2048, 2048], P('fsdp'), may hold values from -1.5 to 1.5
- norm_mlp: bfloat16 [2048], P('fsdp'), may hold values from 0.099609375 to 1.8984375
- w_gate: bfloat16 [2048, 8192], P('fsdp'), may hold values from -0.125 to 0.125
- w_up: bfloat16 [2048, 8192], P('fsdp'), may hold values from -0.125 to 0.125
- w_down: bfloat16 [8192, 2048], P('fsdp'), may hold values from -0.375 to 0.375
Outputs:
- hidden_out: bfloat16 [32, 256, 2048], P(('dp', 'fsdp'))
- input_grad: bfloat16 [32, 256, 2048], P(('dp', 'fsdp'))
- norm_attn_grad: float32 [2048], P('fsdp')
- w_query_grad: float32 [2048, 2048], P('fsdp')
- w_key_grad: float32 [2048, 512], P('fsdp')
- w_value_grad: float32 [2048, 512], P('fsdp')
- w_output_grad: float32 [2048, 2048], P('fsdp')
- norm_mlp_grad: float32 [2048], P('fsdp')
- w_gate_grad: float32 [2048, 8192], P('fsdp')
- w_up_grad: float32 [2048, 8192], P('fsdp')
- w_down_grad: float32 [8192, 2048], P('fsdp')
- statistics: float32 [5], replicated
The draws below stay inside these ranges and needn't reach their ends.
Inputs may be any that keep to these rules, and one draw needn't show every extreme that they name: `segment_ids`: segment numbers start at 0 in each sequence and never fall; each of the 3 documents has 1 to 128 tokens. `valid_mask`: each sequence ends in a tail of 1 to 64 padded tokens marked 0; all others are 1.
All inputs are finite; a program needn't handle non-finite values.
Results may differ from the reference program's by a relative error of at most 0.015.
Values may be sent and summed in bfloat16 or wider, within the bound.
A program may use at most 576 MiB of HBM per device.

```python
import math
import jax
import jax.numpy as jnp
import numpy as np
from jax import lax

D = 2048
H = 32
KV = 8
HD = 64
FF = 8192
SEQ = 256
DOCS = 3
SEQS = 32


def draw_hidden_in(key, part):
    key = jax.random.fold_in(key, 7)
    base_key, row_key, col_key = jax.random.split(key, 3)
    base_draw = jnp.clip(jax.random.normal(base_key, (SEQS, SEQ, D), jnp.float32), -4.0, 4.0)
    row_scale = jnp.exp(jax.random.uniform(row_key, (SEQS, SEQ, 1), jnp.float32, -0.8, 0.8))
    col_scale = jnp.exp(jax.random.uniform(col_key, (1, 1, D), jnp.float32, -1.15, 1.15))
    rising = 0.5 + jnp.arange(SEQS, dtype=jnp.float32)[:, None, None] / max(SEQS - 1, 1)
    return (base_draw * row_scale * col_scale * rising).astype(jnp.bfloat16)


def draw_valid_mask(key, part):
    key = jax.random.fold_in(key, 11)
    tail_size = jax.random.randint(key, (SEQS, 1), 1, SEQ // 4 + 1)
    positions = jnp.arange(SEQ, dtype=jnp.int32)[None, :]
    return (positions < SEQ - tail_size).astype(jnp.int32)


def block_scale(rng, shape, cuts, least, top_value):
    gain = 1.0
    for axis_at, parts in cuts:
        heights = jax.random.uniform(jax.random.fold_in(jax.random.fold_in(rng, 6), axis_at), (parts,), jnp.float32, least / len(cuts), top_value / len(cuts))
        gain = gain * jnp.repeat(jnp.exp(heights), shape[axis_at] // parts).reshape((-1,) + (1,) * (len(shape) - 1 - axis_at))
    return gain


def length_profile(count, total, most, lean):
    portions = [(1 << 20) // math.isqrt(standing ** lean) + 1 for standing in range(2, count + 1)]
    spare, holding = total - most - (count - 1), [1] * (count - 1)
    while spare > 0:
        movable = [i for i in range(count - 1) if holding[i] < most]
        whole, budget = sum([portions[i] for i in movable]), spare
        for i in movable:
            more = min(most - holding[i], max(1, budget * portions[i] // whole), spare)
            holding[i] = holding[i] + more
            spare = spare - more
    return np.array([most] + holding)


def ragged_sizes(key, number_of, total, most, skew):
    if number_of == 2:
        one = jax.random.randint(key, (), max(1, total - most), min(most, total - 1) + 1)
        return jnp.stack([one, total - one])
    lengths = jnp.asarray(length_profile(number_of, total, most, skew), jnp.int32)
    couples = (number_of - 1) // 2
    donor, taker = lengths[1:1 + 2 * couples:2], lengths[2:2 + 2 * couples:2]
    slack = jnp.minimum(donor - 1, most - taker)
    moved = jax.random.randint(jax.random.fold_in(key, 1), (couples,), 0, 1 << 20) % (slack + 1)
    lengths = lengths.at[1:1 + 2 * couples:2].set(donor - moved).at[2:2 + 2 * couples:2].set(taker + moved)
    return lengths[jax.random.permutation(jax.random.fold_in(key, 2), number_of)]


def centred(own_key, dims, scale, reach, cuts=(), held_as=jnp.bfloat16):
    level = block_scale(own_key, dims, cuts, -0.22, 0.18) if cuts else 1.0
    drawn = jax.random.normal(own_key, dims, jnp.float32) * scale * level
    return jnp.minimum(jnp.maximum(drawn, -reach), reach).astype(held_as)


def setup_inputs(seed: int = 0) -> dict:
    splits = jax.random.split(jax.random.key(seed), 14)
    hidden_in = draw_hidden_in(jax.random.fold_in(splits[13], 71), 0)
    segment_ids = jax.vmap(lambda own: jnp.searchsorted(jnp.cumsum(ragged_sizes(own, DOCS, SEQ, SEQ // 2, 0)), jnp.arange(SEQ), side="right"))(jax.random.split(splits[1], SEQS)).reshape((SEQS, SEQ)).astype(jnp.int32)
    valid_mask = draw_valid_mask(jax.random.fold_in(splits[13], 71), 0)
    cotangent = centred(splits[3], (SEQS, SEQ, D), 1.0, 6.0, ((0, 32),))
    norm_attn = jnp.clip(1.0 + 0.18 * jax.random.normal(splits[4], (D,), jnp.float32), 0.099609375, 1.8984375).astype(jnp.bfloat16)
    w_query = centred(splits[5], (D, H * HD), (D // 12) ** -0.5, 0.4375, ((0, 4),))
    w_key = centred(splits[6], (D, KV * HD), (D // 12) ** -0.5, 0.4375, ((0, 4),))
    w_value = centred(splits[7], (D, KV * HD), D ** -0.5, 0.125, ((0, 4),))
    w_output = centred(splits[8], (H * HD, D), (H * HD // 128) ** -0.5, 1.5, ((0, 4),))
    norm_mlp = jnp.clip(1.0 + 0.18 * jax.random.normal(splits[9], (D,), jnp.float32), 0.099609375, 1.8984375).astype(jnp.bfloat16)
    w_gate = centred(splits[10], (D, FF), D ** -0.5, 0.125, ((0, 4),))
    w_up = centred(splits[11], (D, FF), D ** -0.5, 0.125, ((0, 4),))
    w_down = centred(splits[12], (FF, D), (FF // 32) ** -0.5, 0.375, ((0, 4),))
    return {"hidden_in": hidden_in, "segment_ids": segment_ids, "valid_mask": valid_mask, "cotangent": cotangent, "norm_attn": norm_attn, "w_query": w_query, "w_key": w_key, "w_value": w_value, "w_output": w_output, "norm_mlp": norm_mlp, "w_gate": w_gate, "w_up": w_up, "w_down": w_down}


EPSILON = 1e-05
RESIDUAL_SCALE = 0.22
SCORE_SCALE = 1.0 / 64.0
MASKED_SCORE = -1e+30
ROPE_BASE = 10000000.0
HIGHEST_MODE = lax.Precision.HIGHEST

@jax.custom_vjp
def low(v):
    return lax.optimization_barrier(v.astype(jnp.bfloat16)).astype(jnp.float32)

@jax.custom_vjp
def low_back(v):
    return v

def low_keep(v):
    return (low(v), None)

def low_pass(kept, grad):
    return (grad,)

def back_keep(v):
    return (v, None)

def back_low(kept, grad):
    return (low(grad),)
low.defvjp(low_keep, low_pass)
low_back.defvjp(back_keep, back_low)

def rope_tables(length, head_size):
    half_size = head_size // 2
    frequency = ROPE_BASE ** (-(jnp.arange(half_size, dtype=jnp.float32) * 2.0 / head_size))
    angles = jnp.arange(length, dtype=jnp.float32)[:, None] * frequency[None, :]
    return (jnp.cos(angles), jnp.sin(angles))

def rotate(tensor, cos_table, sin_table):
    half_size = tensor.shape[-1] // 2
    front_half = tensor[..., :half_size]
    back_half = tensor[..., half_size:]
    return jnp.concatenate([front_half * cos_table - back_half * sin_table, back_half * cos_table + front_half * sin_table], axis=-1)

def allowed_of(segments, validity):
    length = segments.shape[0]
    row_index = jnp.arange(length, dtype=jnp.int32)[:, None]
    col_index = jnp.arange(length, dtype=jnp.int32)[None, :]
    same_doc = segments[:, None] == segments[None, :]
    return same_doc & (col_index <= row_index) & ((validity[None, :] == 1) | (col_index == row_index))

def attend(pieces):
    queries_in, keys_in, values_in, segments, validity = pieces
    length = queries_in.shape[0]
    groups = queries_in.shape[1] // keys_in.shape[1]
    grouped = queries_in.reshape(length, keys_in.shape[1], groups, queries_in.shape[2])
    scores = low_back(SCORE_SCALE * jnp.einsum('tkgd,ukd->kgtu', grouped, keys_in, precision=HIGHEST_MODE))
    scores = jnp.where(allowed_of(segments, validity)[None, None], scores, MASKED_SCORE)
    row_max = lax.optimization_barrier(jnp.max(scores, axis=-1, keepdims=True))
    shifted = jnp.exp(scores - row_max)
    weights_att = low(shifted / lax.optimization_barrier(jnp.sum(shifted, axis=-1, keepdims=True)))
    combined = jnp.einsum('kgtu,ukd->tkgd', weights_att, values_in, precision=HIGHEST_MODE)
    return combined.reshape(length, queries_in.shape[1] * queries_in.shape[2])

def project(source, weight_mat):
    return jnp.einsum('bsd,df->bsf', source, weight_mat, precision=HIGHEST_MODE)

def layer_math(hidden, params, segments, validity):
    gain_attn, w_query, w_key, w_value, w_output, gain_mlp, w_gate, w_up, w_down = params
    batch_rows = hidden.shape[0]
    cos_table, sin_table = rope_tables(SEQ, HD)
    cos_table = cos_table[None, :, None, :]
    sin_table = sin_table[None, :, None, :]
    scale_one = lax.rsqrt(lax.optimization_barrier(jnp.mean(hidden * hidden, axis=-1, keepdims=True)) + EPSILON)
    normed_one = low(hidden * scale_one * gain_attn)
    query_pre = low_back(project(normed_one, w_query))
    key_pre = low_back(project(normed_one, w_key))
    values = low(low_back(project(normed_one, w_value)))
    queries = low(rotate(query_pre.reshape(batch_rows, SEQ, H, HD), cos_table, sin_table))
    keys = low(rotate(key_pre.reshape(batch_rows, SEQ, KV, HD), cos_table, sin_table))
    attended = lax.map(jax.checkpoint(attend), (queries, keys, values.reshape(batch_rows, SEQ, KV, HD), segments, validity))
    attended = low(low_back(attended))
    attn_branch = low_back(project(attended, w_output))
    middle = hidden + RESIDUAL_SCALE * attn_branch
    scale_two = lax.rsqrt(lax.optimization_barrier(jnp.mean(middle * middle, axis=-1, keepdims=True)) + EPSILON)
    normed_two = low(middle * scale_two * gain_mlp)
    gate_proj = low_back(project(normed_two, w_gate))
    up_proj = low_back(project(normed_two, w_up))
    mixed_act = low(jax.nn.silu(gate_proj) * up_proj)
    mlp_branch = low_back(project(mixed_act, w_down))
    result = middle + RESIDUAL_SCALE * mlp_branch
    keep_mask = validity.astype(jnp.float32)[..., None]
    squares = jnp.stack([jnp.sum(tensor * tensor * keep_mask) for tensor in (hidden, middle, result, attn_branch, mlp_branch)])
    return (result, squares)

def reference(hidden_in, segment_ids, valid_mask, cotangent, norm_attn, w_query, w_key, w_value, w_output, norm_mlp, w_gate, w_up, w_down):
    params = tuple((weight_in.astype(jnp.float32) for weight_in in (norm_attn, w_query, w_key, w_value, w_output, norm_mlp, w_gate, w_up, w_down)))
    group_size = math.gcd(SEQS, max(1, 4096 // SEQ))
    block_count = SEQS // group_size

    def shaped(array_in):
        return array_in.reshape((block_count, group_size) + array_in.shape[1:])

    def advance(state_now, pieces):
        gradients, squares = state_now
        hidden_block, segment_block, valid_block, cot_block = pieces
        result, pullback, block_squares = jax.vjp(lambda hidden, weights: layer_math(hidden, weights, segment_block, valid_block), hidden_block.astype(jnp.float32), params, has_aux=True)
        hidden_grad, weight_grads = pullback(cot_block.astype(jnp.float32))
        gradients = jax.tree.map(lambda running, addend: running + addend, gradients, weight_grads)
        return ((gradients, squares + block_squares), (result.astype(jnp.bfloat16), hidden_grad.astype(jnp.bfloat16)))
    initial = tuple((jnp.zeros_like(weight_in) for weight_in in params))
    (gradients, squares), (outputs, input_grads) = lax.scan(advance, (initial, jnp.zeros((5,), jnp.float32)), (shaped(hidden_in), shaped(segment_ids), shaped(valid_mask), shaped(cotangent)))
    valid_count = jnp.sum(valid_mask.astype(jnp.float32))
    statistics = jnp.sqrt(squares / (valid_count * D))
    return (outputs.reshape(hidden_in.shape), input_grads.reshape(hidden_in.shape), gradients[0], gradients[1], gradients[2], gradients[3], gradients[4], gradients[5], gradients[6], gradients[7], gradients[8], statistics)
```

```python
import jax
import jax.numpy as jnp
from jax import lax
from jax.sharding import Mesh
from jax.sharding import PartitionSpec as P

H = 32
KV = 8
HD = 64
GROUPS = H // KV

EPSILON = 1e-05
RESIDUAL_SCALE = 0.22
SCORE_SCALE = 1.0 / 64.0
MASKED_SCORE = -1e30
ROPE_BASE = 10000000.0

BF16 = jnp.bfloat16
F32 = jnp.float32


def rope_tables(length, head_size):
    half_size = head_size // 2
    frequency = ROPE_BASE ** (-(jnp.arange(half_size, dtype=F32) * 2.0 / head_size))
    angles = jnp.arange(length, dtype=F32)[:, None] * frequency[None, :]
    return (jnp.cos(angles), jnp.sin(angles))


def rotate(tensor, cos_table, sin_table):
    half_size = tensor.shape[-1] // 2
    front_half = tensor[..., :half_size]
    back_half = tensor[..., half_size:]
    return jnp.concatenate(
        [
            front_half * cos_table - back_half * sin_table,
            back_half * cos_table + front_half * sin_table,
        ],
        axis=-1,
    )


def dot_f32(left, right):
    return jnp.dot(left, right, preferred_element_type=F32)


def contract_rows(left, right):
    return jnp.einsum("sa,sb->ab", left, right, preferred_element_type=F32)


def contract_cols(left, right):
    return jnp.einsum("sb,ab->sa", left, right, preferred_element_type=F32)


def row_scale(source):
    return lax.rsqrt(jnp.mean(source * source, axis=-1, keepdims=True) + EPSILON)


def norm_backward(grad_norm, scale_row, unit_rows, gain):
    gain_grad = jnp.sum(grad_norm * unit_rows, axis=0)
    scaled = grad_norm * gain
    source_grad = scale_row * (
        scaled - unit_rows * jnp.mean(scaled * unit_rows, axis=-1, keepdims=True)
    )
    return (gain_grad, source_grad)


def gather_tokens(block):
    return lax.all_gather(block, ("sub", "fsdp"), axis=0, tiled=True)


def scatter_tokens(partial):
    return lax.psum_scatter(partial, ("sub", "fsdp"), scatter_dimension=0, tiled=True)


def column_blocks(weight, owners, subs):
    rows, columns = weight.shape
    blocked = weight.reshape(rows, owners, subs, columns // (owners * subs))
    mine = lax.dynamic_index_in_dim(blocked, lax.axis_index("sub"), axis=2, keepdims=False)
    return jnp.swapaxes(mine, 0, 1)


def regroup_columns(weights, owners, subs):
    blocks = jnp.concatenate([column_blocks(w, owners, subs) for w in weights], axis=-1)
    moved = lax.all_to_all(blocks, "fsdp", split_axis=0, concat_axis=0, tiled=True)
    return moved.reshape(-1, moved.shape[-1])


def row_block(weight, subs):
    rows = weight.shape[0] // subs
    return lax.dynamic_slice_in_dim(weight, lax.axis_index("sub") * rows, rows, axis=0)


def finish_rows(term):
    piece = lax.psum_scatter(term, "rep", scatter_dimension=0, tiled=True)
    spread = lax.all_gather(piece, ("rep", "sub"), axis=0, tiled=False)
    rep, subs = lax.axis_size("rep"), lax.axis_size("sub")
    spread = spread.reshape((rep, subs) + piece.shape)
    return jnp.swapaxes(spread, 0, 1).reshape(-1, piece.shape[-1]).astype(F32)


def finish_columns(term, widths):
    owners, rep, subs = lax.axis_size("fsdp"), lax.axis_size("rep"), lax.axis_size("sub")
    rows, columns = term.shape
    blocked = jnp.swapaxes(term.reshape(owners, rep, rows // (owners * rep), columns), 0, 1)
    blocked = blocked.reshape(rows, columns)
    piece = lax.psum_scatter(blocked, "rep", scatter_dimension=0, tiled=True)
    piece = piece.reshape(owners, -1, columns)
    moved = lax.all_to_all(piece, "fsdp", split_axis=0, concat_axis=0, tiled=True)
    spread = lax.all_gather(moved, ("rep", "sub"), axis=0, tiled=False)
    spread = spread.reshape((rep, subs) + moved.shape)
    outs = []
    at = 0
    for width in widths:
        part = lax.slice_in_dim(spread, at, at + width, axis=4)
        part = jnp.transpose(part, (0, 3, 2, 1, 4))
        outs.append(part.reshape(rep * moved.shape[1], owners * subs * width).astype(F32))
        at += width
    return outs


def shards(
    hidden_in,
    segment_ids,
    valid_mask,
    cotangent,
    norm_attn,
    w_query,
    w_key,
    w_value,
    w_output,
    norm_mlp,
    w_gate,
    w_up,
    w_down,
):
    owners, subs = lax.axis_size("fsdp"), lax.axis_size("sub")
    members = owners * subs
    length, width = hidden_in.shape[1:]
    tokens = members * length

    gains = lax.all_gather(jnp.stack([norm_attn, norm_mlp]), "fsdp", axis=1, tiled=True)
    gain_attn = gains[0].astype(F32)
    gain_mlp = gains[1].astype(F32)
    codes = gather_tokens(segment_ids * 2 + valid_mask)
    hidden_low = gather_tokens(hidden_in).reshape(tokens, width)
    qkv = regroup_columns((w_query, w_key, w_value), owners, subs)
    out_rows = row_block(w_output, subs)
    gate_up = regroup_columns((w_gate, w_up), owners, subs)
    down_rows = row_block(w_down, subs)
    ff = down_rows.shape[0]

    hidden_all = hidden_low.astype(F32)
    normed_one = (hidden_all * row_scale(hidden_all) * gain_attn).astype(BF16)
    projected = dot_f32(normed_one, qkv)
    q_width, k_width = GROUPS * HD, HD
    cos_table, sin_table = rope_tables(length, HD)
    cos_heads = cos_table[None, :, None, :]
    sin_heads = sin_table[None, :, None, :]
    per_seq = projected.reshape(members, length, GROUPS + 2, HD)
    queries = rotate(per_seq[:, :, :GROUPS], cos_heads, sin_heads).astype(BF16)
    keys = rotate(per_seq[:, :, GROUPS : GROUPS + 1], cos_heads, sin_heads).astype(BF16)[:, :, 0]
    values = per_seq[:, :, GROUPS + 1].astype(BF16)

    segments, validity = codes // 2, codes % 2
    row_index = jnp.arange(length, dtype=jnp.int32)[:, None]
    col_index = jnp.arange(length, dtype=jnp.int32)[None, :]
    allowed = (
        (segments[:, :, None] == segments[:, None, :])
        & (col_index <= row_index)
        & ((validity[:, None, :] == 1) | (col_index == row_index))
    )[:, None]
    scores = jnp.einsum("stgd,sud->sgtu", queries, keys, preferred_element_type=F32) * SCORE_SCALE
    scores = jnp.where(allowed, scores, MASKED_SCORE)
    shifted = jnp.exp(scores - jnp.max(scores, axis=-1, keepdims=True))
    probs = shifted / jnp.sum(shifted, axis=-1, keepdims=True)
    probs_low = probs.astype(BF16)
    attended = jnp.einsum("sgtu,sud->stgd", probs_low, values, preferred_element_type=F32)
    attended = attended.reshape(tokens, q_width).astype(BF16)
    attn_branch = scatter_tokens(dot_f32(attended, out_rows).astype(BF16)).astype(F32)

    hidden = hidden_in[0].astype(F32)
    scale_one = row_scale(hidden)
    unit_one = hidden * scale_one
    middle = hidden + RESIDUAL_SCALE * attn_branch
    scale_two = row_scale(middle)
    unit_two = middle * scale_two
    normed_two = gather_tokens((unit_two * gain_mlp).astype(BF16))
    gate_up_proj = dot_f32(normed_two, gate_up)
    gate_proj, up_proj = gate_up_proj[:, :ff], gate_up_proj[:, ff:]
    sigma = jax.nn.sigmoid(gate_proj)
    silu_gate = gate_proj * sigma
    mixed_act = (silu_gate * up_proj).astype(BF16)
    mlp_branch = scatter_tokens(dot_f32(mixed_act, down_rows).astype(BF16)).astype(F32)
    result = middle + RESIDUAL_SCALE * mlp_branch

    result_grad = cotangent[0].astype(F32)
    mlp_out_grad = gather_tokens((RESIDUAL_SCALE * result_grad).astype(BF16))
    mixed_grad = contract_cols(mlp_out_grad, down_rows)
    down_w_grad = contract_rows(mixed_act, mlp_out_grad).astype(BF16)
    slope = sigma * (1.0 + gate_proj * (1.0 - sigma))
    gate_grad = (mixed_grad * up_proj * slope).astype(BF16)
    up_grad = (mixed_grad * silu_gate).astype(BF16)
    gate_up_grad = jnp.concatenate([gate_grad, up_grad], axis=1)
    normed_two_grad = scatter_tokens(contract_cols(gate_up_grad, gate_up).astype(BF16)).astype(F32)
    gate_up_w_grad = contract_rows(normed_two, gate_up_grad).astype(BF16)
    gain_mlp_grad, middle_part = norm_backward(normed_two_grad, scale_two, unit_two, gain_mlp)
    middle_grad = result_grad + middle_part

    attn_out_grad = gather_tokens((RESIDUAL_SCALE * middle_grad).astype(BF16))
    attended_grad = contract_cols(attn_out_grad, out_rows).astype(BF16)
    output_w_grad = contract_rows(attended, attn_out_grad).astype(BF16)
    heads_grad = attended_grad.reshape(members, length, GROUPS, HD)
    prob_grad = jnp.einsum("stgd,sud->sgtu", heads_grad, values, preferred_element_type=F32)
    row_dot = jnp.sum(probs * prob_grad, axis=-1, keepdims=True)
    score_grad = (probs * (prob_grad - row_dot)).astype(BF16)
    query_grad = (
        jnp.einsum("sgtu,sud->stgd", score_grad, keys, preferred_element_type=F32) * SCORE_SCALE
    )
    key_grad = (
        jnp.einsum("sgtu,stgd->sud", score_grad, queries, preferred_element_type=F32) * SCORE_SCALE
    )
    value_grad = jnp.einsum("sgtu,stgd->sud", probs_low, heads_grad, preferred_element_type=F32)
    qkv_grad = jnp.concatenate(
        [
            rotate(query_grad, cos_heads, -sin_heads),
            rotate(key_grad[:, :, None], cos_heads, -sin_heads),
            value_grad[:, :, None],
        ],
        axis=2,
    )
    qkv_grad = qkv_grad.reshape(tokens, q_width + 2 * k_width).astype(BF16)
    normed_one_grad = scatter_tokens(contract_cols(qkv_grad, qkv).astype(BF16)).astype(F32)
    qkv_w_grad = contract_rows(normed_one, qkv_grad).astype(BF16)
    gain_attn_grad, hidden_part = norm_backward(normed_one_grad, scale_one, unit_one, gain_attn)
    input_grad = (middle_grad + hidden_part).astype(BF16)

    validity_own = valid_mask[0].astype(F32)[:, None]
    squares = [
        jnp.sum(tensor * tensor * validity_own)
        for tensor in (hidden, middle, result, attn_branch, mlp_branch)
    ]
    tally = jnp.concatenate(
        [gain_attn_grad, gain_mlp_grad, jnp.stack(squares + [jnp.sum(validity_own)])]
    )
    tally = lax.psum(tally, ("rep", "sub", "fsdp"))
    part = width // owners
    start = lax.axis_index("fsdp") * part
    gain_attn_out = lax.dynamic_slice_in_dim(tally, start, part)
    gain_mlp_out = lax.dynamic_slice_in_dim(tally, width + start, part)
    statistics = jnp.sqrt(tally[2 * width : 2 * width + 5] / (tally[2 * width + 5] * width))

    down_out = finish_rows(down_w_grad)
    gate_out, up_out = finish_columns(gate_up_w_grad, (ff, ff))
    output_out = finish_rows(output_w_grad)
    query_out, key_out, value_out = finish_columns(qkv_w_grad, (q_width, k_width, k_width))
    return (
        result.astype(BF16)[None],
        input_grad[None],
        gain_attn_out,
        query_out,
        key_out,
        value_out,
        output_out,
        gain_mlp_out,
        gate_out,
        up_out,
        down_out,
        statistics,
    )


def solution(mesh):
    fsdp = mesh.shape["fsdp"]
    subs = max(1, KV // fsdp)
    rep = mesh.shape["dp"] // subs
    plane_mesh = Mesh(mesh.devices.reshape(rep, subs, fsdp), ("rep", "sub", "fsdp"))
    batch = ("rep", "sub", "fsdp")
    return jax.shard_map(
        shards,
        mesh=plane_mesh,
        in_specs=(
            P(batch, None, None),
            P(batch, None),
            P(batch, None),
            P(batch, None, None),
            P("fsdp"),
            P("fsdp", None),
            P("fsdp", None),
            P("fsdp", None),
            P("fsdp", None),
            P("fsdp"),
            P("fsdp", None),
            P("fsdp", None),
            P("fsdp", None),
        ),
        out_specs=(
            P(batch, None, None),
            P(batch, None, None),
            P("fsdp"),
            P("fsdp", None),
            P("fsdp", None),
            P("fsdp", None),
            P("fsdp", None),
            P("fsdp"),
            P("fsdp", None),
            P("fsdp", None),
            P("fsdp", None),
            P(),
        ),
        check_vma=False,
    )
```

```python
import functools

import jax
import jax.numpy as jnp
from jax import lax
from jax.experimental import pallas as pl
from jax.experimental.pallas import tpu as pltpu
from jax.sharding import Mesh
from jax.sharding import PartitionSpec as P

H = 32
KV = 8
HD = 64
GROUPS = H // KV

EPSILON = 1e-05
RESIDUAL_SCALE = 0.22
SCORE_SCALE = 1.0 / 64.0
MASKED_SCORE = -1e30
ROPE_BASE = 10000000.0

BF16 = jnp.bfloat16
F32 = jnp.float32
MESH = pl.DeviceIdType.MESH
SCALE = 3_300_000
HBM = pl.BlockSpec(memory_space=pltpu.HBM)
VM = pl.BlockSpec(memory_space=pltpu.VMEM)


def rope_tables(length, head_size):
    half_size = head_size // 2
    frequency = ROPE_BASE ** (-(jnp.arange(half_size, dtype=F32) * 2.0 / head_size))
    angles = jnp.arange(length, dtype=F32)[:, None] * frequency[None, :]
    return (jnp.cos(angles), jnp.sin(angles))


def rotate(tensor, cos_table, sin_table):
    half_size = tensor.shape[-1] // 2
    front_half = tensor[..., :half_size]
    back_half = tensor[..., half_size:]
    return jnp.concatenate(
        [
            front_half * cos_table - back_half * sin_table,
            back_half * cos_table + front_half * sin_table,
        ],
        axis=-1,
    )


def dot_f32(left, right):
    return jnp.dot(left, right, preferred_element_type=F32)


def contract_rows(left, right):
    return jnp.einsum("sa,sb->ab", left, right, preferred_element_type=F32)


def contract_cols(left, right):
    return jnp.einsum("sb,ab->sa", left, right, preferred_element_type=F32)


def row_scale(source):
    return lax.rsqrt(jnp.mean(source * source, axis=-1, keepdims=True) + EPSILON)


def norm_backward(grad_norm, scale_row, unit_rows, gain):
    gain_grad = jnp.sum(grad_norm * unit_rows, axis=0)
    scaled = grad_norm * gain
    source_grad = scale_row * (
        scaled - unit_rows * jnp.mean(scaled * unit_rows, axis=-1, keepdims=True)
    )
    return (gain_grad, source_grad)


def after(value, *others):
    return lax.optimization_barrier((value,) + others)[0]


def plane_position():
    rep, core, own = lax.axis_index("rep"), lax.axis_index("sub"), lax.axis_index("fsdp")
    row, col = own // 2, own % 2
    across = row * 2 + (1 - col)
    down = (1 - row) * 2 + col
    corner = (1 - row) * 2 + (1 - col)
    return rep, core, own, across, down, corner


def meet(devices):
    barrier = pltpu.get_barrier_semaphore()
    for device in devices:
        pl.semaphore_signal(barrier, inc=1, device_id=device, device_id_type=MESH)
    pl.semaphore_wait(barrier, len(devices))


def params(collective_id, megabytes=16):
    return pltpu.CompilerParams(
        collective_id=collective_id, has_side_effects=True, vmem_limit_bytes=megabytes << 20
    )


def link_cost(microseconds, flops=0):
    return pl.CostEstimate(
        flops=0, bytes_accessed=int(microseconds * SCALE), transcendentals=0
    )


class Sender:
    def __init__(self, send_sems, recv_sems):
        self.send_sems, self.recv_sems, self.copies = send_sems, recv_sems, []

    def send(self, src, dst, device):
        index = len(self.copies)
        copy = pltpu.make_async_remote_copy(
            src_ref=src,
            dst_ref=dst,
            send_sem=self.send_sems.at[index],
            recv_sem=self.recv_sems.at[index],
            device_id=device,
            device_id_type=MESH,
        )
        copy.start()
        self.copies.append(copy)
        return copy

    def finish(self):
        for copy in self.copies:
            copy.wait_send()


class Gather:
    def __init__(self, sender, x_ref, out_ref, local_sem, place):
        self.sender, self.x_ref, self.out_ref, self.place = sender, x_ref, out_ref, place
        rep, core, own, across, down, _ = place
        self.to_across, self.to_down = (rep, core, across), (rep, core, down)
        self.to_core = (rep, 1 - core, own)
        half = x_ref.shape[0] // 2
        self.low, self.high, self.whole = pl.ds(0, half), pl.ds(half, half), pl.ds(0, 2 * half)
        self.base = core * 4
        self.mine = pltpu.make_async_copy(x_ref, out_ref.at[self.base + own], local_sem)

    def first(self, rows, device):
        own = self.place[2]
        return self.sender.send(
            self.x_ref.at[rows], self.out_ref.at[self.base + own, rows], device
        )

    def forward(self, block, rows, device):
        ref = self.out_ref.at[self.base + block, rows]
        return self.sender.send(ref, ref, device)

    def begin(self):
        self.across_low = self.first(self.low, self.to_across)
        self.down_high = self.first(self.high, self.to_down)
        self.across_high = self.first(self.high, self.to_across)
        self.down_low = self.first(self.low, self.to_down)
        self.swaps = [self.first(self.whole, self.to_core)]
        self.mine.start()

    def relay(self):
        _, _, _, across, down, _ = self.place
        low, high, to_core = self.low, self.high, self.to_core
        self.across_low.wait_recv()
        self.corner_low = self.forward(across, low, self.to_down)
        self.swaps.append(self.forward(across, low, to_core))
        self.down_high.wait_recv()
        self.corner_high = self.forward(down, high, self.to_across)
        self.swaps.append(self.forward(down, high, to_core))
        self.across_high.wait_recv()
        self.swaps.append(self.forward(across, high, to_core))
        self.down_low.wait_recv()
        self.swaps.append(self.forward(down, low, to_core))

    def finish(self):
        corner = self.place[5]
        self.corner_low.wait_recv()
        self.swaps.append(self.forward(corner, self.low, self.to_core))
        self.corner_high.wait_recv()
        self.swaps.append(self.forward(corner, self.high, self.to_core))
        for swap in self.swaps:
            swap.wait_recv()
        self.mine.wait()


def gather_kernel(count, *refs):
    xs, outs = refs[:count], refs[count : 2 * count]
    local_sems, send_sems, recv_sems = refs[2 * count :]
    place = plane_position()
    rep, core, own, across, down, _ = place
    meet([(rep, core, across), (rep, core, down), (rep, 1 - core, own)])
    sender = Sender(send_sems, recv_sems)
    moves = [
        Gather(sender, x, out, local_sems.at[i], place) for i, (x, out) in enumerate(zip(xs, outs))
    ]
    for move in moves:
        move.begin()
    for move in moves:
        move.relay()
    for move in moves:
        move.finish()
    sender.finish()


def gather_plane(blocks, collective_id):
    count = len(blocks)
    return pl.pallas_call(
        functools.partial(gather_kernel, count),
        out_shape=[jax.ShapeDtypeStruct((8,) + x.shape, x.dtype) for x in blocks],
        in_specs=[HBM] * count,
        out_specs=[HBM] * count,
        scratch_shapes=[
            pltpu.SemaphoreType.DMA((count,)),
            pltpu.SemaphoreType.DMA((13 * count,)),
            pltpu.SemaphoreType.DMA((13 * count,)),
        ],
        compiler_params=params(collective_id),
        cost_estimate=link_cost(40 * count),
    )(*blocks)


def quarter_kernel(gate_ref, up_ref, out_ref, local_sems, send_sems, recv_sems):
    rep, core, own, across, down, corner = plane_position()
    peers = (corner, across, down)
    meet([(rep, core, peer) for peer in peers])
    rows = out_ref.shape[1]
    width = out_ref.shape[2] // 2
    mine = pl.ds(pl.multiple_of(rep * rows, rows), rows)

    def source(ref, block):
        columns = pl.ds(pl.multiple_of((block * 2 + core) * width, width), width)
        return ref.at[mine, columns]

    sender = Sender(send_sems, recv_sems)
    for peer in peers:
        for k, ref in enumerate((gate_ref, up_ref)):
            target = out_ref.at[own, :, pl.ds(k * width, width)]
            sender.send(source(ref, peer), target, (rep, core, peer))
    local = []
    for k, ref in enumerate((gate_ref, up_ref)):
        copy = pltpu.make_async_copy(
            source(ref, own), out_ref.at[own, :, pl.ds(k * width, width)], local_sems.at[k]
        )
        copy.start()
        local.append(copy)
    for copy in sender.copies:
        copy.wait_recv()
    sender.finish()
    for copy in local:
        copy.wait()


def quarter_columns(w_gate, w_up, reps, collective_id):
    rows, columns = w_gate.shape
    return pl.pallas_call(
        quarter_kernel,
        out_shape=jax.ShapeDtypeStruct((4, rows // reps, columns // 4), BF16),
        in_specs=[HBM, HBM],
        out_specs=HBM,
        scratch_shapes=[
            pltpu.SemaphoreType.DMA((2,)),
            pltpu.SemaphoreType.DMA((6,)),
            pltpu.SemaphoreType.DMA((6,)),
        ],
        compiler_params=params(collective_id),
        cost_estimate=link_cost(25),
    )(w_gate, w_up)


def start_kernel(
    x_ref, code_ref, gain_ref, q_ref, k_ref, v_ref,
    x_out, code_out, gain_out, q_out, k_out, v_out,
    local_sems, send_sems, recv_sems,
):
    place = plane_position()
    rep, core, own, across, down, corner = place
    peers = (corner, across, down)
    meet([(rep, core, peer) for peer in peers] + [(rep, 1 - core, peer) for peer in peers]
         + [(rep, 1 - core, own)])
    sender = Sender(send_sems, recv_sems)
    direct, local = [], []

    def keep(src, dst):
        copy = pltpu.make_async_copy(src, dst, local_sems.at[1 + len(local)])
        copy.start()
        local.append(copy)

    def columns(ref, block, width):
        return ref.at[:, pl.ds(pl.multiple_of(block * width, width), width)]

    def weights():
        for peer in peers:
            there = (rep, core, peer)
            direct.append(sender.send(gain_ref, gain_out.at[own], there))
            direct.append(sender.send(columns(q_ref, peer * 2 + core, 256), q_out.at[own], there))
            direct.append(sender.send(columns(k_ref, peer, 128), k_out.at[own], there))
            direct.append(sender.send(columns(v_ref, peer, 128), v_out.at[own], there))
            direct.append(sender.send(code_ref, code_out.at[core * 4 + own], there))
            other = (rep, 1 - core, peer)
            direct.append(sender.send(code_ref, code_out.at[core * 4 + own], other))
        direct.append(sender.send(code_ref, code_out.at[core * 4 + own], (rep, 1 - core, own)))
        keep(gain_ref, gain_out.at[own])
        keep(columns(q_ref, own * 2 + core, 256), q_out.at[own])
        keep(columns(k_ref, own, 128), k_out.at[own])
        keep(columns(v_ref, own, 128), v_out.at[own])
        keep(code_ref, code_out.at[core * 4 + own])

    move = Gather(sender, x_ref, x_out, local_sems.at[0], place)
    move.begin()
    weights()
    move.relay()
    move.finish()
    for copy in direct:
        copy.wait_recv()
    sender.finish()
    for copy in local:
        copy.wait()


def start_plane(hidden, codes, gains, w_query, w_key, w_value, collective_id):
    rows = w_query.shape[0]
    shapes = [
        ((8,) + hidden.shape, BF16),
        ((8,) + codes.shape, jnp.int32),
        ((4,) + gains.shape, BF16),
        ((4, rows, GROUPS * HD), BF16),
        ((4, rows, 2 * HD), BF16),
        ((4, rows, 2 * HD), BF16),
    ]
    return pl.pallas_call(
        start_kernel,
        out_shape=[jax.ShapeDtypeStruct(s, d) for s, d in shapes],
        in_specs=[HBM] * 6,
        out_specs=[HBM] * 6,
        scratch_shapes=[
            pltpu.SemaphoreType.DMA((6,)),
            pltpu.SemaphoreType.DMA((32,)),
            pltpu.SemaphoreType.DMA((32,)),
        ],
        compiler_params=params(collective_id),
        cost_estimate=link_cost(60),
    )(hidden, codes, gains, w_query, w_key, w_value)


def product_scatter_kernel(turned, count, *refs):
    x_hbm, w_hbm, out_ref = refs[:count], refs[count], refs[count + 1]
    x_refs, w_ref = refs[count + 2 : 2 * count + 2], refs[2 * count + 2]
    (
        swap, held, from_core, from_across, from_down, last_across, last_down,
        x_sems, w_sems, core_send, core_recv, send_sems, recv_sems,
    ) = refs[2 * count + 3 :]
    rep, core, own, across, down, corner = plane_position()
    to_across, to_down, to_core = (rep, core, across), (rep, core, down), (rep, 1 - core, own)
    _, rows, wide = held.shape
    depth = x_refs[0].shape[1]
    tile = 512
    tiles = wide // tile
    half = rows // 2
    low, high = pl.ds(0, half), pl.ds(half, half)
    order = []
    for block in (corner, across, down, own):
        order += [(1 - core) * 4 + block, core * 4 + block]

    def rows_of(block):
        return pl.ds(pl.multiple_of(block * rows, rows), rows)

    x_loads = [
        [
            pltpu.make_async_copy(
                x_hbm[i].at[rows_of(block)], x_refs[i].at[rows_of(block)], x_sems.at[i, n]
            )
            for i in range(count)
        ]
        for n, block in enumerate(order)
    ]
    w_loads = []
    for t in range(tiles):
        columns = pl.ds(t * tile, tile)
        if turned:
            src, dst = w_hbm.at[columns], w_ref.at[columns]
        else:
            kept = pl.ds(pl.multiple_of(core * depth, depth), depth)
            src, dst = w_hbm.at[kept, columns], w_ref.at[:, columns]
        w_loads.append(pltpu.make_async_copy(src, dst, w_sems.at[t]))
    for load in x_loads[0]:
        load.start()
    for load in w_loads:
        load.start()
    for loads in x_loads[1:]:
        for load in loads:
            load.start()
    meet([to_across, to_down, to_core])

    def product(dst, mine, columns):
        total = None
        for i in range(count):
            x = x_refs[i][mine, :]
            if turned:
                w = w_ref[columns, pl.ds(i * depth, depth)]
                part = lax.dot_general(
                    x, w, (((1,), (1,)), ((), ())), preferred_element_type=F32
                )
            else:
                part = dot_f32(x, w_ref[:, columns])
            total = part if total is None else total + part
        dst[:, columns] = total.astype(BF16)

    def fill(dst, n):
        for load in x_loads[n]:
            load.wait()
        mine = rows_of(order[n])
        if n == 0:
            for t in range(tiles):
                w_loads[t].wait()
                product(dst, mine, pl.ds(t * tile, tile))
        else:

            @pl.loop(0, tiles)
            def _(t):
                product(dst, mine, pl.ds(pl.multiple_of(t * tile, tile), tile))

    swaps = Sender(core_send, core_recv)
    sender = Sender(send_sems, recv_sems)
    sent = {}
    for k in range(4):
        fill(swap.at[k], 2 * k)
        swaps.send(swap.at[k], from_core.at[k], to_core)
        fill(held.at[k], 2 * k + 1)
        swaps.copies[k].wait_recv()
        held[k] = held[k] + from_core[k]
        if k == 0:
            sent[0] = sender.send(held.at[0, low], from_across.at[0], to_across)
            sent[1] = sender.send(held.at[0, high], from_down.at[0], to_down)
        if k == 1:
            sent[2] = sender.send(held.at[1, low], from_across.at[1], to_across)
        if k == 2:
            sent[3] = sender.send(held.at[2, high], from_down.at[1], to_down)
    sent[0].wait_recv()
    held[2, low] = held[2, low] + from_across[0]
    to_last = sender.send(held.at[2, low], last_down, to_down)
    sent[1].wait_recv()
    held[1, high] = held[1, high] + from_down[0]
    across_last = sender.send(held.at[1, high], last_across, to_across)
    sent[2].wait_recv()
    sent[3].wait_recv()
    to_last.wait_recv()
    out_ref[low] = (
        held[3, low].astype(F32) + from_across[1].astype(F32) + last_down[...].astype(F32)
    )
    across_last.wait_recv()
    out_ref[high] = (
        held[3, high].astype(F32) + from_down[1].astype(F32) + last_across[...].astype(F32)
    )
    swaps.finish()
    sender.finish()


def product_scatter(xs, w, turned, collective_id):
    count = len(xs)
    tokens, depth = xs[0].shape
    rows = tokens // 8
    wide = w.shape[0] if turned else w.shape[1]
    half = rows // 2
    return pl.pallas_call(
        functools.partial(product_scatter_kernel, turned, count),
        out_shape=jax.ShapeDtypeStruct((rows, wide), F32),
        in_specs=[HBM] * (count + 1),
        out_specs=VM,
        scratch_shapes=[pltpu.VMEM((tokens, depth), BF16)] * count
        + [
            pltpu.VMEM((wide, depth * count) if turned else (depth, wide), BF16),
            pltpu.VMEM((4, rows, wide), BF16),
            pltpu.VMEM((4, rows, wide), BF16),
            pltpu.VMEM((4, rows, wide), BF16),
            pltpu.VMEM((2, half, wide), BF16),
            pltpu.VMEM((2, half, wide), BF16),
            pltpu.VMEM((half, wide), BF16),
            pltpu.VMEM((half, wide), BF16),
            pltpu.SemaphoreType.DMA((count, 8)),
            pltpu.SemaphoreType.DMA((wide // 512,)),
            pltpu.SemaphoreType.DMA((4,)),
            pltpu.SemaphoreType.DMA((4,)),
            pltpu.SemaphoreType.DMA((6,)),
            pltpu.SemaphoreType.DMA((6,)),
        ],
        compiler_params=params(collective_id, 56),
        cost_estimate=link_cost(44, 2 * tokens * depth * count * wide),
    )(*xs, w)


def cast_kernel(x_ref, out_ref):
    out_ref[...] = x_ref[...].reshape(out_ref.shape).astype(F32)


def cast_rows(spread):
    reps, subs, rows, columns = spread.shape
    return pl.pallas_call(
        cast_kernel,
        grid=(subs, reps),
        out_shape=jax.ShapeDtypeStruct((reps * subs * rows, columns), F32),
        in_specs=[pl.BlockSpec((1, 1, rows, columns), lambda s, r: (r, s, 0, 0))],
        out_specs=pl.BlockSpec((rows, columns), lambda s, r: (s * reps + r, 0)),
        cost_estimate=link_cost(8),
    )(spread)


def cast_columns(spread):
    reps, subs, owners, rows, columns = spread.shape
    return pl.pallas_call(
        cast_kernel,
        grid=(reps, owners, subs),
        out_shape=jax.ShapeDtypeStruct((reps * rows, owners * subs * columns), F32),
        in_specs=[
            pl.BlockSpec((1, 1, 1, rows, columns), lambda r, j, s: (r, s, j, 0, 0)),
        ],
        out_specs=pl.BlockSpec((rows, columns), lambda r, j, s: (r, j * subs + s)),
        cost_estimate=link_cost(8),
    )(spread)


def column_blocks(weight, owners, subs):
    rows, columns = weight.shape
    blocked = weight.reshape(rows, owners, subs, columns // (owners * subs))
    mine = lax.dynamic_index_in_dim(blocked, lax.axis_index("sub"), axis=2, keepdims=False)
    return jnp.swapaxes(mine, 0, 1)


def regroup_columns(weights, owners, subs):
    blocks = jnp.concatenate([column_blocks(w, owners, subs) for w in weights], axis=-1)
    moved = lax.all_to_all(blocks, "fsdp", split_axis=0, concat_axis=0, tiled=True)
    return moved.reshape(-1, moved.shape[-1])


def row_block(weight, subs):
    rows = weight.shape[0] // subs
    return lax.dynamic_slice_in_dim(weight, lax.axis_index("sub") * rows, rows, axis=0)


def gather_tokens(block):
    return lax.all_gather(block, ("sub", "fsdp"), axis=0, tiled=True)


def scatter_tokens(partial):
    return lax.psum_scatter(partial, ("sub", "fsdp"), scatter_dimension=0, tiled=True)


def sum_planes(term):
    return lax.psum_scatter(term, "rep", scatter_dimension=0, tiled=True)


def spread_planes(piece):
    rep, subs = lax.axis_size("rep"), lax.axis_size("sub")
    spread = lax.all_gather(piece, ("rep", "sub"), axis=0, tiled=False)
    return spread.reshape((rep, subs) + piece.shape)


def owner_major(term):
    owners, rep = lax.axis_size("fsdp"), lax.axis_size("rep")
    rows, columns = term.shape
    blocked = jnp.swapaxes(term.reshape(owners, rep, rows // (owners * rep), columns), 0, 1)
    return blocked.reshape(rows, columns)


def to_owners(piece):
    blocked = piece.reshape(lax.axis_size("fsdp"), -1, piece.shape[1])
    return lax.all_to_all(blocked, "fsdp", split_axis=0, concat_axis=0, tiled=True)


def place_columns(spread):
    reps, subs, owners, rows, columns = spread.shape
    part = jnp.transpose(spread, (0, 3, 2, 1, 4))
    return part.reshape(reps * rows, owners * subs * columns).astype(F32)


def shards(
    kernels,
    hidden_in,
    segment_ids,
    valid_mask,
    cotangent,
    norm_attn,
    w_query,
    w_key,
    w_value,
    w_output,
    norm_mlp,
    w_gate,
    w_up,
    w_down,
):
    owners, subs, reps = lax.axis_size("fsdp"), lax.axis_size("sub"), lax.axis_size("rep")
    members = owners * subs
    length, width = hidden_in.shape[1:]
    tokens = members * length
    q_width, k_width = GROUPS * HD, HD

    def gathered(blocks, collective_id):
        if kernels:
            outs = gather_plane(blocks, collective_id)
        else:
            outs = [gather_tokens(block) for block in blocks]
        return [out.reshape(tokens, -1) for out in outs]

    def scattered(xs, w, turned, collective_id):
        if kernels:
            return product_scatter(xs, w, turned, collective_id)
        x = jnp.concatenate(xs, axis=1)
        if turned:
            return scatter_tokens(contract_cols(x, w).astype(BF16)).astype(F32)
        return scatter_tokens(dot_f32(x, row_block(w, subs)).astype(BF16)).astype(F32)

    codes = segment_ids * 2 + valid_mask
    gains = jnp.stack([norm_attn, norm_mlp])
    result_grad = cotangent[0].astype(F32)
    mlp_out_low = (RESIDUAL_SCALE * result_grad).astype(BF16)
    if kernels:
        quarter = quarter_columns(w_gate, w_up, reps, 0)
        hidden_tied = after(hidden_in[0], quarter)
        hidden_low, codes, gains, q_cols, k_cols, v_cols = start_plane(
            hidden_tied, codes, gains, w_query, w_key, w_value, 1
        )
        hidden_low = hidden_low.reshape(tokens, width)
        codes = codes.reshape(members, length)
        gains = jnp.swapaxes(gains, 0, 1).reshape(2, width)
        core_at = lax.axis_index("sub") * HD
        qkv = jnp.concatenate(
            [
                q_cols,
                lax.dynamic_slice_in_dim(k_cols, core_at, HD, axis=2),
                lax.dynamic_slice_in_dim(v_cols, core_at, HD, axis=2),
            ],
            axis=2,
        ).reshape(width, q_width + 2 * k_width)
        gate_up = lax.all_gather(quarter, "rep", axis=1, tiled=True).reshape(width, -1)
    else:
        gains = lax.all_gather(gains, "fsdp", axis=1, tiled=True)
        codes = gather_tokens(codes)
        hidden_low = gather_tokens(hidden_in[0])
        qkv = regroup_columns((w_query, w_key, w_value), owners, subs)
        gate_up = regroup_columns((w_gate, w_up), owners, subs)
    gain_attn = gains[0].astype(F32)
    gain_mlp = gains[1].astype(F32)
    ff = gate_up.shape[1] // 2

    hidden_all = hidden_low.astype(F32)
    normed_one = (hidden_all * row_scale(hidden_all) * gain_attn).astype(BF16)
    projected = dot_f32(normed_one, qkv)
    cos_table, sin_table = rope_tables(length, HD)
    cos_heads = cos_table[None, :, None, :]
    sin_heads = sin_table[None, :, None, :]
    per_seq = projected.reshape(members, length, GROUPS + 2, HD)
    queries = rotate(per_seq[:, :, :GROUPS], cos_heads, sin_heads).astype(BF16)
    keys = rotate(per_seq[:, :, GROUPS : GROUPS + 1], cos_heads, sin_heads).astype(BF16)[:, :, 0]
    values = per_seq[:, :, GROUPS + 1].astype(BF16)

    segments, validity = codes // 2, codes % 2
    row_index = jnp.arange(length, dtype=jnp.int32)[:, None]
    col_index = jnp.arange(length, dtype=jnp.int32)[None, :]
    allowed = (
        (segments[:, :, None] == segments[:, None, :])
        & (col_index <= row_index)
        & ((validity[:, None, :] == 1) | (col_index == row_index))
    )[:, None]
    scores = jnp.einsum("stgd,sud->sgtu", queries, keys, preferred_element_type=F32) * SCORE_SCALE
    scores = jnp.where(allowed, scores, MASKED_SCORE)
    shifted = jnp.exp(scores - jnp.max(scores, axis=-1, keepdims=True))
    probs = shifted / jnp.sum(shifted, axis=-1, keepdims=True)
    probs_low = probs.astype(BF16)
    attended = jnp.einsum("sgtu,sud->stgd", probs_low, values, preferred_element_type=F32)
    attended = attended.reshape(tokens, q_width).astype(BF16)
    attn_branch = scattered([attended], w_output, False, 2)

    hidden = hidden_in[0].astype(F32)
    scale_one = row_scale(hidden)
    unit_one = hidden * scale_one
    middle = hidden + RESIDUAL_SCALE * attn_branch
    scale_two = row_scale(middle)
    unit_two = middle * scale_two
    normed_two, mlp_out_grad = gathered([(unit_two * gain_mlp).astype(BF16), mlp_out_low], 3)
    gate_up_proj = dot_f32(normed_two, gate_up)
    gate_proj, up_proj = gate_up_proj[:, :ff], gate_up_proj[:, ff:]
    sigma = jax.nn.sigmoid(gate_proj)
    silu_gate = gate_proj * sigma
    mixed_act = (silu_gate * up_proj).astype(BF16)

    down_w_grad = contract_rows(mixed_act, mlp_out_grad).astype(BF16)
    down_w_piece = sum_planes(down_w_grad)
    mixed_grad = contract_cols(after(mlp_out_grad, down_w_grad), row_block(w_down, subs))
    slope = sigma * (1.0 + gate_proj * (1.0 - sigma))
    gate_grad = (mixed_grad * up_proj * slope).astype(BF16)
    up_grad = (mixed_grad * silu_gate).astype(BF16)
    gate_w_grad = owner_major(contract_rows(normed_two, gate_grad).astype(BF16))
    up_w_grad = owner_major(contract_rows(normed_two, up_grad).astype(BF16))
    gate_sum = sum_planes(gate_w_grad)
    up_sum = sum_planes(up_w_grad)
    gate_up_grad = [after(gate_grad, gate_w_grad, up_w_grad), up_grad]
    normed_two_grad = scattered(gate_up_grad, gate_up, True, 4)
    gain_mlp_grad, middle_part = norm_backward(normed_two_grad, scale_two, unit_two, gain_mlp)
    middle_grad = result_grad + middle_part

    attn_out_low = after((RESIDUAL_SCALE * middle_grad).astype(BF16), down_w_piece)
    (attn_out_grad,) = gathered([attn_out_low], 5)
    attn_out_grad = after(attn_out_grad, gate_sum)
    attended_grad = contract_cols(attn_out_grad, row_block(w_output, subs)).astype(BF16)
    output_w_grad = contract_rows(attended, attn_out_grad).astype(BF16)
    output_w_piece = sum_planes(output_w_grad)
    heads_grad = attended_grad.reshape(members, length, GROUPS, HD)
    prob_grad = jnp.einsum("stgd,sud->sgtu", heads_grad, values, preferred_element_type=F32)
    row_dot = jnp.sum(probs * prob_grad, axis=-1, keepdims=True)
    score_grad = (probs * (prob_grad - row_dot)).astype(BF16)
    query_grad = (
        jnp.einsum("sgtu,sud->stgd", score_grad, keys, preferred_element_type=F32) * SCORE_SCALE
    )
    key_grad = (
        jnp.einsum("sgtu,stgd->sud", score_grad, queries, preferred_element_type=F32) * SCORE_SCALE
    )
    value_grad = jnp.einsum("sgtu,stgd->sud", probs_low, heads_grad, preferred_element_type=F32)
    qkv_grad = jnp.concatenate(
        [
            rotate(query_grad, cos_heads, -sin_heads),
            rotate(key_grad[:, :, None], cos_heads, -sin_heads),
            value_grad[:, :, None],
        ],
        axis=2,
    )
    qkv_grad = qkv_grad.reshape(tokens, q_width + 2 * k_width).astype(BF16)
    qkv_tied = after(qkv_grad, output_w_grad)
    normed_one_grad = scattered([qkv_tied], qkv, True, 6)
    qkv_w_grad = owner_major(contract_rows(normed_one, after(qkv_grad, normed_one_grad, up_sum)).astype(BF16))
    qkv_sum = sum_planes(qkv_w_grad)
    gate_piece, up_piece, qkv_piece = (to_owners(t) for t in (gate_sum, up_sum, qkv_sum))
    gain_attn_grad, hidden_part = norm_backward(normed_one_grad, scale_one, unit_one, gain_attn)
    input_grad = (middle_grad + hidden_part).astype(BF16)

    mixed_tied = after(mixed_act, normed_one_grad, qkv_w_grad)
    mlp_branch = scattered([mixed_tied], w_down, False, 7)
    result = middle + RESIDUAL_SCALE * mlp_branch

    validity_own = valid_mask[0].astype(F32)[:, None]
    squares = [
        jnp.sum(tensor * tensor * validity_own)
        for tensor in (hidden, middle, result, attn_branch, mlp_branch)
    ]
    tally = jnp.concatenate(
        [gain_attn_grad, gain_mlp_grad, jnp.stack(squares + [jnp.sum(validity_own)])]
    )
    tally = lax.psum(tally, ("rep", "sub", "fsdp"))
    part = width // owners
    start = lax.axis_index("fsdp") * part
    gain_attn_out = lax.dynamic_slice_in_dim(tally, start, part)
    gain_mlp_out = lax.dynamic_slice_in_dim(tally, width + start, part)
    statistics = jnp.sqrt(tally[2 * width : 2 * width + 5] / (tally[2 * width + 5] * width))

    down_spread = spread_planes(down_w_piece)
    gate_spread = spread_planes(gate_piece)
    up_spread = spread_planes(up_piece)
    output_spread = spread_planes(output_w_piece)
    qkv_spread = spread_planes(qkv_piece)
    query_out = place_columns(qkv_spread[..., :q_width])
    key_out = place_columns(qkv_spread[..., q_width : q_width + k_width])
    value_out = place_columns(qkv_spread[..., q_width + k_width :])
    if kernels:
        down_out, output_out = cast_rows(down_spread), cast_rows(output_spread)
        gate_out, up_out = cast_columns(gate_spread), cast_columns(up_spread)
    else:
        down_out, output_out = (
            jnp.swapaxes(s, 0, 1).reshape(-1, width).astype(F32)
            for s in (down_spread, output_spread)
        )
        gate_out, up_out = place_columns(gate_spread), place_columns(up_spread)
    return (
        result.astype(BF16)[None],
        input_grad[None],
        gain_attn_out,
        query_out,
        key_out,
        value_out,
        output_out,
        gain_mlp_out,
        gate_out,
        up_out,
        down_out,
        statistics,
    )


def solution(mesh):
    fsdp = mesh.shape["fsdp"]
    subs = max(1, KV // fsdp)
    rep = mesh.shape["dp"] // subs
    kernels = fsdp == 4 and subs == 2
    plane_mesh = Mesh(mesh.devices.reshape(rep, subs, fsdp), ("rep", "sub", "fsdp"))
    batch = ("rep", "sub", "fsdp")
    return jax.shard_map(
        functools.partial(shards, kernels),
        mesh=plane_mesh,
        in_specs=(
            P(batch, None, None),
            P(batch, None),
            P(batch, None),
            P(batch, None, None),
            P("fsdp"),
            P("fsdp", None),
            P("fsdp", None),
            P("fsdp", None),
            P("fsdp", None),
            P("fsdp"),
            P("fsdp", None),
            P("fsdp", None),
            P("fsdp", None),
        ),
        out_specs=(
            P(batch, None, None),
            P(batch, None, None),
            P("fsdp"),
            P("fsdp", None),
            P("fsdp", None),
            P("fsdp", None),
            P("fsdp", None),
            P("fsdp"),
            P("fsdp", None),
            P("fsdp", None),
            P("fsdp", None),
            P(),
        ),
        check_vma=False,
    )
```

```python
import functools

import jax
import jax.numpy as jnp
from jax import lax
from jax.experimental import pallas as pl
from jax.experimental.pallas import tpu as pltpu
from jax.sharding import Mesh
from jax.sharding import PartitionSpec as P

H = 32
KV = 8
HD = 64
GROUPS = H // KV

EPSILON = 1e-05
RESIDUAL_SCALE = 0.22
SCORE_SCALE = 1.0 / 64.0
MASKED_SCORE = -1e30
ROPE_BASE = 10000000.0

BF16 = jnp.bfloat16
F32 = jnp.float32
MESH = pl.DeviceIdType.MESH
SCALE = 3_300_000
HBM = pl.BlockSpec(memory_space=pltpu.HBM)
VM = pl.BlockSpec(memory_space=pltpu.VMEM)


def rope_tables(length, head_size):
    half_size = head_size // 2
    frequency = ROPE_BASE ** (-(jnp.arange(half_size, dtype=F32) * 2.0 / head_size))
    angles = jnp.arange(length, dtype=F32)[:, None] * frequency[None, :]
    return (jnp.cos(angles), jnp.sin(angles))


def rotate(tensor, cos_table, sin_table):
    half_size = tensor.shape[-1] // 2
    front_half = tensor[..., :half_size]
    back_half = tensor[..., half_size:]
    return jnp.concatenate(
        [
            front_half * cos_table - back_half * sin_table,
            back_half * cos_table + front_half * sin_table,
        ],
        axis=-1,
    )


def dot_f32(left, right):
    return jnp.dot(left, right, preferred_element_type=F32)


def contract_rows(left, right):
    return jnp.einsum("sa,sb->ab", left, right, preferred_element_type=F32)


def contract_cols(left, right):
    return jnp.einsum("sb,ab->sa", left, right, preferred_element_type=F32)


def row_scale(source):
    return lax.rsqrt(jnp.mean(source * source, axis=-1, keepdims=True) + EPSILON)


def norm_backward(grad_norm, scale_row, unit_rows, gain):
    gain_grad = jnp.sum(grad_norm * unit_rows, axis=0)
    scaled = grad_norm * gain
    source_grad = scale_row * (
        scaled - unit_rows * jnp.mean(scaled * unit_rows, axis=-1, keepdims=True)
    )
    return (gain_grad, source_grad)


def after(value, *others):
    return lax.optimization_barrier((value,) + others)[0]


def plane_position():
    rep, core, own = lax.axis_index("rep"), lax.axis_index("sub"), lax.axis_index("fsdp")
    row, col = own // 2, own % 2
    across = row * 2 + (1 - col)
    down = (1 - row) * 2 + col
    corner = (1 - row) * 2 + (1 - col)
    return rep, core, own, across, down, corner


def meet(devices):
    barrier = pltpu.get_barrier_semaphore()
    for device in devices:
        pl.semaphore_signal(barrier, inc=1, device_id=device, device_id_type=MESH)
    pl.semaphore_wait(barrier, len(devices))


def params(collective_id, megabytes=16):
    return pltpu.CompilerParams(
        collective_id=collective_id, has_side_effects=True, vmem_limit_bytes=megabytes << 20
    )


def link_cost(microseconds, flops=0):
    return pl.CostEstimate(
        flops=0, bytes_accessed=int(microseconds * SCALE), transcendentals=0
    )


class Sender:
    def __init__(self, send_sems, recv_sems):
        self.send_sems, self.recv_sems, self.copies = send_sems, recv_sems, []

    def send(self, src, dst, device):
        index = len(self.copies)
        copy = pltpu.make_async_remote_copy(
            src_ref=src,
            dst_ref=dst,
            send_sem=self.send_sems.at[index],
            recv_sem=self.recv_sems.at[index],
            device_id=device,
            device_id_type=MESH,
        )
        copy.start()
        self.copies.append(copy)
        return copy

    def finish(self):
        for copy in self.copies:
            copy.wait_send()


class Gather:
    def __init__(self, sender, x_ref, out_ref, local_sem, place):
        self.sender, self.x_ref, self.out_ref, self.place = sender, x_ref, out_ref, place
        rep, core, own, across, down, _ = place
        self.to_across, self.to_down = (rep, core, across), (rep, core, down)
        self.to_core = (rep, 1 - core, own)
        half = x_ref.shape[0] // 2
        self.low, self.high, self.whole = pl.ds(0, half), pl.ds(half, half), pl.ds(0, 2 * half)
        self.base = core * 4
        self.mine = pltpu.make_async_copy(x_ref, out_ref.at[self.base + own], local_sem)

    def first(self, rows, device):
        own = self.place[2]
        return self.sender.send(
            self.x_ref.at[rows], self.out_ref.at[self.base + own, rows], device
        )

    def forward(self, block, rows, device):
        ref = self.out_ref.at[self.base + block, rows]
        return self.sender.send(ref, ref, device)

    def begin(self):
        self.across_low = self.first(self.low, self.to_across)
        self.down_high = self.first(self.high, self.to_down)
        self.across_high = self.first(self.high, self.to_across)
        self.down_low = self.first(self.low, self.to_down)
        self.swaps = [self.first(self.whole, self.to_core)]
        self.mine.start()

    def relay(self):
        _, _, _, across, down, _ = self.place
        low, high, to_core = self.low, self.high, self.to_core
        self.across_low.wait_recv()
        self.corner_low = self.forward(across, low, self.to_down)
        self.swaps.append(self.forward(across, low, to_core))
        self.down_high.wait_recv()
        self.corner_high = self.forward(down, high, self.to_across)
        self.swaps.append(self.forward(down, high, to_core))
        self.across_high.wait_recv()
        self.swaps.append(self.forward(across, high, to_core))
        self.down_low.wait_recv()
        self.swaps.append(self.forward(down, low, to_core))

    def finish(self):
        corner = self.place[5]
        self.corner_low.wait_recv()
        self.swaps.append(self.forward(corner, self.low, self.to_core))
        self.corner_high.wait_recv()
        self.swaps.append(self.forward(corner, self.high, self.to_core))
        for swap in self.swaps:
            swap.wait_recv()
        self.mine.wait()


class ExchangeJob:
    def __init__(self, source):
        self.rows = source.shape[0] // 4
        self.arrays = [source]
        self.corner = True
        self.outs = [jax.ShapeDtypeStruct((4, self.rows, source.shape[1]), BF16)]
        self.scratch = [pltpu.SemaphoreType.DMA((3,))] * 2 + [pltpu.SemaphoreType.DMA]

    def open(self, arrays, outs, scratch, place):
        self.source, self.out = arrays[0], outs[0]
        self.sems, self.keep_sem, self.place = scratch[:2], scratch[2], place

    def part(self, block):
        return self.source.at[pl.ds(pl.multiple_of(block * self.rows, 16), self.rows)]

    def stage(self, n):
        rep, core, own, across, down, corner = self.place
        if n == 0:
            self.sender = Sender(*self.sems)
            for peer in (corner, across, down):
                self.sender.send(self.part(peer), self.out.at[own], (rep, core, peer))
            self.keep = pltpu.make_async_copy(self.part(own), self.out.at[own], self.keep_sem)
            self.keep.start()
        if n == 6:
            for copy in self.sender.copies:
                copy.wait()
            self.keep.wait()


def column_place(place, reps):
    rep, core, own = place[:3]
    up = (rep == 0, rep == reps - 1, (rep + 1, core, own), (rep - 1, core, own))
    down = (rep == reps - 1, rep == 0, (rep - 1, core, own), (rep + 1, core, own))
    return (up, down)


def skewed(rep, reps, count, act, i):
    for low in (True, False):
        near = 0 if low else 1

        @pl.when((rep * 2 < reps) == low)
        def _(near=near):
            if i < count:
                act(near, i)
            if i >= 1:
                act(1 - near, i - 1)


class SumJob:
    def __init__(self, sources, blocks, cuts, reps, steps):
        self.blocks, self.cuts, self.reps, self.steps = blocks, cuts, reps, steps
        self.arrays = sources
        self.corner = blocks > 1
        rows = sources[0].shape[0]
        self.span = rows // blocks
        self.half = self.span // 2
        self.size = self.half // cuts
        self.widths = [source.shape[1] for source in sources]
        wide = sum(self.widths)
        self.outs = [jax.ShapeDtypeStruct((2, blocks, self.half, wide), BF16)]
        self.count = blocks * cuts
        sems = pltpu.SemaphoreType.DMA((2, self.count))
        self.scratch = [
            pltpu.VMEM((2, blocks, self.half, wide), BF16),
            pltpu.VMEM((2, blocks, self.half, wide), BF16),
            pltpu.SemaphoreType.DMA((2, blocks, len(sources))),
        ] + [sems] * 5

    def open(self, arrays, outs, scratch, place):
        self.sources, self.fin = arrays, outs[0]
        self.held, self.landed, self.load_sems = scratch[:3]
        self.chain_sems, self.give_sems, self.keep_sems = scratch[3:5], scratch[5:7], scratch[7]
        self.rep, self.core, self.own = place[:3]
        self.ways = column_place(place, self.reps)
        for k in range(self.blocks):
            for way in range(2):
                for load in self.loads(way, k):
                    load.start()

    def block(self, k):
        return (self.own + k) % self.blocks

    def loads(self, way, k):
        copies = []
        at = 0
        for n, (source, width) in enumerate(zip(self.sources, self.widths)):
            start = pl.multiple_of(self.block(k) * self.span + way * self.half, 16)
            src = source.at[pl.ds(start, self.half)]
            dst = self.held.at[way, k, :, pl.ds(at, width)]
            copies.append(pltpu.make_async_copy(src, dst, self.load_sems.at[way, k, n]))
            at += width
        return copies

    def rows(self, i):
        return i // self.cuts, pl.ds(i % self.cuts * self.size, self.size)

    def chain(self, way, i):
        k, rows = self.rows(i)
        return pltpu.make_async_remote_copy(
            src_ref=self.held.at[way, k, rows],
            dst_ref=self.landed.at[way, k, rows],
            send_sem=self.chain_sems[0].at[way, i],
            recv_sem=self.chain_sems[1].at[way, i],
            device_id=self.ways[way][2],
            device_id_type=MESH,
        )

    def give(self, way, i):
        k, rows = self.rows(i)
        return pltpu.make_async_remote_copy(
            src_ref=self.held.at[way, k, rows],
            dst_ref=self.fin.at[way, self.own, rows],
            send_sem=self.give_sems[0].at[way, i],
            recv_sem=self.give_sems[1].at[way, i],
            device_id=(self.rep, self.core, self.block(k)),
            device_id_type=MESH,
        )

    def keep(self, way, i):
        k, rows = self.rows(i)
        own = self.own if self.blocks > 1 else 0
        src, dst = self.held.at[way, k, rows], self.fin.at[way, own, rows]
        return pltpu.make_async_copy(src, dst, self.keep_sems.at[way, i])

    def loaded(self, way, i):
        if i % self.cuts == 0:
            for load in self.loads(way, i // self.cuts):
                load.wait()

    def prime(self):
        for way in range(2):

            @pl.when(self.ways[way][0])
            def _(way=way):
                for i in range(self.count):
                    self.loaded(way, i)
                    self.chain(way, i).start()

    def add(self, way, i):
        first, last = self.ways[way][:2]
        k, rows = self.rows(i)

        @pl.when(jnp.logical_not(first))
        def _():
            self.loaded(way, i)
            self.chain(way, i).wait_recv()
            self.held[way, k, rows] = self.held[way, k, rows] + self.landed[way, k, rows]

            @pl.when(jnp.logical_not(last))
            def _():
                self.chain(way, i).start()

            @pl.when(last)
            def _():
                if k == 0:
                    self.keep(way, i).start()
                else:
                    self.give(way, i).start()

    def step(self, i):
        skewed(self.rep, self.reps, self.count, self.add, i)

    def stage(self, n):
        if n == 1:
            self.prime()
        if n in self.steps:
            for i in self.steps[n]:
                self.step(i)
        if n == 7:
            for way in range(2):
                last = self.ways[way][1]
                for i in range(self.count):

                    @pl.when(jnp.logical_not(last))
                    def _(way=way, i=i):
                        self.chain(way, i).wait_send()

                    @pl.when(last)
                    def _(way=way, i=i):
                        if i // self.cuts == 0:
                            self.keep(way, i).wait()
                        else:
                            self.give(way, i).wait()


class HandJob:
    def __init__(self, source, reps):
        self.inner = isinstance(source, SumJob)
        self.sums = source if self.inner else None
        shape = source.outs[0].shape if self.inner else source.shape
        self.arrays = [] if self.inner else [source]
        self.reps, self.blocks = reps, shape[1]
        self.corner = False
        self.outs = [jax.ShapeDtypeStruct((2, 2) + shape[1:], BF16)]
        self.scratch = [pltpu.SemaphoreType.DMA((2, self.blocks))] * 5

    def open(self, arrays, outs, scratch, place):
        self.fin = None if self.inner else arrays[0]
        self.out = outs[0]
        self.hand_sems, self.side_sems, self.keep_sems = scratch[:2], scratch[2:4], scratch[4]
        self.rep, self.core, self.own = place[:3]
        self.ways = column_place(place, self.reps)

    def remote(self, src, way, j, sems, device):
        return pltpu.make_async_remote_copy(
            src_ref=src,
            dst_ref=self.out.at[way, self.core, j],
            send_sem=sems[0].at[way, j],
            recv_sem=sems[1].at[way, j],
            device_id=device,
            device_id_type=MESH,
        )

    def beside(self):
        return (self.rep, 1 - self.core, self.own)

    def begin(self):
        fin = self.sums.fin if self.inner else self.fin
        for j in range(self.blocks):
            for way in range(2):

                @pl.when(self.ways[way][1])
                def _(way=way, j=j):
                    src = fin.at[way, j]
                    self.remote(src, way, j, self.hand_sems, self.ways[way][3]).start()
                    self.remote(src, way, j, self.side_sems, self.beside()).start()
                    dst = self.out.at[way, self.core, j]
                    pltpu.make_async_copy(src, dst, self.keep_sems.at[way, j]).start()

    def hand(self, way, j):
        first, last = self.ways[way][:2]

        @pl.when(jnp.logical_not(last))
        def _():
            ref = self.out.at[way, self.core, j]
            hand = self.remote(ref, way, j, self.hand_sems, self.ways[way][3])
            hand.wait_recv()

            @pl.when(jnp.logical_not(first))
            def _():
                hand.start()

            self.remote(ref, way, j, self.side_sems, self.beside()).start()

    def pass_on(self):
        for j in range(self.blocks + 1):
            skewed(self.rep, self.reps, self.blocks, lambda w, i: self.hand(1 - w, i), j)

    def close(self):
        for j in range(self.blocks):
            for way in range(2):
                first, last = self.ways[way][:2]
                ref = self.out.at[way, self.core, j]
                self.remote(ref, way, j, self.side_sems, self.beside()).wait()

                @pl.when(jnp.logical_not(first))
                def _(way=way, j=j, ref=ref):
                    self.remote(ref, way, j, self.hand_sems, self.ways[way][3]).wait_send()

                @pl.when(last)
                def _(way=way, j=j, ref=ref):
                    pltpu.make_async_copy(ref, ref, self.keep_sems.at[way, j]).wait()

    def stage(self, n):
        if n == (7 if self.inner else 0):
            self.begin()
        if n == (8 if self.inner else 6):
            self.pass_on()
        if n == 9:
            self.close()


class Jobs:
    def __init__(self, jobs, reps):
        self.jobs, self.reps = jobs, reps
        self.arrays = [a for job in jobs for a in job.arrays]
        self.out_shapes = [o for job in jobs for o in job.outs]
        self.scratch = [x for job in jobs for x in job.scratch]

    def greet(self, place):
        rep, core, own, across, down, corner = place
        devices = [(rep, core, across), (rep, core, down), (rep, 1 - core, own)]
        if self.jobs:
            devices += [((rep + 1) % self.reps, core, own)]
            devices += [((rep + self.reps - 1) % self.reps, core, own)]
        if any(job.corner for job in self.jobs):
            devices.append((rep, core, corner))
        meet(devices)

    def open(self, arrays, outs, scratch, place):
        arrays, outs, scratch = list(arrays), list(outs), list(scratch)

        def take(refs, count):
            taken = refs[:count]
            del refs[:count]
            return taken

        for job in self.jobs:
            mine = [take(arrays, len(job.arrays)), take(outs, len(job.outs))]
            job.open(*mine, take(scratch, len(job.scratch)), place)

    def stage(self, n):
        for job in self.jobs:
            job.stage(n)


def gather_kernel(count, jobs, *refs):
    arrays, outs = len(jobs.arrays), len(jobs.out_shapes)
    xs, job_arrays = refs[:count], refs[count : count + arrays]
    refs = refs[count + arrays :]
    x_outs, job_outs = refs[:count], refs[count : count + outs]
    refs = refs[count + outs :]
    local_sems, send_sems, recv_sems = refs[:3]
    place = plane_position()
    jobs.greet(place)
    sender = Sender(send_sems, recv_sems)
    moves = [
        Gather(sender, x, out, local_sems.at[i], place)
        for i, (x, out) in enumerate(zip(xs, x_outs))
    ]
    for move in moves:
        move.begin()
    jobs.open(job_arrays, job_outs, refs[3:], place)
    jobs.stage(0)
    jobs.stage(1)
    for move in moves:
        move.relay()
    jobs.stage(5)
    for move in moves:
        move.finish()
    sender.finish()
    for n in (6, 7, 8, 9):
        jobs.stage(n)


def gather_plane(blocks, collective_id, jobs=(), reps=1):
    count = len(blocks)
    jobs = Jobs(jobs, reps)
    return pl.pallas_call(
        functools.partial(gather_kernel, count, jobs),
        out_shape=[jax.ShapeDtypeStruct((8,) + x.shape, x.dtype) for x in blocks]
        + jobs.out_shapes,
        in_specs=[HBM] * (count + len(jobs.arrays)),
        out_specs=[HBM] * (count + len(jobs.out_shapes)),
        scratch_shapes=[
            pltpu.SemaphoreType.DMA((count,)),
            pltpu.SemaphoreType.DMA((13 * count,)),
            pltpu.SemaphoreType.DMA((13 * count,)),
        ]
        + jobs.scratch,
        compiler_params=params(collective_id, 60),
        cost_estimate=link_cost(40 * count),
    )(*blocks, *jobs.arrays)


def quarter_kernel(gate_ref, up_ref, out_ref, local_sems, send_sems, recv_sems):
    rep, core, own, across, down, corner = plane_position()
    peers = (corner, across, down)
    meet([(rep, core, peer) for peer in peers])
    rows = out_ref.shape[1]
    width = out_ref.shape[2] // 2
    mine = pl.ds(pl.multiple_of(rep * rows, rows), rows)

    def source(ref, block):
        columns = pl.ds(pl.multiple_of((block * 2 + core) * width, width), width)
        return ref.at[mine, columns]

    sender = Sender(send_sems, recv_sems)
    for peer in peers:
        for k, ref in enumerate((gate_ref, up_ref)):
            target = out_ref.at[own, :, pl.ds(k * width, width)]
            sender.send(source(ref, peer), target, (rep, core, peer))
    local = []
    for k, ref in enumerate((gate_ref, up_ref)):
        copy = pltpu.make_async_copy(
            source(ref, own), out_ref.at[own, :, pl.ds(k * width, width)], local_sems.at[k]
        )
        copy.start()
        local.append(copy)
    for copy in sender.copies:
        copy.wait_recv()
    sender.finish()
    for copy in local:
        copy.wait()


def quarter_columns(w_gate, w_up, reps, collective_id):
    rows, columns = w_gate.shape
    return pl.pallas_call(
        quarter_kernel,
        out_shape=jax.ShapeDtypeStruct((4, rows // reps, columns // 4), BF16),
        in_specs=[HBM, HBM],
        out_specs=HBM,
        scratch_shapes=[
            pltpu.SemaphoreType.DMA((2,)),
            pltpu.SemaphoreType.DMA((6,)),
            pltpu.SemaphoreType.DMA((6,)),
        ],
        compiler_params=params(collective_id, 60),
        cost_estimate=link_cost(25),
    )(w_gate, w_up)


def start_kernel(
    x_ref, code_ref, gain_ref, q_ref, k_ref, v_ref,
    x_out, code_out, gain_out, q_out, k_out, v_out,
    local_sems, send_sems, recv_sems,
):
    place = plane_position()
    rep, core, own, across, down, corner = place
    peers = (corner, across, down)
    meet([(rep, core, peer) for peer in peers] + [(rep, 1 - core, peer) for peer in peers]
         + [(rep, 1 - core, own)])
    sender = Sender(send_sems, recv_sems)
    direct, local = [], []

    def keep(src, dst):
        copy = pltpu.make_async_copy(src, dst, local_sems.at[1 + len(local)])
        copy.start()
        local.append(copy)

    def columns(ref, block, width):
        return ref.at[:, pl.ds(pl.multiple_of(block * width, width), width)]

    def weights():
        for peer in peers:
            there = (rep, core, peer)
            direct.append(sender.send(gain_ref, gain_out.at[own], there))
            direct.append(sender.send(columns(q_ref, peer * 2 + core, 256), q_out.at[own], there))
            direct.append(sender.send(columns(k_ref, peer, 128), k_out.at[own], there))
            direct.append(sender.send(columns(v_ref, peer, 128), v_out.at[own], there))
            direct.append(sender.send(code_ref, code_out.at[core * 4 + own], there))
            other = (rep, 1 - core, peer)
            direct.append(sender.send(code_ref, code_out.at[core * 4 + own], other))
        direct.append(sender.send(code_ref, code_out.at[core * 4 + own], (rep, 1 - core, own)))
        keep(gain_ref, gain_out.at[own])
        keep(columns(q_ref, own * 2 + core, 256), q_out.at[own])
        keep(columns(k_ref, own, 128), k_out.at[own])
        keep(columns(v_ref, own, 128), v_out.at[own])
        keep(code_ref, code_out.at[core * 4 + own])

    move = Gather(sender, x_ref, x_out, local_sems.at[0], place)
    move.begin()
    weights()
    move.relay()
    move.finish()
    for copy in direct:
        copy.wait_recv()
    sender.finish()
    for copy in local:
        copy.wait()


def start_plane(hidden, codes, gains, w_query, w_key, w_value, collective_id):
    rows = w_query.shape[0]
    shapes = [
        ((8,) + hidden.shape, BF16),
        ((8,) + codes.shape, jnp.int32),
        ((4,) + gains.shape, BF16),
        ((4, rows, GROUPS * HD), BF16),
        ((4, rows, 2 * HD), BF16),
        ((4, rows, 2 * HD), BF16),
    ]
    return pl.pallas_call(
        start_kernel,
        out_shape=[jax.ShapeDtypeStruct(s, d) for s, d in shapes],
        in_specs=[HBM] * 6,
        out_specs=[HBM] * 6,
        scratch_shapes=[
            pltpu.SemaphoreType.DMA((6,)),
            pltpu.SemaphoreType.DMA((32,)),
            pltpu.SemaphoreType.DMA((32,)),
        ],
        compiler_params=params(collective_id, 60),
        cost_estimate=link_cost(60),
    )(hidden, codes, gains, w_query, w_key, w_value)


def product_scatter_kernel(turned, count, jobs, *refs):
    arrays, outs = len(jobs.arrays), len(jobs.out_shapes)
    x_hbm, w_hbm, job_arrays = refs[:count], refs[count], refs[count + 1 : count + 1 + arrays]
    refs = refs[count + 1 + arrays :]
    out_ref, job_outs = refs[0], refs[1 : 1 + outs]
    refs = refs[1 + outs :]
    x_refs, w_ref = refs[:count], refs[count]
    (
        swap, held, from_core, from_across, from_down, last_across, last_down,
        x_sems, w_sems, core_send, core_recv, send_sems, recv_sems,
    ) = refs[count + 1 : count + 14]
    place = plane_position()
    rep, core, own, across, down, corner = place
    to_across, to_down, to_core = (rep, core, across), (rep, core, down), (rep, 1 - core, own)
    _, rows, wide = held.shape
    depth = x_refs[0].shape[1]
    tile = 512
    tiles = wide // tile
    half = rows // 2
    low, high = pl.ds(0, half), pl.ds(half, half)
    order = []
    for block in (corner, across, down, own):
        order += [(1 - core) * 4 + block, core * 4 + block]

    def rows_of(block):
        return pl.ds(pl.multiple_of(block * rows, rows), rows)

    x_loads = [
        [
            pltpu.make_async_copy(
                x_hbm[i].at[rows_of(block)], x_refs[i].at[rows_of(block)], x_sems.at[i, n]
            )
            for i in range(count)
        ]
        for n, block in enumerate(order)
    ]
    w_loads = []
    for t in range(tiles):
        columns = pl.ds(t * tile, tile)
        if turned:
            src, dst = w_hbm.at[columns], w_ref.at[columns]
        else:
            kept = pl.ds(pl.multiple_of(core * depth, depth), depth)
            src, dst = w_hbm.at[kept, columns], w_ref.at[:, columns]
        w_loads.append(pltpu.make_async_copy(src, dst, w_sems.at[t]))
    for load in x_loads[0]:
        load.start()
    for load in w_loads:
        load.start()
    for loads in x_loads[1:]:
        for load in loads:
            load.start()
    jobs.open(job_arrays, job_outs, refs[count + 14 :], place)
    jobs.greet(place)
    jobs.stage(0)

    def product(dst, mine, columns):
        total = None
        for i in range(count):
            x = x_refs[i][mine, :]
            if turned:
                w = w_ref[columns, pl.ds(i * depth, depth)]
                part = lax.dot_general(
                    x, w, (((1,), (1,)), ((), ())), preferred_element_type=F32
                )
            else:
                part = dot_f32(x, w_ref[:, columns])
            total = part if total is None else total + part
        dst[:, columns] = total.astype(BF16)

    def fill(dst, n):
        for load in x_loads[n]:
            load.wait()
        mine = rows_of(order[n])
        if n == 0:
            for t in range(tiles):
                w_loads[t].wait()
                product(dst, mine, pl.ds(t * tile, tile))
        else:

            @pl.loop(0, tiles)
            def _(t):
                product(dst, mine, pl.ds(pl.multiple_of(t * tile, tile), tile))

    swaps = Sender(core_send, core_recv)
    sender = Sender(send_sems, recv_sems)
    sent = {}
    for k in range(4):
        fill(swap.at[k], 2 * k)
        swaps.send(swap.at[k], from_core.at[k], to_core)
        fill(held.at[k], 2 * k + 1)
        swaps.copies[k].wait_recv()
        held[k] = held[k] + from_core[k]
        if k == 0:
            sent[0] = sender.send(held.at[0, low], from_across.at[0], to_across)
            sent[1] = sender.send(held.at[0, high], from_down.at[0], to_down)
        if k == 1:
            sent[2] = sender.send(held.at[1, low], from_across.at[1], to_across)
        if k == 2:
            sent[3] = sender.send(held.at[2, high], from_down.at[1], to_down)
        jobs.stage(1 + k)
    sent[0].wait_recv()
    held[2, low] = held[2, low] + from_across[0]
    to_last = sender.send(held.at[2, low], last_down, to_down)
    sent[1].wait_recv()
    held[1, high] = held[1, high] + from_down[0]
    across_last = sender.send(held.at[1, high], last_across, to_across)
    jobs.stage(5)
    sent[2].wait_recv()
    sent[3].wait_recv()
    to_last.wait_recv()
    out_ref[low] = (
        held[3, low].astype(F32) + from_across[1].astype(F32) + last_down[...].astype(F32)
    )
    across_last.wait_recv()
    out_ref[high] = (
        held[3, high].astype(F32) + from_down[1].astype(F32) + last_across[...].astype(F32)
    )
    swaps.finish()
    sender.finish()
    for n in (6, 7, 8, 9):
        jobs.stage(n)


def product_scatter(xs, w, turned, collective_id, jobs=(), reps=1):
    count = len(xs)
    jobs = Jobs(jobs, reps)
    tokens, depth = xs[0].shape
    rows = tokens // 8
    wide = w.shape[0] if turned else w.shape[1]
    half = rows // 2
    return pl.pallas_call(
        functools.partial(product_scatter_kernel, turned, count, jobs),
        out_shape=[jax.ShapeDtypeStruct((rows, wide), F32)] + jobs.out_shapes,
        in_specs=[HBM] * (count + 1 + len(jobs.arrays)),
        out_specs=[VM] + [HBM] * len(jobs.out_shapes),
        scratch_shapes=[pltpu.VMEM((tokens, depth), BF16)] * count
        + [
            pltpu.VMEM((wide, depth * count) if turned else (depth, wide), BF16),
            pltpu.VMEM((4, rows, wide), BF16),
            pltpu.VMEM((4, rows, wide), BF16),
            pltpu.VMEM((4, rows, wide), BF16),
            pltpu.VMEM((2, half, wide), BF16),
            pltpu.VMEM((2, half, wide), BF16),
            pltpu.VMEM((half, wide), BF16),
            pltpu.VMEM((half, wide), BF16),
            pltpu.SemaphoreType.DMA((count, 8)),
            pltpu.SemaphoreType.DMA((wide // 512,)),
            pltpu.SemaphoreType.DMA((4,)),
            pltpu.SemaphoreType.DMA((4,)),
            pltpu.SemaphoreType.DMA((6,)),
            pltpu.SemaphoreType.DMA((6,)),
        ]
        + jobs.scratch,
        compiler_params=params(collective_id, 60),
        cost_estimate=link_cost(44, 2 * tokens * depth * count * wide),
    )(*xs, w, *jobs.arrays)


def cast_rows_kernel(x_ref, out_ref):
    out_ref[...] = x_ref[0, 0].astype(F32)


def cast_rows(spread):
    reps, subs, rows, columns = spread.shape
    return pl.pallas_call(
        cast_rows_kernel,
        grid=(subs, reps),
        out_shape=jax.ShapeDtypeStruct((reps * subs * rows, columns), F32),
        in_specs=[pl.BlockSpec((1, 1, rows, columns), lambda s, r: (r, s, 0, 0))],
        out_specs=pl.BlockSpec((rows, columns), lambda s, r: (s * reps + r, 0)),
        cost_estimate=link_cost(8),
    )(spread)


def cast_columns_kernel(x_ref, out_ref):
    _, subs, owners, _, columns = x_ref.shape
    for j in range(owners):
        for s in range(subs):
            at = (j * subs + s) * columns
            out_ref[:, at : at + columns] = x_ref[0, s, j].astype(F32)


def cast_columns(handed, columns):
    parts, subs, owners, rows, _ = handed.shape
    wide = owners * subs * columns
    cuts = 4
    block = (1, subs, owners, rows // cuts, columns)
    return pl.pallas_call(
        cast_columns_kernel,
        grid=(parts, cuts),
        out_shape=jax.ShapeDtypeStruct((parts * rows, wide), F32),
        in_specs=[pl.BlockSpec(block, lambda r, h: (r, 0, 0, h, 0))],
        out_specs=pl.BlockSpec((rows // cuts, wide), lambda r, h: (r * cuts + h, 0)),
        cost_estimate=link_cost(8),
    )(handed)


def cast_heads_kernel(q_ref, kv_ref, q_out, k_out, v_out):
    _, subs, owners, _, columns = q_ref.shape
    for j in range(owners):
        for s in range(subs):
            at = (j * subs + s) * columns
            q_out[:, at : at + columns] = q_ref[0, s, j].astype(F32)
        pair = [kv_ref[0, s, j].astype(F32) for s in range(subs)]
        wide = HD * subs
        at = j * wide
        k_out[:, at : at + wide] = jnp.concatenate([p[:, :HD] for p in pair], axis=1)
        v_out[:, at : at + wide] = jnp.concatenate([p[:, HD:] for p in pair], axis=1)


def cast_heads(handed, skip):
    parts, subs, owners, rows, _ = handed.shape
    q_wide, k_wide = GROUPS * HD, 2 * HD
    members = owners * subs

    def source(wide, at):
        return pl.BlockSpec((1, subs, owners, rows, wide), lambda r: (r, 0, 0, 0, at // wide))

    def shape(wide):
        return jax.ShapeDtypeStruct((parts * rows, wide), F32)

    widths = (members * q_wide, members * HD, members * HD)
    return pl.pallas_call(
        cast_heads_kernel,
        grid=(parts,),
        out_shape=[shape(w) for w in widths],
        in_specs=[source(q_wide, skip), source(k_wide, skip + q_wide)],
        out_specs=[pl.BlockSpec((rows, w), lambda r: (r, 0)) for w in widths],
        compiler_params=pltpu.CompilerParams(vmem_limit_bytes=48 << 20),
        cost_estimate=link_cost(5),
    )(handed, handed)


def tally_kernel(x_ref, out_ref, plane, planes, total, sems, plane_sems):
    rep, core, own, _, _, _ = plane_position()
    reps = planes.shape[0]
    mates = [(c, j) for c in range(2) for j in range(4)][1:]
    others = [(rep, (core + c) % 2, (own + j) % 4) for c, j in mates]
    above = [((rep + r) % reps, core, own) for r in range(1, reps)]
    meet(others + above)
    sender = Sender(sems.at[0], sems.at[1])
    for device in others:
        sender.send(x_ref, plane.at[core * 4 + own], device)
    plane[core * 4 + own] = x_ref[...]
    for copy in sender.copies:
        copy.wait_recv()
    mine = plane[0]
    for k in range(1, 8):
        mine = mine + plane[k]
    total[...] = mine
    climber = Sender(plane_sems.at[0], plane_sems.at[1])
    for device in above:
        climber.send(total, planes.at[rep], device)
    planes[rep] = mine
    for copy in climber.copies:
        copy.wait_recv()
    whole = planes[0]
    for k in range(1, reps):
        whole = whole + planes[k]
    out_ref[...] = whole
    sender.finish()
    climber.finish()


def tally_all(values, reps, collective_id):
    size = values.shape[0]
    rows = -(-size // 1024) * 8
    padded = jnp.pad(values, (0, rows * 128 - size)).reshape(rows, 128)
    block = pltpu.VMEM((rows, 128), F32)
    summed = pl.pallas_call(
        tally_kernel,
        out_shape=jax.ShapeDtypeStruct((rows, 128), F32),
        in_specs=[VM],
        out_specs=VM,
        scratch_shapes=[
            pltpu.VMEM((8, rows, 128), F32),
            pltpu.VMEM((reps, rows, 128), F32),
            block,
            pltpu.SemaphoreType.DMA((2, 7)),
            pltpu.SemaphoreType.DMA((2, reps - 1)),
        ],
        compiler_params=params(collective_id),
        cost_estimate=link_cost(10),
    )(padded)
    return summed.reshape(-1)[:size]


def column_blocks(weight, owners, subs):
    rows, columns = weight.shape
    blocked = weight.reshape(rows, owners, subs, columns // (owners * subs))
    mine = lax.dynamic_index_in_dim(blocked, lax.axis_index("sub"), axis=2, keepdims=False)
    return jnp.swapaxes(mine, 0, 1)


def regroup_columns(weights, owners, subs):
    blocks = jnp.concatenate([column_blocks(w, owners, subs) for w in weights], axis=-1)
    moved = lax.all_to_all(blocks, "fsdp", split_axis=0, concat_axis=0, tiled=True)
    return moved.reshape(-1, moved.shape[-1])


def row_block(weight, subs):
    rows = weight.shape[0] // subs
    return lax.dynamic_slice_in_dim(weight, lax.axis_index("sub") * rows, rows, axis=0)


def gather_tokens(block):
    return lax.all_gather(block, ("sub", "fsdp"), axis=0, tiled=True)


def scatter_tokens(partial):
    return lax.psum_scatter(partial, ("sub", "fsdp"), scatter_dimension=0, tiled=True)


def sum_planes(term):
    return lax.psum_scatter(term, "rep", scatter_dimension=0, tiled=True)


def spread_planes(piece):
    rep, subs = lax.axis_size("rep"), lax.axis_size("sub")
    spread = lax.all_gather(piece, ("rep", "sub"), axis=0, tiled=False)
    return spread.reshape((rep, subs) + piece.shape)


def owner_major(term):
    owners, rep = lax.axis_size("fsdp"), lax.axis_size("rep")
    rows, columns = term.shape
    blocked = jnp.swapaxes(term.reshape(owners, rep, rows // (owners * rep), columns), 0, 1)
    return blocked.reshape(rows, columns)


def to_owners(piece):
    blocked = piece.reshape(lax.axis_size("fsdp"), -1, piece.shape[1])
    return lax.all_to_all(blocked, "fsdp", split_axis=0, concat_axis=0, tiled=True)


def place_columns(spread):
    reps, subs, owners, rows, columns = spread.shape
    part = jnp.transpose(spread, (0, 3, 2, 1, 4))
    return part.reshape(reps * rows, owners * subs * columns).astype(F32)


def shards(
    kernels,
    hidden_in,
    segment_ids,
    valid_mask,
    cotangent,
    norm_attn,
    w_query,
    w_key,
    w_value,
    w_output,
    norm_mlp,
    w_gate,
    w_up,
    w_down,
):
    owners, subs, reps = lax.axis_size("fsdp"), lax.axis_size("sub"), lax.axis_size("rep")
    members = owners * subs
    length, width = hidden_in.shape[1:]
    tokens = members * length
    q_width, k_width = GROUPS * HD, HD

    def gathered(blocks, collective_id, jobs=()):
        if kernels:
            outs = list(gather_plane(blocks, collective_id, jobs, reps))
        else:
            outs = [gather_tokens(block) for block in blocks]
        return [o.reshape(tokens, -1) for o in outs[: len(blocks)]] + outs[len(blocks) :]

    def scattered(xs, w, turned, collective_id, jobs=()):
        if kernels:
            return product_scatter(xs, w, turned, collective_id, jobs, reps)
        x = jnp.concatenate(xs, axis=1)
        product = contract_cols(x, w) if turned else dot_f32(x, row_block(w, subs))
        return [scatter_tokens(product.astype(BF16)).astype(F32)]

    codes = segment_ids * 2 + valid_mask
    gains = jnp.stack([norm_attn, norm_mlp])
    result_grad = cotangent[0].astype(F32)
    mlp_out_low = (RESIDUAL_SCALE * result_grad).astype(BF16)
    if kernels:
        quarter = quarter_columns(w_gate, w_up, reps, 0)
        hidden_tied = after(hidden_in[0], quarter)
        hidden_low, codes, gains, q_cols, k_cols, v_cols = start_plane(
            hidden_tied, codes, gains, w_query, w_key, w_value, 1
        )
        hidden_low = hidden_low.reshape(tokens, width)
        codes = codes.reshape(members, length)
        gains = jnp.swapaxes(gains, 0, 1).reshape(2, width)
        core_at = lax.axis_index("sub") * HD
        qkv = jnp.concatenate(
            [
                q_cols,
                lax.dynamic_slice_in_dim(k_cols, core_at, HD, axis=2),
                lax.dynamic_slice_in_dim(v_cols, core_at, HD, axis=2),
            ],
            axis=2,
        ).reshape(width, q_width + 2 * k_width)
        gate_up = lax.all_gather(quarter, "rep", axis=1, tiled=True).reshape(width, -1)
    else:
        gains = lax.all_gather(gains, "fsdp", axis=1, tiled=True)
        codes = gather_tokens(codes)
        hidden_low = gather_tokens(hidden_in[0])
        qkv = regroup_columns((w_query, w_key, w_value), owners, subs)
        gate_up = regroup_columns((w_gate, w_up), owners, subs)
    gain_attn = gains[0].astype(F32)
    gain_mlp = gains[1].astype(F32)
    ff = gate_up.shape[1] // 2

    hidden_all = hidden_low.astype(F32)
    normed_one = (hidden_all * row_scale(hidden_all) * gain_attn).astype(BF16)
    projected = dot_f32(normed_one, qkv)
    cos_table, sin_table = rope_tables(length, HD)
    cos_heads = cos_table[None, :, None, :]
    sin_heads = sin_table[None, :, None, :]
    per_seq = projected.reshape(members, length, GROUPS + 2, HD)
    queries = rotate(per_seq[:, :, :GROUPS], cos_heads, sin_heads).astype(BF16)
    keys = rotate(per_seq[:, :, GROUPS : GROUPS + 1], cos_heads, sin_heads).astype(BF16)[:, :, 0]
    values = per_seq[:, :, GROUPS + 1].astype(BF16)

    segments, validity = codes // 2, codes % 2
    row_index = jnp.arange(length, dtype=jnp.int32)[:, None]
    col_index = jnp.arange(length, dtype=jnp.int32)[None, :]
    allowed = (
        (segments[:, :, None] == segments[:, None, :])
        & (col_index <= row_index)
        & ((validity[:, None, :] == 1) | (col_index == row_index))
    )[:, None]
    scores = jnp.einsum("stgd,sud->sgtu", queries, keys, preferred_element_type=F32) * SCORE_SCALE
    scores = jnp.where(allowed, scores, MASKED_SCORE)
    shifted = jnp.exp(scores - jnp.max(scores, axis=-1, keepdims=True))
    probs = shifted / jnp.sum(shifted, axis=-1, keepdims=True)
    probs_low = probs.astype(BF16)
    attended = jnp.einsum("sgtu,sud->stgd", probs_low, values, preferred_element_type=F32)
    attended = attended.reshape(tokens, q_width).astype(BF16)
    (attn_branch,) = scattered([attended], w_output, False, 2)

    hidden = hidden_in[0].astype(F32)
    scale_one = row_scale(hidden)
    unit_one = hidden * scale_one
    middle = hidden + RESIDUAL_SCALE * attn_branch
    scale_two = row_scale(middle)
    unit_two = middle * scale_two
    normed_two, mlp_out_grad = gathered([(unit_two * gain_mlp).astype(BF16), mlp_out_low], 3)
    gate_up_proj = dot_f32(normed_two, gate_up)
    gate_proj, up_proj = gate_up_proj[:, :ff], gate_up_proj[:, ff:]
    sigma = jax.nn.sigmoid(gate_proj)
    silu_gate = gate_proj * sigma
    mixed_act = (silu_gate * up_proj).astype(BF16)

    down_w_grad = contract_rows(mixed_act, mlp_out_grad).astype(BF16)
    down_w_piece = sum_planes(down_w_grad)
    mixed_grad = contract_cols(after(mlp_out_grad, down_w_grad), row_block(w_down, subs))
    slope = sigma * (1.0 + gate_proj * (1.0 - sigma))
    gate_grad = (mixed_grad * up_proj * slope).astype(BF16)
    up_grad = (mixed_grad * silu_gate).astype(BF16)
    gate_w_grad = contract_rows(normed_two, gate_grad).astype(BF16)
    up_w_grad = contract_rows(normed_two, up_grad).astype(BF16)
    gate_sum = sum_planes(owner_major(gate_w_grad))
    gate_up_grad = [after(gate_grad, gate_w_grad, up_w_grad), up_grad]
    (normed_two_grad,) = scattered(gate_up_grad, gate_up, True, 4)
    gain_mlp_grad, middle_part = norm_backward(normed_two_grad, scale_two, unit_two, gain_mlp)
    middle_grad = result_grad + middle_part

    attn_out_low = (RESIDUAL_SCALE * middle_grad).astype(BF16)
    down_spread = spread_planes(after(down_w_piece, normed_two_grad))
    (attn_out_grad,) = gathered([attn_out_low], 5)
    attended_grad = contract_cols(attn_out_grad, row_block(w_output, subs)).astype(BF16)
    output_w_grad = contract_rows(attended, attn_out_grad).astype(BF16)
    heads_grad = attended_grad.reshape(members, length, GROUPS, HD)
    prob_grad = jnp.einsum("stgd,sud->sgtu", heads_grad, values, preferred_element_type=F32)
    row_dot = jnp.sum(probs * prob_grad, axis=-1, keepdims=True)
    score_grad = (probs * (prob_grad - row_dot)).astype(BF16)
    query_grad = (
        jnp.einsum("sgtu,sud->stgd", score_grad, keys, preferred_element_type=F32) * SCORE_SCALE
    )
    key_grad = (
        jnp.einsum("sgtu,stgd->sud", score_grad, queries, preferred_element_type=F32) * SCORE_SCALE
    )
    value_grad = jnp.einsum("sgtu,stgd->sud", probs_low, heads_grad, preferred_element_type=F32)
    qkv_grad = jnp.concatenate(
        [
            rotate(query_grad, cos_heads, -sin_heads),
            rotate(key_grad[:, :, None], cos_heads, -sin_heads),
            value_grad[:, :, None],
        ],
        axis=2,
    )
    qkv_grad = qkv_grad.reshape(tokens, q_width + 2 * k_width).astype(BF16)
    qkv_tied = after(qkv_grad, output_w_grad, down_spread)
    (normed_one_grad,) = scattered([qkv_tied], qkv, True, 6)
    qkv_grad = after(qkv_grad, normed_one_grad, gate_sum)
    qkv_w_grad = contract_rows(normed_one, qkv_grad).astype(BF16)
    gain_attn_grad, hidden_part = norm_backward(normed_one_grad, scale_one, unit_one, gain_attn)
    input_grad = (middle_grad + hidden_part).astype(BF16)

    mixed_tied = after(mixed_act, normed_one_grad, qkv_w_grad)
    last_jobs = []
    if kernels:
        up_job = SumJob(
            [up_w_grad, qkv_w_grad], 4, 2, reps, {1: (0, 1), 2: (2, 3), 3: (4, 5), 4: (6, 7, 8)}
        )
        output_job = SumJob([output_w_grad], 1, 1, reps, {4: (0, 1)})
        last_jobs = [ExchangeJob(gate_sum), up_job, output_job]
        last_jobs += [HandJob(up_job, reps), HandJob(output_job, reps)]
    mlp_branch, *last = scattered([mixed_tied], w_down, False, 7, last_jobs)
    result = middle + RESIDUAL_SCALE * mlp_branch

    validity_own = valid_mask[0].astype(F32)[:, None]
    squares = [
        jnp.sum(tensor * tensor * validity_own)
        for tensor in (hidden, middle, result, attn_branch, mlp_branch)
    ]
    tally = jnp.concatenate(
        [gain_attn_grad, gain_mlp_grad, jnp.stack(squares + [jnp.sum(validity_own)])]
    )
    tally = tally_all(tally, reps, 8) if kernels else lax.psum(tally, ("rep", "sub", "fsdp"))
    part = width // owners
    start = lax.axis_index("fsdp") * part
    gain_attn_out = lax.dynamic_slice_in_dim(tally, start, part)
    gain_mlp_out = lax.dynamic_slice_in_dim(tally, width + start, part)
    statistics = jnp.sqrt(tally[2 * width : 2 * width + 5] / (tally[2 * width + 5] * width))

    if kernels:
        gate_piece, _, _, up_handed, output_handed = last
        gate_spread = spread_planes(gate_piece)
        down_out = cast_rows(down_spread)
        output_out = cast_rows(output_handed.reshape((2, 2) + output_handed.shape[3:]))
        gate_out, up_out = cast_columns(gate_spread, ff), cast_columns(up_handed, ff)
        query_out, key_out, value_out = cast_heads(up_handed, ff)
    else:
        down_out, output_out = (
            jnp.swapaxes(s, 0, 1).reshape(-1, width).astype(F32)
            for s in (down_spread, spread_planes(sum_planes(output_w_grad)))
        )
        gate_spread, up_spread, qkv_spread = (
            spread_planes(to_owners(g))
            for g in (
                gate_sum,
                sum_planes(owner_major(up_w_grad)),
                sum_planes(owner_major(qkv_w_grad)),
            )
        )
        gate_out, up_out = place_columns(gate_spread), place_columns(up_spread)
        query_out = place_columns(qkv_spread[..., :q_width])
        key_out = place_columns(qkv_spread[..., q_width : q_width + k_width])
        value_out = place_columns(qkv_spread[..., q_width + k_width :])
    return (
        result.astype(BF16)[None],
        input_grad[None],
        gain_attn_out,
        query_out,
        key_out,
        value_out,
        output_out,
        gain_mlp_out,
        gate_out,
        up_out,
        down_out,
        statistics,
    )


def solution(mesh):
    fsdp = mesh.shape["fsdp"]
    subs = max(1, KV // fsdp)
    rep = mesh.shape["dp"] // subs
    kernels = fsdp == 4 and subs == 2 and rep >= 3
    plane_mesh = Mesh(mesh.devices.reshape(rep, subs, fsdp), ("rep", "sub", "fsdp"))
    batch = ("rep", "sub", "fsdp")
    return jax.shard_map(
        functools.partial(shards, kernels),
        mesh=plane_mesh,
        in_specs=(
            P(batch, None, None),
            P(batch, None),
            P(batch, None),
            P(batch, None, None),
            P("fsdp"),
            P("fsdp", None),
            P("fsdp", None),
            P("fsdp", None),
            P("fsdp", None),
            P("fsdp"),
            P("fsdp", None),
            P("fsdp", None),
            P("fsdp", None),
        ),
        out_specs=(
            P(batch, None, None),
            P(batch, None, None),
            P("fsdp"),
            P("fsdp", None),
            P("fsdp", None),
            P("fsdp", None),
            P("fsdp", None),
            P("fsdp"),
            P("fsdp", None),
            P("fsdp", None),
            P("fsdp", None),
            P(),
        ),
        check_vma=False,
    )
```

```python
import functools

import jax
import jax.numpy as jnp
from jax import lax
from jax.experimental import pallas as pl
from jax.experimental.pallas import tpu as pltpu
from jax.sharding import Mesh
from jax.sharding import PartitionSpec as P

H = 32
KV = 8
HD = 64
GROUPS = H // KV

EPSILON = 1e-05
RESIDUAL_SCALE = 0.22
SCORE_SCALE = 1.0 / 64.0
MASKED_SCORE = -1e30
ROPE_BASE = 10000000.0

BF16 = jnp.bfloat16
F32 = jnp.float32
MESH = pl.DeviceIdType.MESH
SCALE = 3_300_000
HBM = pl.BlockSpec(memory_space=pltpu.HBM)
VM = pl.BlockSpec(memory_space=pltpu.VMEM)


def rope_tables(length, head_size):
    half_size = head_size // 2
    frequency = ROPE_BASE ** (-(jnp.arange(half_size, dtype=F32) * 2.0 / head_size))
    angles = jnp.arange(length, dtype=F32)[:, None] * frequency[None, :]
    return (jnp.cos(angles), jnp.sin(angles))


def rotate(tensor, cos_table, sin_table):
    half_size = tensor.shape[-1] // 2
    front_half = tensor[..., :half_size]
    back_half = tensor[..., half_size:]
    return jnp.concatenate(
        [
            front_half * cos_table - back_half * sin_table,
            back_half * cos_table + front_half * sin_table,
        ],
        axis=-1,
    )


def dot_f32(left, right):
    return jnp.dot(left, right, preferred_element_type=F32)


def contract_rows(left, right):
    return jnp.einsum("sa,sb->ab", left, right, preferred_element_type=F32)


def contract_cols(left, right):
    return jnp.einsum("sb,ab->sa", left, right, preferred_element_type=F32)


def row_scale(source):
    return lax.rsqrt(jnp.mean(source * source, axis=-1, keepdims=True) + EPSILON)


def norm_backward(grad_norm, scale_row, unit_rows, gain):
    gain_grad = jnp.sum(grad_norm * unit_rows, axis=0)
    scaled = grad_norm * gain
    source_grad = scale_row * (
        scaled - unit_rows * jnp.mean(scaled * unit_rows, axis=-1, keepdims=True)
    )
    return (gain_grad, source_grad)


def after(value, *others):
    return lax.optimization_barrier((value,) + others)[0]


def plane_position():
    rep, core, own = lax.axis_index("rep"), lax.axis_index("sub"), lax.axis_index("fsdp")
    row, col = own // 2, own % 2
    across = row * 2 + (1 - col)
    down = (1 - row) * 2 + col
    corner = (1 - row) * 2 + (1 - col)
    return rep, core, own, across, down, corner


def meet(devices):
    barrier = pltpu.get_barrier_semaphore()
    for device in devices:
        pl.semaphore_signal(barrier, inc=1, device_id=device, device_id_type=MESH)
    pl.semaphore_wait(barrier, len(devices))


def params(collective_id, megabytes=16):
    return pltpu.CompilerParams(
        collective_id=collective_id, has_side_effects=True, vmem_limit_bytes=megabytes << 20
    )


def link_cost(microseconds, flops=0):
    return pl.CostEstimate(
        flops=0, bytes_accessed=int(microseconds * SCALE), transcendentals=0
    )


class Sender:
    def __init__(self, send_sems, recv_sems):
        self.send_sems, self.recv_sems, self.copies = send_sems, recv_sems, []

    def send(self, src, dst, device):
        copy = self.make(src, dst, device)
        copy.start()
        return copy

    def make(self, src, dst, device):
        index = len(self.copies)
        copy = pltpu.make_async_remote_copy(
            src_ref=src,
            dst_ref=dst,
            send_sem=self.send_sems.at[index],
            recv_sem=self.recv_sems.at[index],
            device_id=device,
            device_id_type=MESH,
        )
        self.copies.append(copy)
        return copy

    def finish(self):
        for copy in self.copies:
            copy.wait_send()


class Bounce:
    def __init__(self, src, dst, room, sems):
        self.fetch = pltpu.make_async_copy(src, room, sems.at[0])
        self.store = pltpu.make_async_copy(room, dst, sems.at[1])

    def start(self):
        self.fetch.start()

    def turn(self):
        self.fetch.wait()
        self.store.start()

    def wait(self):
        self.store.wait()


class Gather:
    def __init__(self, sender, x_ref, out_ref, local_sem, place):
        rep, core, own, across, down, corner = place
        to_across, to_down, to_core = (rep, core, across), (rep, core, down), (rep, 1 - core, own)
        half = x_ref.shape[0] // 2
        low, high, whole = pl.ds(0, half), pl.ds(half, half), pl.ds(0, 2 * half)
        base = core * 4

        def first(rows, device):
            return sender.make(x_ref.at[rows], out_ref.at[base + own, rows], device)

        def forward(block, rows, device):
            ref = out_ref.at[base + block, rows]
            return sender.make(ref, ref, device)

        self.across_low, self.down_high = first(low, to_across), first(high, to_down)
        self.across_high, self.down_low = first(high, to_across), first(low, to_down)
        self.corner_low = forward(across, low, to_down)
        self.corner_high = forward(down, high, to_across)
        self.swap_own = first(whole, to_core)
        self.swap_near = [
            forward(across, low, to_core),
            forward(down, high, to_core),
            forward(across, high, to_core),
            forward(down, low, to_core),
        ]
        self.swap_corner = [forward(corner, low, to_core), forward(corner, high, to_core)]
        self.mine = pltpu.make_async_copy(x_ref, out_ref.at[base + own], local_sem)

    def begin(self):
        for copy in (self.across_low, self.down_high, self.across_high, self.down_low):
            copy.start()
        self.swap_own.start()
        self.mine.start()

    def relay(self):
        self.across_low.wait_recv()
        self.corner_low.start()
        self.swap_near[0].start()
        self.down_high.wait_recv()
        self.corner_high.start()
        self.swap_near[1].start()
        self.across_high.wait_recv()
        self.swap_near[2].start()
        self.down_low.wait_recv()
        self.swap_near[3].start()

    def finish(self):
        self.corner_low.wait_recv()
        self.swap_corner[0].start()
        self.corner_high.wait_recv()
        self.swap_corner[1].start()
        for swap in [self.swap_own] + self.swap_near + self.swap_corner:
            swap.wait_recv()
        self.mine.wait()


class ExchangeJob:
    climbs = False
    corner = True

    def __init__(self, source):
        self.rows = source.shape[0] // 4
        shape = (self.rows, source.shape[1])
        self.arrays = [source]
        self.outs = [jax.ShapeDtypeStruct((4,) + shape, BF16)]
        self.scratch = [pltpu.SemaphoreType.DMA((3,))] * 2
        self.scratch += [pltpu.VMEM(shape, BF16), pltpu.SemaphoreType.DMA((2,))]

    def open(self, arrays, outs, scratch, place):
        self.source, self.out, self.place = arrays[0], outs[0], place
        own = place[2]
        self.sems = scratch[:2]
        self.keep = Bounce(self.part(own), self.out.at[own], scratch[2], scratch[3])

    def part(self, block):
        return self.source.at[pl.ds(pl.multiple_of(block * self.rows, 16), self.rows)]

    def stage(self, n):
        rep, core, own, across, down, corner = self.place
        if n == 0:
            self.keep.start()
            self.sender = Sender(*self.sems)
            for peer in (corner, across, down):
                self.sender.send(self.part(peer), self.out.at[own], (rep, core, peer))
        if n == 1:
            self.keep.turn()
        if n == 6:
            for copy in self.sender.copies:
                copy.wait()
            self.keep.wait()


class KeepJob:
    climbs = False
    corner = False

    def __init__(self, source):
        self.arrays = [source]
        self.outs = [jax.ShapeDtypeStruct(source.shape, BF16)]
        self.scratch = [pltpu.VMEM(source.shape, BF16), pltpu.SemaphoreType.DMA((2,))]

    def open(self, arrays, outs, scratch, place):
        self.keep = Bounce(arrays[0], outs[0], *scratch)

    def stage(self, n):
        if n == 0:
            self.keep.start()
        if n == 1:
            self.keep.turn()
        if n == 6:
            self.keep.wait()


def column_place(place, reps):
    rep, core, own = place[:3]
    up = (rep == 0, rep == reps - 1, (rep + 1, core, own), (rep - 1, core, own))
    down = (rep == reps - 1, rep == 0, (rep - 1, core, own), (rep + 1, core, own))
    return (up, down)


def skewed(rep, reps, count, act, i):
    for low in (True, False):
        near = 0 if low else 1

        @pl.when((rep * 2 < reps) == low)
        def _(near=near):
            if i < count:
                act(near, i)
            if i >= 1:
                act(1 - near, i - 1)


class SumJob:
    climbs = True

    def __init__(self, sources, blocks, cuts, reps, steps):
        self.blocks, self.cuts, self.reps, self.steps = blocks, cuts, reps, steps
        self.arrays = sources
        self.corner = blocks > 1
        rows = sources[0].shape[0]
        self.span = rows // blocks
        self.half = self.span // 2
        self.size = self.half // cuts
        self.widths = [source.shape[1] for source in sources]
        wide = sum(self.widths)
        self.shape = (2, blocks, self.half, wide)
        self.outs = []
        self.count = blocks * cuts
        sems = pltpu.SemaphoreType.DMA((2, self.count))
        self.scratch = [
            pltpu.VMEM(self.shape, BF16),
            pltpu.VMEM(self.shape, BF16),
            pltpu.VMEM(self.shape, BF16),
            pltpu.SemaphoreType.DMA((2, blocks, len(sources))),
        ] + [sems] * 5

    def open(self, arrays, outs, scratch, place):
        self.sources = arrays
        self.held, self.landed, self.fin, self.load_sems = scratch[:4]
        self.chain_sems, self.give_sems, self.keep_sems = scratch[4:6], scratch[6:8], scratch[8]
        self.rep, self.core, self.own = place[:3]
        self.ways = column_place(place, self.reps)
        for k in range(self.blocks):
            for way in range(2):
                for load in self.loads(way, k):
                    load.start()

    def block(self, k):
        return (self.own + k) % self.blocks

    def loads(self, way, k):
        copies = []
        at = 0
        for n, (source, width) in enumerate(zip(self.sources, self.widths)):
            start = pl.multiple_of(self.block(k) * self.span + way * self.half, 16)
            src = source.at[pl.ds(start, self.half)]
            dst = self.held.at[way, k, :, pl.ds(at, width)]
            copies.append(pltpu.make_async_copy(src, dst, self.load_sems.at[way, k, n]))
            at += width
        return copies

    def rows(self, i):
        return i // self.cuts, pl.ds(i % self.cuts * self.size, self.size)

    def chain(self, way, i):
        k, rows = self.rows(i)
        return pltpu.make_async_remote_copy(
            src_ref=self.held.at[way, k, rows],
            dst_ref=self.landed.at[way, k, rows],
            send_sem=self.chain_sems[0].at[way, i],
            recv_sem=self.chain_sems[1].at[way, i],
            device_id=self.ways[way][2],
            device_id_type=MESH,
        )

    def give(self, way, i):
        k, rows = self.rows(i)
        return pltpu.make_async_remote_copy(
            src_ref=self.held.at[way, k, rows],
            dst_ref=self.fin.at[way, self.own, rows],
            send_sem=self.give_sems[0].at[way, i],
            recv_sem=self.give_sems[1].at[way, i],
            device_id=(self.rep, self.core, self.block(k)),
            device_id_type=MESH,
        )

    def keep(self, way, i):
        k, rows = self.rows(i)
        own = self.own if self.blocks > 1 else 0
        src, dst = self.held.at[way, k, rows], self.fin.at[way, own, rows]
        return pltpu.make_async_copy(src, dst, self.keep_sems.at[way, i])

    def loaded(self, way, i):
        if i % self.cuts == 0:
            for load in self.loads(way, i // self.cuts):
                load.wait()

    def prime(self):
        for way in range(2):

            @pl.when(self.ways[way][0])
            def _(way=way):
                for i in range(self.count):
                    self.loaded(way, i)
                    self.chain(way, i).start()

    def add(self, way, i):
        first, last = self.ways[way][:2]
        k, rows = self.rows(i)

        @pl.when(jnp.logical_not(first))
        def _():
            self.loaded(way, i)
            self.chain(way, i).wait_recv()
            self.held[way, k, rows] = self.held[way, k, rows] + self.landed[way, k, rows]

            @pl.when(jnp.logical_not(last))
            def _():
                self.chain(way, i).start()

            @pl.when(last)
            def _():
                if k == 0:
                    self.keep(way, i).start()
                else:
                    self.give(way, i).start()

    def step(self, i):
        skewed(self.rep, self.reps, self.count, self.add, i)

    def stage(self, n):
        if n == 1:
            self.prime()
        if n in self.steps:
            for i in self.steps[n]:
                self.step(i)
        if n == 7:
            for way in range(2):
                last = self.ways[way][1]
                for i in range(self.count):

                    @pl.when(jnp.logical_not(last))
                    def _(way=way, i=i):
                        self.chain(way, i).wait_send()

                    @pl.when(last)
                    def _(way=way, i=i):
                        if i // self.cuts == 0:
                            self.keep(way, i).wait()
                        else:
                            self.give(way, i).wait()


class HandJob:
    climbs = True

    def __init__(self, sums, reps, cuts):
        self.sums, self.arrays = sums, []
        shape = sums.shape
        self.reps, self.cuts, self.size = reps, cuts, shape[2] // cuts
        self.count = shape[1] * cuts
        self.corner = False
        self.outs = [jax.ShapeDtypeStruct((2, 2) + shape[1:], BF16)]
        self.scratch = [pltpu.SemaphoreType.DMA((2, self.count))] * 5

    def open(self, arrays, outs, scratch, place):
        self.out = outs[0]
        self.hand_sems, self.side_sems, self.keep_sems = scratch[:2], scratch[2:4], scratch[4]
        self.rep, self.core, self.own = place[:3]
        self.ways = column_place(place, self.reps)

    def rows(self, j):
        return j // self.cuts, pl.ds(j % self.cuts * self.size, self.size)

    def place(self, way, j):
        block, rows = self.rows(j)
        return self.out.at[way, self.core, block, rows]

    def remote(self, src, way, j, sems, device):
        return pltpu.make_async_remote_copy(
            src_ref=src,
            dst_ref=self.place(way, j),
            send_sem=sems[0].at[way, j],
            recv_sem=sems[1].at[way, j],
            device_id=device,
            device_id_type=MESH,
        )

    def beside(self):
        return (self.rep, 1 - self.core, self.own)

    def begin(self):
        fin = self.sums.fin
        for j in range(self.count):
            for way in range(2):

                @pl.when(self.ways[way][1])
                def _(way=way, j=j):
                    block, rows = self.rows(j)
                    src = fin.at[way, block, rows]
                    self.remote(src, way, j, self.hand_sems, self.ways[way][3]).start()
                    self.remote(src, way, j, self.side_sems, self.beside()).start()
                    dst = self.place(way, j)
                    pltpu.make_async_copy(src, dst, self.keep_sems.at[way, j]).start()

    def hand(self, way, j):
        first, last = self.ways[way][:2]

        @pl.when(jnp.logical_not(last))
        def _():
            ref = self.place(way, j)
            hand = self.remote(ref, way, j, self.hand_sems, self.ways[way][3])
            hand.wait_recv()

            @pl.when(jnp.logical_not(first))
            def _():
                hand.start()

            self.remote(ref, way, j, self.side_sems, self.beside()).start()

    def pass_on(self):
        for j in range(self.count + 1):
            skewed(self.rep, self.reps, self.count, lambda w, i: self.hand(1 - w, i), j)

    def close(self):
        for j in range(self.count):
            for way in range(2):
                first, last = self.ways[way][:2]
                ref = self.place(way, j)
                self.remote(ref, way, j, self.side_sems, self.beside()).wait()

                @pl.when(jnp.logical_not(first))
                def _(way=way, j=j, ref=ref):
                    self.remote(ref, way, j, self.hand_sems, self.ways[way][3]).wait_send()

                @pl.when(last)
                def _(way=way, j=j, ref=ref):
                    pltpu.make_async_copy(ref, ref, self.keep_sems.at[way, j]).wait()

    def stage(self, n):
        if n == 7:
            self.begin()
        if n == 8:
            self.pass_on()
        if n == 9:
            self.close()


class Jobs:
    def __init__(self, jobs, reps):
        self.jobs, self.reps = jobs, reps
        self.arrays = [a for job in jobs for a in job.arrays]
        self.out_shapes = [o for job in jobs for o in job.outs]
        self.scratch = [x for job in jobs for x in job.scratch]

    def greet(self, place):
        rep, core, own, across, down, corner = place
        devices = [(rep, core, across), (rep, core, down), (rep, 1 - core, own)]
        if any(job.climbs for job in self.jobs):
            devices += [((rep + 1) % self.reps, core, own)]
            devices += [((rep + self.reps - 1) % self.reps, core, own)]
        if any(job.corner for job in self.jobs):
            devices.append((rep, core, corner))
        meet(devices)

    def open(self, arrays, outs, scratch, place):
        arrays, outs, scratch = list(arrays), list(outs), list(scratch)

        def take(refs, count):
            taken = refs[:count]
            del refs[:count]
            return taken

        for job in self.jobs:
            mine = [take(arrays, len(job.arrays)), take(outs, len(job.outs))]
            job.open(*mine, take(scratch, len(job.scratch)), place)

    def stage(self, n):
        for job in self.jobs:
            job.stage(n)


def gather_kernel(count, jobs, *refs):
    arrays, outs = len(jobs.arrays), len(jobs.out_shapes)
    xs, job_arrays = refs[:count], refs[count : count + arrays]
    refs = refs[count + arrays :]
    x_outs, job_outs = refs[:count], refs[count : count + outs]
    refs = refs[count + outs :]
    local_sems, send_sems, recv_sems = refs[:3]
    place = plane_position()
    jobs.greet(place)
    sender = Sender(send_sems, recv_sems)
    moves = [
        Gather(sender, x, out, local_sems.at[i], place)
        for i, (x, out) in enumerate(zip(xs, x_outs))
    ]
    for move in moves:
        move.begin()
    jobs.open(job_arrays, job_outs, refs[3:], place)
    jobs.stage(0)
    jobs.stage(1)
    for move in moves:
        move.relay()
    jobs.stage(5)
    for move in moves:
        move.finish()
    sender.finish()
    for n in (6, 7, 8, 9):
        jobs.stage(n)


def gather_plane(blocks, collective_id, jobs=(), reps=1):
    count = len(blocks)
    jobs = Jobs(jobs, reps)
    return pl.pallas_call(
        functools.partial(gather_kernel, count, jobs),
        out_shape=[jax.ShapeDtypeStruct((8,) + x.shape, x.dtype) for x in blocks]
        + jobs.out_shapes,
        in_specs=[VM] * count + [HBM] * len(jobs.arrays),
        out_specs=[HBM] * (count + len(jobs.out_shapes)),
        scratch_shapes=[
            pltpu.SemaphoreType.DMA((count,)),
            pltpu.SemaphoreType.DMA((13 * count,)),
            pltpu.SemaphoreType.DMA((13 * count,)),
        ]
        + jobs.scratch,
        compiler_params=params(collective_id, 60),
        cost_estimate=link_cost(40 * count),
    )(*blocks, *jobs.arrays)


def quarter_kernel(gate_ref, up_ref, out_ref, room, local_sems, send_sems, recv_sems):
    rep, core, own, across, down, corner = plane_position()
    peers = (corner, across, down)
    meet([(rep, core, peer) for peer in peers])
    rows = out_ref.shape[1]
    width = out_ref.shape[2] // 2
    mine = pl.ds(pl.multiple_of(rep * rows, rows), rows)

    def source(ref, block):
        columns = pl.ds(pl.multiple_of((block * 2 + core) * width, width), width)
        return ref.at[mine, columns]

    sender = Sender(send_sems, recv_sems)
    for peer in peers:
        for k, ref in enumerate((gate_ref, up_ref)):
            target = out_ref.at[own, :, pl.ds(k * width, width)]
            sender.send(source(ref, peer), target, (rep, core, peer))
    local = []
    for k, ref in enumerate((gate_ref, up_ref)):
        target = out_ref.at[own, :, pl.ds(k * width, width)]
        copy = Bounce(source(ref, own), target, room.at[k], local_sems.at[k])
        copy.start()
        local.append(copy)
    for copy in local:
        copy.turn()
    for copy in sender.copies:
        copy.wait_recv()
    sender.finish()
    for copy in local:
        copy.wait()


def quarter_columns(w_gate, w_up, reps, collective_id):
    rows, columns = w_gate.shape
    return pl.pallas_call(
        quarter_kernel,
        out_shape=jax.ShapeDtypeStruct((4, rows // reps, columns // 4), BF16),
        in_specs=[HBM, HBM],
        out_specs=HBM,
        scratch_shapes=[
            pltpu.VMEM((2, rows // reps, columns // 8), BF16),
            pltpu.SemaphoreType.DMA((2, 2)),
            pltpu.SemaphoreType.DMA((6,)),
            pltpu.SemaphoreType.DMA((6,)),
        ],
        compiler_params=params(collective_id, 60),
        cost_estimate=link_cost(25),
    )(w_gate, w_up)


def start_kernel(
    x_ref, code_ref, gain_ref, q_ref, k_ref, v_ref,
    x_out, code_out, gain_out, q_out, k_out, v_out,
    q_room, k_room, v_room, bounce_sems, local_sems, send_sems, recv_sems,
):
    place = plane_position()
    rep, core, own, across, down, corner = place
    peers = (corner, across, down)
    meet([(rep, core, peer) for peer in peers] + [(rep, 1 - core, peer) for peer in peers]
         + [(rep, 1 - core, own)])
    sender = Sender(send_sems, recv_sems)
    direct, local, bounced = [], [], []

    def keep(src, dst):
        copy = pltpu.make_async_copy(src, dst, local_sems.at[1 + len(local)])
        copy.start()
        local.append(copy)

    def bounce(src, dst, room):
        copy = Bounce(src, dst, room, bounce_sems.at[len(bounced)])
        copy.start()
        bounced.append(copy)

    def columns(ref, block, width):
        return ref.at[:, pl.ds(pl.multiple_of(block * width, width), width)]

    def weights():
        for peer in peers:
            there = (rep, core, peer)
            direct.append(sender.send(gain_ref, gain_out.at[own], there))
            direct.append(sender.send(columns(q_ref, peer * 2 + core, 256), q_out.at[own], there))
            direct.append(sender.send(columns(k_ref, peer, 128), k_out.at[own], there))
            direct.append(sender.send(columns(v_ref, peer, 128), v_out.at[own], there))
            direct.append(sender.send(code_ref, code_out.at[core * 4 + own], there))
            other = (rep, 1 - core, peer)
            direct.append(sender.send(code_ref, code_out.at[core * 4 + own], other))
        direct.append(sender.send(code_ref, code_out.at[core * 4 + own], (rep, 1 - core, own)))
        keep(gain_ref, gain_out.at[own])
        bounce(columns(q_ref, own * 2 + core, 256), q_out.at[own], q_room)
        bounce(columns(k_ref, own, 128), k_out.at[own], k_room)
        bounce(columns(v_ref, own, 128), v_out.at[own], v_room)
        keep(code_ref, code_out.at[core * 4 + own])

    move = Gather(sender, x_ref, x_out, local_sems.at[0], place)
    move.begin()
    weights()
    for copy in bounced:
        copy.turn()
    move.relay()
    move.finish()
    for copy in direct:
        copy.wait_recv()
    sender.finish()
    for copy in local + bounced:
        copy.wait()


def start_plane(hidden, codes, gains, w_query, w_key, w_value, collective_id):
    rows = w_query.shape[0]
    shapes = [
        ((8,) + hidden.shape, BF16),
        ((8,) + codes.shape, jnp.int32),
        ((4,) + gains.shape, BF16),
        ((4, rows, GROUPS * HD), BF16),
        ((4, rows, 2 * HD), BF16),
        ((4, rows, 2 * HD), BF16),
    ]
    return pl.pallas_call(
        start_kernel,
        out_shape=[jax.ShapeDtypeStruct(s, d) for s, d in shapes],
        in_specs=[VM] + [HBM] * 5,
        out_specs=[HBM] * 6,
        scratch_shapes=[
            pltpu.VMEM((rows, GROUPS * HD), BF16),
            pltpu.VMEM((rows, 2 * HD), BF16),
            pltpu.VMEM((rows, 2 * HD), BF16),
            pltpu.SemaphoreType.DMA((3, 2)),
            pltpu.SemaphoreType.DMA((3,)),
            pltpu.SemaphoreType.DMA((32,)),
            pltpu.SemaphoreType.DMA((32,)),
        ],
        compiler_params=params(collective_id, 60),
        cost_estimate=link_cost(60),
    )(hidden, codes, gains, w_query, w_key, w_value)


def product_scatter_kernel(turned, count, jobs, *refs):
    arrays, outs = len(jobs.arrays), len(jobs.out_shapes)
    x_hbm, w_hbm, job_arrays = refs[:count], refs[count], refs[count + 1 : count + 1 + arrays]
    refs = refs[count + 1 + arrays :]
    out_ref, job_outs = refs[0], refs[1 : 1 + outs]
    refs = refs[1 + outs :]
    x_refs, w_ref = refs[:count], refs[count]
    (
        swap, held, from_core, from_across, from_down, last_across, last_down,
        x_sems, w_sems, core_send, core_recv, send_sems, recv_sems,
    ) = refs[count + 1 : count + 14]
    place = plane_position()
    rep, core, own, across, down, corner = place
    to_across, to_down, to_core = (rep, core, across), (rep, core, down), (rep, 1 - core, own)
    _, rows, wide = held.shape
    depth = x_refs[0].shape[1]
    tile = 512
    tiles = wide // tile
    half = rows // 2
    low, high = pl.ds(0, half), pl.ds(half, half)
    order = []
    for block in (corner, across, down, own):
        order += [(1 - core) * 4 + block, core * 4 + block]

    def rows_of(block):
        return pl.ds(pl.multiple_of(block * rows, rows), rows)

    x_loads = [
        [
            pltpu.make_async_copy(
                x_hbm[i].at[rows_of(block)], x_refs[i].at[rows_of(block)], x_sems.at[i, n]
            )
            for i in range(count)
        ]
        for n, block in enumerate(order)
    ]
    w_loads = []
    for t in range(tiles):
        columns = pl.ds(t * tile, tile)
        if turned:
            src, dst = w_hbm.at[columns], w_ref.at[columns]
        else:
            kept = pl.ds(pl.multiple_of(core * depth, depth), depth)
            src, dst = w_hbm.at[kept, columns], w_ref.at[:, columns]
        w_loads.append(pltpu.make_async_copy(src, dst, w_sems.at[t]))
    for load in x_loads[0]:
        load.start()
    for load in w_loads:
        load.start()
    for loads in x_loads[1:]:
        for load in loads:
            load.start()
    jobs.open(job_arrays, job_outs, refs[count + 14 :], place)
    jobs.greet(place)
    jobs.stage(0)

    def product(dst, mine, columns):
        total = None
        for i in range(count):
            x = x_refs[i][mine, :]
            if turned:
                w = w_ref[columns, pl.ds(i * depth, depth)]
                part = lax.dot_general(
                    x, w, (((1,), (1,)), ((), ())), preferred_element_type=F32
                )
            else:
                part = dot_f32(x, w_ref[:, columns])
            total = part if total is None else total + part
        dst[:, columns] = total.astype(BF16)

    def fill(dst, n):
        for load in x_loads[n]:
            load.wait()
        mine = rows_of(order[n])
        if n == 0:
            for t in range(tiles):
                w_loads[t].wait()
                product(dst, mine, pl.ds(t * tile, tile))
        else:

            @pl.loop(0, tiles)
            def _(t):
                product(dst, mine, pl.ds(pl.multiple_of(t * tile, tile), tile))

    swaps = Sender(core_send, core_recv)
    sender = Sender(send_sems, recv_sems)
    sent = {}
    for k in range(4):
        fill(swap.at[k], 2 * k)
        swaps.send(swap.at[k], from_core.at[k], to_core)
        fill(held.at[k], 2 * k + 1)
        swaps.copies[k].wait_recv()
        held[k] = held[k] + from_core[k]
        if k == 0:
            sent[0] = sender.send(held.at[0, low], from_across.at[0], to_across)
            sent[1] = sender.send(held.at[0, high], from_down.at[0], to_down)
        if k == 1:
            sent[2] = sender.send(held.at[1, low], from_across.at[1], to_across)
        if k == 2:
            sent[3] = sender.send(held.at[2, high], from_down.at[1], to_down)
        jobs.stage(1 + k)
    sent[0].wait_recv()
    held[2, low] = held[2, low] + from_across[0]
    to_last = sender.send(held.at[2, low], last_down, to_down)
    sent[1].wait_recv()
    held[1, high] = held[1, high] + from_down[0]
    across_last = sender.send(held.at[1, high], last_across, to_across)
    jobs.stage(5)
    sent[2].wait_recv()
    sent[3].wait_recv()
    to_last.wait_recv()
    out_ref[low] = (
        held[3, low].astype(F32) + from_across[1].astype(F32) + last_down[...].astype(F32)
    )
    across_last.wait_recv()
    out_ref[high] = (
        held[3, high].astype(F32) + from_down[1].astype(F32) + last_across[...].astype(F32)
    )
    swaps.finish()
    sender.finish()
    for n in (6, 7, 8, 9):
        jobs.stage(n)


def product_scatter(xs, w, turned, collective_id, jobs=(), reps=1):
    count = len(xs)
    jobs = Jobs(jobs, reps)
    tokens, depth = xs[0].shape
    rows = tokens // 8
    wide = w.shape[0] if turned else w.shape[1]
    half = rows // 2
    return pl.pallas_call(
        functools.partial(product_scatter_kernel, turned, count, jobs),
        out_shape=[jax.ShapeDtypeStruct((rows, wide), F32)] + jobs.out_shapes,
        in_specs=[HBM] * (count + 1 + len(jobs.arrays)),
        out_specs=[VM] + [HBM] * len(jobs.out_shapes),
        scratch_shapes=[pltpu.VMEM((tokens, depth), BF16)] * count
        + [
            pltpu.VMEM((wide, depth * count) if turned else (depth, wide), BF16),
            pltpu.VMEM((4, rows, wide), BF16),
            pltpu.VMEM((4, rows, wide), BF16),
            pltpu.VMEM((4, rows, wide), BF16),
            pltpu.VMEM((2, half, wide), BF16),
            pltpu.VMEM((2, half, wide), BF16),
            pltpu.VMEM((half, wide), BF16),
            pltpu.VMEM((half, wide), BF16),
            pltpu.SemaphoreType.DMA((count, 8)),
            pltpu.SemaphoreType.DMA((wide // 512,)),
            pltpu.SemaphoreType.DMA((4,)),
            pltpu.SemaphoreType.DMA((4,)),
            pltpu.SemaphoreType.DMA((6,)),
            pltpu.SemaphoreType.DMA((6,)),
        ]
        + jobs.scratch,
        compiler_params=params(collective_id, 60),
        cost_estimate=link_cost(44, 2 * tokens * depth * count * wide),
    )(*xs, w, *jobs.arrays)


def turn(value, cos_ref, sin_ref, back):
    wide = value.shape[1]
    lanes = lax.broadcasted_iota(jnp.int32, value.shape, 1)
    front = lax.rem(lanes, HD) < HD // 2
    ahead = pltpu.roll(value, wide - HD // 2, 1)
    behind = pltpu.roll(value, HD // 2, 1)
    swapped = jnp.where(front, -ahead, behind) * sin_ref[...]
    turned = value * cos_ref[...]
    return turned - swapped if back else turned + swapped


def allowed_pairs(row_ref, col_ref):
    keys, queries = row_ref[0], col_ref[0]
    length = keys.shape[1]
    row_index = lax.broadcasted_iota(jnp.int32, (length, length), 0)
    col_index = lax.broadcasted_iota(jnp.int32, (length, length), 1)
    same = lax.shift_right_logical(keys, 1) == lax.shift_right_logical(queries, 1)
    valid = jnp.bitwise_and(keys, 1) == 1
    return same & (col_index <= row_index) & (valid | (col_index == row_index))


def head_probs(query, keys, allowed):
    scores = lax.dot_general(
        query, keys, (((1,), (1,)), ((), ())), preferred_element_type=F32
    )
    scores = jnp.where(allowed, scores * SCORE_SCALE, MASKED_SCORE)
    shifted = jnp.exp(scores - jnp.max(scores, axis=-1, keepdims=True))
    return shifted / jnp.sum(shifted, axis=-1, keepdims=True)


def attend_kernel(
    x_ref, gain_ref, w_ref, cos_ref, sin_ref, row_ref, col_ref, cot_ref,
    normed_ref, heads_ref, attended_ref, cot_out,
    local_sem, send_sems, recv_sems,
):
    at = pl.program_id(0)
    place = plane_position()
    rep, core, own, across, down, _ = place
    sender = Sender(send_sems, recv_sems)
    move = Gather(sender, cot_ref, cot_out, local_sem, place)

    @pl.when(at == 0)
    def _():
        meet([(rep, core, across), (rep, core, down), (rep, 1 - core, own)])
        move.begin()

    @pl.when(at == 5)
    def _():
        move.relay()

    @pl.when(at == 7)
    def _():
        move.finish()
        sender.finish()

    @pl.loop(0, x_ref.shape[1] // 32)
    def _(t):
        rows = pl.ds(pl.multiple_of(t * 32, 32), 32)
        x = x_ref[0, rows].astype(F32)
        normed_ref[0, rows] = (x * row_scale(x) * gain_ref[...]).astype(BF16)

    projected = dot_f32(normed_ref[0], w_ref[...])
    heads = turn(projected, cos_ref, sin_ref, False).astype(BF16)
    heads_ref[0] = heads
    allowed = allowed_pairs(row_ref, col_ref)
    keys = heads[:, GROUPS * HD : (GROUPS + 1) * HD]
    values = heads[:, (GROUPS + 1) * HD :]
    parts = []
    for h in range(GROUPS):
        probs = head_probs(heads[:, h * HD : (h + 1) * HD], keys, allowed)
        parts.append(dot_f32(probs.astype(BF16), values))
    attended_ref[0] = jnp.concatenate(parts, axis=1).astype(BF16)


def attend(hidden, gain, qkv, tables, codes, cotangent, collective_id):
    members, length, width = hidden.shape
    wide = qkv.shape[1]
    q_wide = GROUPS * HD

    def one(columns):
        return pl.BlockSpec((1, length, columns), lambda i: (i, 0, 0))

    def fixed(*shape):
        return pl.BlockSpec(shape, lambda i: (0,) * len(shape))

    return pl.pallas_call(
        attend_kernel,
        grid=(members,),
        out_shape=[
            jax.ShapeDtypeStruct((members, length, width), BF16),
            jax.ShapeDtypeStruct((members, length, wide), BF16),
            jax.ShapeDtypeStruct((members, length, q_wide), BF16),
            jax.ShapeDtypeStruct((8,) + cotangent.shape, BF16),
        ],
        in_specs=[
            one(width), fixed(1, width), fixed(width, wide), fixed(length, wide),
            fixed(length, wide), pl.BlockSpec((1, 1, length), lambda i: (i, 0, 0)), one(1), VM,
        ],
        out_specs=[one(width), one(wide), one(q_wide), HBM],
        scratch_shapes=[
            pltpu.SemaphoreType.DMA,
            pltpu.SemaphoreType.DMA((13,)),
            pltpu.SemaphoreType.DMA((13,)),
        ],
        compiler_params=params(collective_id, 60),
        cost_estimate=link_cost(40),
    )(hidden, gain, qkv, *tables, codes[:, None, :], codes[:, :, None], cotangent)


def attend_back_kernel(
    out_grad_ref, w_ref, heads_ref, attended_ref, cos_ref, sin_ref, row_ref, col_ref,
    grad_ref, w_grad_ref, total,
):
    at = pl.program_id(0)
    out_grad = out_grad_ref[0]
    heads = heads_ref[0]
    attended_grad = lax.dot_general(
        out_grad, w_ref[...], (((1,), (1,)), ((), ())), preferred_element_type=F32
    ).astype(BF16)
    term = lax.dot_general(
        attended_ref[0], out_grad, (((0,), (0,)), ((), ())), preferred_element_type=F32
    )

    @pl.when(at == 0)
    def _():
        total[...] = term

    @pl.when(at > 0)
    def _():
        total[...] = total[...] + term

    @pl.when(at == pl.num_programs(0) - 1)
    def _():
        w_grad_ref[...] = total[...].astype(BF16)

    allowed = allowed_pairs(row_ref, col_ref)
    keys = heads[:, GROUPS * HD : (GROUPS + 1) * HD]
    values = heads[:, (GROUPS + 1) * HD :]
    grads = []
    key_grad, value_grad = None, None
    for h in range(GROUPS):
        lanes = slice(h * HD, (h + 1) * HD)
        query, head_grad = heads[:, lanes], attended_grad[:, lanes]
        probs = head_probs(query, keys, allowed)
        prob_grad = lax.dot_general(
            head_grad, values, (((1,), (1,)), ((), ())), preferred_element_type=F32
        )
        row_dot = jnp.sum(probs * prob_grad, axis=-1, keepdims=True)
        score_grad = (probs * (prob_grad - row_dot)).astype(BF16)
        grads.append(dot_f32(score_grad, keys) * SCORE_SCALE)
        key_part = lax.dot_general(
            score_grad, query, (((0,), (0,)), ((), ())), preferred_element_type=F32
        )
        value_part = lax.dot_general(
            probs.astype(BF16), head_grad, (((0,), (0,)), ((), ())), preferred_element_type=F32
        )
        key_grad = key_part if key_grad is None else key_grad + key_part
        value_grad = value_part if value_grad is None else value_grad + value_part
    grads += [key_grad * SCORE_SCALE, value_grad]
    grad_ref[0] = turn(jnp.concatenate(grads, axis=1), cos_ref, sin_ref, True).astype(BF16)


def attend_back(out_grad, out_rows, heads, attended, tables, codes):
    members, length, width = out_grad.shape
    wide, q_wide = heads.shape[2], attended.shape[2]

    def one(columns):
        return pl.BlockSpec((1, length, columns), lambda i: (i, 0, 0))

    def fixed(*shape):
        return pl.BlockSpec(shape, lambda i: (0,) * len(shape))

    return pl.pallas_call(
        attend_back_kernel,
        grid=(members,),
        out_shape=[
            jax.ShapeDtypeStruct((members, length, wide), BF16),
            jax.ShapeDtypeStruct((q_wide, width), BF16),
        ],
        in_specs=[
            one(width), fixed(q_wide, width), one(wide), one(q_wide), fixed(length, wide),
            fixed(length, wide), pl.BlockSpec((1, 1, length), lambda i: (i, 0, 0)), one(1),
        ],
        out_specs=[one(wide), fixed(q_wide, width)],
        scratch_shapes=[pltpu.VMEM((q_wide, width), F32)],
        compiler_params=pltpu.CompilerParams(vmem_limit_bytes=48 << 20),
        cost_estimate=link_cost(25),
    )(out_grad, out_rows, heads, attended, *tables, codes[:, None, :], codes[:, :, None])


def cast_rows_kernel(x_ref, out_ref):
    out_ref[...] = x_ref[0, 0].astype(F32)


def cast_rows(spread):
    reps, subs, rows, columns = spread.shape
    return pl.pallas_call(
        cast_rows_kernel,
        grid=(subs, reps),
        out_shape=jax.ShapeDtypeStruct((reps * subs * rows, columns), F32),
        in_specs=[pl.BlockSpec((1, 1, rows, columns), lambda s, r: (r, s, 0, 0))],
        out_specs=pl.BlockSpec((rows, columns), lambda s, r: (s * reps + r, 0)),
        cost_estimate=link_cost(8),
    )(spread)


def cast_columns_kernel(x_ref, out_ref):
    _, subs, owners, _, columns = x_ref.shape
    for j in range(owners):
        for s in range(subs):
            at = (j * subs + s) * columns
            out_ref[:, at : at + columns] = x_ref[0, s, j].astype(F32)


def cast_columns(handed, columns):
    parts, subs, owners, rows, _ = handed.shape
    wide = owners * subs * columns
    cuts = 4
    block = (1, subs, owners, rows // cuts, columns)
    return pl.pallas_call(
        cast_columns_kernel,
        grid=(parts, cuts),
        out_shape=jax.ShapeDtypeStruct((parts * rows, wide), F32),
        in_specs=[pl.BlockSpec(block, lambda r, h: (r, 0, 0, h, 0))],
        out_specs=pl.BlockSpec((rows // cuts, wide), lambda r, h: (r * cuts + h, 0)),
        cost_estimate=link_cost(8),
    )(handed)


def cast_heads_kernel(q_ref, kv_ref, q_out, k_out, v_out):
    _, subs, owners, _, columns = q_ref.shape
    for j in range(owners):
        for s in range(subs):
            at = (j * subs + s) * columns
            q_out[:, at : at + columns] = q_ref[0, s, j].astype(F32)
        pair = [kv_ref[0, s, j].astype(F32) for s in range(subs)]
        wide = HD * subs
        at = j * wide
        k_out[:, at : at + wide] = jnp.concatenate([p[:, :HD] for p in pair], axis=1)
        v_out[:, at : at + wide] = jnp.concatenate([p[:, HD:] for p in pair], axis=1)


def cast_heads(handed, skip):
    parts, subs, owners, rows, _ = handed.shape
    q_wide, k_wide = GROUPS * HD, 2 * HD
    members = owners * subs

    def source(wide, at):
        return pl.BlockSpec((1, subs, owners, rows, wide), lambda r: (r, 0, 0, 0, at // wide))

    def shape(wide):
        return jax.ShapeDtypeStruct((parts * rows, wide), F32)

    widths = (members * q_wide, members * HD, members * HD)
    return pl.pallas_call(
        cast_heads_kernel,
        grid=(parts,),
        out_shape=[shape(w) for w in widths],
        in_specs=[source(q_wide, skip), source(k_wide, skip + q_wide)],
        out_specs=[pl.BlockSpec((rows, w), lambda r: (r, 0)) for w in widths],
        compiler_params=pltpu.CompilerParams(vmem_limit_bytes=48 << 20),
        cost_estimate=link_cost(5),
    )(handed, handed)


def tally_kernel(x_ref, out_ref, plane, planes, total, sems, plane_sems):
    rep, core, own, _, _, _ = plane_position()
    reps = planes.shape[0]
    mates = [(c, j) for c in range(2) for j in range(4)][1:]
    others = [(rep, (core + c) % 2, (own + j) % 4) for c, j in mates]
    above = [((rep + r) % reps, core, own) for r in range(1, reps)]
    meet(others + above)
    sender = Sender(sems.at[0], sems.at[1])
    for device in others:
        sender.send(x_ref, plane.at[core * 4 + own], device)
    plane[core * 4 + own] = x_ref[...]
    for copy in sender.copies:
        copy.wait_recv()
    mine = plane[0]
    for k in range(1, 8):
        mine = mine + plane[k]
    total[...] = mine
    climber = Sender(plane_sems.at[0], plane_sems.at[1])
    for device in above:
        climber.send(total, planes.at[rep], device)
    planes[rep] = mine
    for copy in climber.copies:
        copy.wait_recv()
    whole = planes[0]
    for k in range(1, reps):
        whole = whole + planes[k]
    out_ref[...] = whole
    sender.finish()
    climber.finish()


def tally_all(values, reps, collective_id):
    size = values.shape[0]
    rows = -(-size // 1024) * 8
    padded = jnp.pad(values, (0, rows * 128 - size)).reshape(rows, 128)
    block = pltpu.VMEM((rows, 128), F32)
    summed = pl.pallas_call(
        tally_kernel,
        out_shape=jax.ShapeDtypeStruct((rows, 128), F32),
        in_specs=[VM],
        out_specs=VM,
        scratch_shapes=[
            pltpu.VMEM((8, rows, 128), F32),
            pltpu.VMEM((reps, rows, 128), F32),
            block,
            pltpu.SemaphoreType.DMA((2, 7)),
            pltpu.SemaphoreType.DMA((2, reps - 1)),
        ],
        compiler_params=params(collective_id),
        cost_estimate=link_cost(10),
    )(padded)
    return summed.reshape(-1)[:size]


def column_blocks(weight, owners, subs):
    rows, columns = weight.shape
    blocked = weight.reshape(rows, owners, subs, columns // (owners * subs))
    mine = lax.dynamic_index_in_dim(blocked, lax.axis_index("sub"), axis=2, keepdims=False)
    return jnp.swapaxes(mine, 0, 1)


def regroup_columns(weights, owners, subs):
    blocks = jnp.concatenate([column_blocks(w, owners, subs) for w in weights], axis=-1)
    moved = lax.all_to_all(blocks, "fsdp", split_axis=0, concat_axis=0, tiled=True)
    return moved.reshape(-1, moved.shape[-1])


def row_block(weight, subs):
    rows = weight.shape[0] // subs
    return lax.dynamic_slice_in_dim(weight, lax.axis_index("sub") * rows, rows, axis=0)


def gather_tokens(block):
    return lax.all_gather(block, ("sub", "fsdp"), axis=0, tiled=True)


def scatter_tokens(partial):
    return lax.psum_scatter(partial, ("sub", "fsdp"), scatter_dimension=0, tiled=True)


def sum_planes(term):
    return lax.psum_scatter(term, "rep", scatter_dimension=0, tiled=True)


def spread_planes(piece):
    rep, subs = lax.axis_size("rep"), lax.axis_size("sub")
    spread = lax.all_gather(piece, ("rep", "sub"), axis=0, tiled=False)
    return spread.reshape((rep, subs) + piece.shape)


def owner_major(term):
    owners, rep = lax.axis_size("fsdp"), lax.axis_size("rep")
    rows, columns = term.shape
    blocked = jnp.swapaxes(term.reshape(owners, rep, rows // (owners * rep), columns), 0, 1)
    return blocked.reshape(rows, columns)


def to_owners(piece):
    blocked = piece.reshape(lax.axis_size("fsdp"), -1, piece.shape[1])
    return lax.all_to_all(blocked, "fsdp", split_axis=0, concat_axis=0, tiled=True)


def place_columns(spread):
    reps, subs, owners, rows, columns = spread.shape
    part = jnp.transpose(spread, (0, 3, 2, 1, 4))
    return part.reshape(reps * rows, owners * subs * columns).astype(F32)


def shards(
    kernels,
    hidden_in,
    segment_ids,
    valid_mask,
    cotangent,
    norm_attn,
    w_query,
    w_key,
    w_value,
    w_output,
    norm_mlp,
    w_gate,
    w_up,
    w_down,
):
    owners, subs, reps = lax.axis_size("fsdp"), lax.axis_size("sub"), lax.axis_size("rep")
    members = owners * subs
    length, width = hidden_in.shape[1:]
    tokens = members * length
    q_width, k_width = GROUPS * HD, HD

    def gathered(blocks, collective_id, jobs=()):
        if kernels:
            outs = list(gather_plane(blocks, collective_id, jobs, reps))
        else:
            outs = [gather_tokens(block) for block in blocks]
        return [o.reshape(tokens, -1) for o in outs[: len(blocks)]] + outs[len(blocks) :]

    def scattered(xs, w, turned, collective_id, jobs=()):
        if kernels:
            return product_scatter(xs, w, turned, collective_id, jobs, reps)
        x = jnp.concatenate(xs, axis=1)
        product = contract_cols(x, w) if turned else dot_f32(x, row_block(w, subs))
        return [scatter_tokens(product.astype(BF16)).astype(F32)]

    codes = segment_ids * 2 + valid_mask
    gains = jnp.stack([norm_attn, norm_mlp])
    result_grad = cotangent[0].astype(F32)
    mlp_out_low = (RESIDUAL_SCALE * result_grad).astype(BF16)
    if kernels:
        quarter = quarter_columns(w_gate, w_up, reps, 0)
        hidden_tied = after(hidden_in[0], quarter)
        hidden_low, codes, gains, q_cols, k_cols, v_cols = start_plane(
            hidden_tied, codes, gains, w_query, w_key, w_value, 1
        )
        hidden_low = hidden_low.reshape(tokens, width)
        codes = codes.reshape(members, length)
        gains = jnp.swapaxes(gains, 0, 1).reshape(2, width)
        core_at = lax.axis_index("sub") * HD
        qkv = jnp.concatenate(
            [
                q_cols,
                lax.dynamic_slice_in_dim(k_cols, core_at, HD, axis=2),
                lax.dynamic_slice_in_dim(v_cols, core_at, HD, axis=2),
            ],
            axis=2,
        ).reshape(width, q_width + 2 * k_width)
        gate_up = lax.all_gather(quarter, "rep", axis=1, tiled=True).reshape(width, -1)
    else:
        gains = lax.all_gather(gains, "fsdp", axis=1, tiled=True)
        codes = gather_tokens(codes)
        hidden_low = gather_tokens(hidden_in[0])
        qkv = regroup_columns((w_query, w_key, w_value), owners, subs)
        gate_up = regroup_columns((w_gate, w_up), owners, subs)
    gain_attn = gains[0].astype(F32)
    gain_mlp = gains[1].astype(F32)
    ff = gate_up.shape[1] // 2

    cos_table, sin_table = rope_tables(length, HD)
    if kernels:
        plain = jnp.ones((length, HD), F32)
        tables = (
            jnp.concatenate([cos_table] * (2 * (GROUPS + 1)) + [plain], axis=1),
            jnp.concatenate([sin_table] * (2 * (GROUPS + 1)) + [plain * 0.0], axis=1),
        )
        normed_one, heads, attended, mlp_out_grad = attend(
            hidden_low.reshape(members, length, width), gain_attn[None], qkv, tables, codes,
            mlp_out_low, 9,
        )
        normed_one = normed_one.reshape(tokens, width)
        mlp_out_grad = mlp_out_grad.reshape(tokens, width)
        attended = attended.reshape(tokens, q_width)
    else:
        hidden_all = hidden_low.astype(F32)
        normed_one = (hidden_all * row_scale(hidden_all) * gain_attn).astype(BF16)
        projected = dot_f32(normed_one, qkv)
        cos_heads = cos_table[None, :, None, :]
        sin_heads = sin_table[None, :, None, :]
        per_seq = projected.reshape(members, length, GROUPS + 2, HD)
        queries = rotate(per_seq[:, :, :GROUPS], cos_heads, sin_heads).astype(BF16)
        keys = rotate(per_seq[:, :, GROUPS : GROUPS + 1], cos_heads, sin_heads).astype(BF16)[:, :, 0]
        values = per_seq[:, :, GROUPS + 1].astype(BF16)

        segments, validity = codes // 2, codes % 2
        row_index = jnp.arange(length, dtype=jnp.int32)[:, None]
        col_index = jnp.arange(length, dtype=jnp.int32)[None, :]
        allowed = (
            (segments[:, :, None] == segments[:, None, :])
            & (col_index <= row_index)
            & ((validity[:, None, :] == 1) | (col_index == row_index))
        )[:, None]
        scores = jnp.einsum("stgd,sud->sgtu", queries, keys, preferred_element_type=F32) * SCORE_SCALE
        scores = jnp.where(allowed, scores, MASKED_SCORE)
        shifted = jnp.exp(scores - jnp.max(scores, axis=-1, keepdims=True))
        probs = shifted / jnp.sum(shifted, axis=-1, keepdims=True)
        probs_low = probs.astype(BF16)
        attended = jnp.einsum("sgtu,sud->stgd", probs_low, values, preferred_element_type=F32)
        attended = attended.reshape(tokens, q_width).astype(BF16)
    (attn_branch,) = scattered([attended], w_output, False, 2)

    hidden = hidden_in[0].astype(F32)
    scale_one = row_scale(hidden)
    unit_one = hidden * scale_one
    middle = hidden + RESIDUAL_SCALE * attn_branch
    scale_two = row_scale(middle)
    unit_two = middle * scale_two
    (normed_two,) = gathered([(unit_two * gain_mlp).astype(BF16)], 3)
    if not kernels:
        (mlp_out_grad,) = gathered([mlp_out_low], 3)
    gate_up_proj = dot_f32(normed_two, gate_up)
    gate_proj, up_proj = gate_up_proj[:, :ff], gate_up_proj[:, ff:]
    sigma = jax.nn.sigmoid(gate_proj)
    silu_gate = gate_proj * sigma
    mixed_act = (silu_gate * up_proj).astype(BF16)

    down_w_grad = contract_rows(mixed_act, mlp_out_grad).astype(BF16)
    down_w_piece = sum_planes(down_w_grad)
    mixed_grad = contract_cols(after(mlp_out_grad, down_w_grad), row_block(w_down, subs))
    slope = sigma * (1.0 + gate_proj * (1.0 - sigma))
    gate_grad = (mixed_grad * up_proj * slope).astype(BF16)
    up_grad = (mixed_grad * silu_gate).astype(BF16)
    gate_w_grad = contract_rows(normed_two, gate_grad).astype(BF16)
    up_w_grad = contract_rows(normed_two, up_grad).astype(BF16)
    gate_sum = sum_planes(owner_major(gate_w_grad))
    gate_up_grad = [after(gate_grad, gate_w_grad, up_w_grad), up_grad]
    (normed_two_grad,) = scattered(gate_up_grad, gate_up, True, 4)
    gain_mlp_grad, middle_part = norm_backward(normed_two_grad, scale_two, unit_two, gain_mlp)
    middle_grad = result_grad + middle_part

    attn_out_low = (RESIDUAL_SCALE * middle_grad).astype(BF16)
    passed = [KeepJob(down_w_piece)] if kernels else []
    attn_out_grad, *passed = gathered([attn_out_low], 5, passed)
    down_spread = spread_planes(passed[0] if kernels else down_w_piece)
    if kernels:
        qkv_grad, output_w_grad = attend_back(
            attn_out_grad.reshape(members, length, width), row_block(w_output, subs), heads,
            attended.reshape(members, length, q_width), tables, codes,
        )
        qkv_grad = qkv_grad.reshape(tokens, q_width + 2 * k_width)
    else:
        attended_grad = contract_cols(attn_out_grad, row_block(w_output, subs)).astype(BF16)
        output_w_grad = contract_rows(attended, attn_out_grad).astype(BF16)
        heads_grad = attended_grad.reshape(members, length, GROUPS, HD)
        prob_grad = jnp.einsum("stgd,sud->sgtu", heads_grad, values, preferred_element_type=F32)
        row_dot = jnp.sum(probs * prob_grad, axis=-1, keepdims=True)
        score_grad = (probs * (prob_grad - row_dot)).astype(BF16)
        query_grad = (
            jnp.einsum("sgtu,sud->stgd", score_grad, keys, preferred_element_type=F32) * SCORE_SCALE
        )
        key_grad = (
            jnp.einsum("sgtu,stgd->sud", score_grad, queries, preferred_element_type=F32) * SCORE_SCALE
        )
        value_grad = jnp.einsum("sgtu,stgd->sud", probs_low, heads_grad, preferred_element_type=F32)
        qkv_grad = jnp.concatenate(
            [
                rotate(query_grad, cos_heads, -sin_heads),
                rotate(key_grad[:, :, None], cos_heads, -sin_heads),
                value_grad[:, :, None],
            ],
            axis=2,
        )
        qkv_grad = qkv_grad.reshape(tokens, q_width + 2 * k_width).astype(BF16)
    qkv_tied = after(qkv_grad, output_w_grad)
    gate_job = [ExchangeJob(gate_sum)] if kernels else []
    normed_one_grad, *gate_piece = scattered([qkv_tied], qkv, True, 6, gate_job)
    qkv_grad = after(qkv_grad, normed_one_grad)
    qkv_w_grad = contract_rows(normed_one, qkv_grad).astype(BF16)
    gain_attn_grad, hidden_part = norm_backward(normed_one_grad, scale_one, unit_one, gain_attn)
    input_grad = (middle_grad + hidden_part).astype(BF16)

    mixed_tied = after(mixed_act, normed_one_grad, qkv_w_grad, down_spread)
    last_jobs = []
    if kernels:
        up_job = SumJob(
            [up_w_grad, qkv_w_grad], 4, 4, reps,
            {1: range(4), 2: range(4, 8), 3: range(8, 12), 4: range(12, 17)},
        )
        output_job = SumJob([output_w_grad], 1, 2, reps, {4: range(3)})
        last_jobs = [KeepJob(gate_piece[0]), up_job, output_job]
        last_jobs += [HandJob(up_job, reps, 2), HandJob(output_job, reps, 2)]
    mlp_branch, *last = scattered([mixed_tied], w_down, False, 7, last_jobs)
    result = middle + RESIDUAL_SCALE * mlp_branch

    validity_own = valid_mask[0].astype(F32)[:, None]
    squares = [
        jnp.sum(tensor * tensor * validity_own)
        for tensor in (hidden, middle, result, attn_branch, mlp_branch)
    ]
    tally = jnp.concatenate(
        [gain_attn_grad, gain_mlp_grad, jnp.stack(squares + [jnp.sum(validity_own)])]
    )
    tally = tally_all(tally, reps, 8) if kernels else lax.psum(tally, ("rep", "sub", "fsdp"))
    part = width // owners
    start = lax.axis_index("fsdp") * part
    gain_attn_out = lax.dynamic_slice_in_dim(tally, start, part)
    gain_mlp_out = lax.dynamic_slice_in_dim(tally, width + start, part)
    statistics = jnp.sqrt(tally[2 * width : 2 * width + 5] / (tally[2 * width + 5] * width))

    if kernels:
        gate_piece, up_handed, output_handed = last
        gate_spread = spread_planes(gate_piece)
        down_out = cast_rows(down_spread)
        output_out = cast_rows(output_handed.reshape((2, 2) + output_handed.shape[3:]))
        gate_out, up_out = cast_columns(gate_spread, ff), cast_columns(up_handed, ff)
        query_out, key_out, value_out = cast_heads(up_handed, ff)
    else:
        down_out, output_out = (
            jnp.swapaxes(s, 0, 1).reshape(-1, width).astype(F32)
            for s in (down_spread, spread_planes(sum_planes(output_w_grad)))
        )
        gate_spread, up_spread, qkv_spread = (
            spread_planes(to_owners(g))
            for g in (
                gate_sum,
                sum_planes(owner_major(up_w_grad)),
                sum_planes(owner_major(qkv_w_grad)),
            )
        )
        gate_out, up_out = place_columns(gate_spread), place_columns(up_spread)
        query_out = place_columns(qkv_spread[..., :q_width])
        key_out = place_columns(qkv_spread[..., q_width : q_width + k_width])
        value_out = place_columns(qkv_spread[..., q_width + k_width :])
    return (
        result.astype(BF16)[None],
        input_grad[None],
        gain_attn_out,
        query_out,
        key_out,
        value_out,
        output_out,
        gain_mlp_out,
        gate_out,
        up_out,
        down_out,
        statistics,
    )


def solution(mesh):
    fsdp = mesh.shape["fsdp"]
    subs = max(1, KV // fsdp)
    rep = mesh.shape["dp"] // subs
    kernels = fsdp == 4 and subs == 2 and rep >= 3
    plane_mesh = Mesh(mesh.devices.reshape(rep, subs, fsdp), ("rep", "sub", "fsdp"))
    batch = ("rep", "sub", "fsdp")
    return jax.shard_map(
        functools.partial(shards, kernels),
        mesh=plane_mesh,
        in_specs=(
            P(batch, None, None),
            P(batch, None),
            P(batch, None),
            P(batch, None, None),
            P("fsdp"),
            P("fsdp", None),
            P("fsdp", None),
            P("fsdp", None),
            P("fsdp", None),
            P("fsdp"),
            P("fsdp", None),
            P("fsdp", None),
            P("fsdp", None),
        ),
        out_specs=(
            P(batch, None, None),
            P(batch, None, None),
            P("fsdp"),
            P("fsdp", None),
            P("fsdp", None),
            P("fsdp", None),
            P("fsdp", None),
            P("fsdp"),
            P("fsdp", None),
            P("fsdp", None),
            P("fsdp", None),
            P(),
        ),
        check_vma=False,
    )
```

```python
import functools

import jax
import jax.numpy as jnp
import numpy as np
from jax import lax
from jax.experimental import pallas as pl
from jax.experimental.pallas import tpu as pltpu
from jax.sharding import Mesh
from jax.sharding import PartitionSpec as P

H = 32
KV = 8
HD = 64
GROUPS = H // KV

EPSILON = 1e-05
RESIDUAL_SCALE = 0.22
SCORE_SCALE = 1.0 / 64.0
MASKED_SCORE = -1e30
ROPE_BASE = 10000000.0

BF16 = jnp.bfloat16
F32 = jnp.float32
MESH = pl.DeviceIdType.MESH
SCALE = 3_300_000
HBM = pl.BlockSpec(memory_space=pltpu.HBM)
VM = pl.BlockSpec(memory_space=pltpu.VMEM)


def rope_tables(length, head_size):
    half_size = head_size // 2
    frequency = ROPE_BASE ** (-(jnp.arange(half_size, dtype=F32) * 2.0 / head_size))
    angles = jnp.arange(length, dtype=F32)[:, None] * frequency[None, :]
    return (jnp.cos(angles), jnp.sin(angles))


def turn_tables(length):
    half = HD // 2
    frequency = (ROPE_BASE ** (-2.0 * np.arange(half) / HD)).astype(np.float32)
    angles = np.arange(length, dtype=np.float32)[:, None] * frequency[None, :]
    plain = np.zeros((length, HD))
    angles = np.concatenate([angles] * (2 * (GROUPS + 1)) + [plain], axis=1).astype(np.float64)
    return jnp.asarray(np.cos(angles), F32), jnp.asarray(np.sin(angles), F32)


def rotate(tensor, cos_table, sin_table):
    half_size = tensor.shape[-1] // 2
    front_half = tensor[..., :half_size]
    back_half = tensor[..., half_size:]
    return jnp.concatenate(
        [
            front_half * cos_table - back_half * sin_table,
            back_half * cos_table + front_half * sin_table,
        ],
        axis=-1,
    )


def dot_f32(left, right):
    return jnp.dot(left, right, preferred_element_type=F32)


def contract_rows(left, right):
    return jnp.einsum("sa,sb->ab", left, right, preferred_element_type=F32)


def contract_cols(left, right):
    return jnp.einsum("sb,ab->sa", left, right, preferred_element_type=F32)


def row_scale(source):
    return lax.rsqrt(jnp.mean(source * source, axis=-1, keepdims=True) + EPSILON)


def norm_backward(grad_norm, scale_row, unit_rows, gain):
    gain_grad = jnp.sum(grad_norm * unit_rows, axis=0)
    scaled = grad_norm * gain
    source_grad = scale_row * (
        scaled - unit_rows * jnp.mean(scaled * unit_rows, axis=-1, keepdims=True)
    )
    return (gain_grad, source_grad)


def after(value, *others):
    return lax.optimization_barrier((value,) + others)[0]


def plane_position():
    rep, core, own = lax.axis_index("rep"), lax.axis_index("sub"), lax.axis_index("fsdp")
    row, col = own // 2, own % 2
    across = row * 2 + (1 - col)
    down = (1 - row) * 2 + col
    corner = (1 - row) * 2 + (1 - col)
    return rep, core, own, across, down, corner


def meet(devices):
    barrier = pltpu.get_barrier_semaphore()
    for device in devices:
        pl.semaphore_signal(barrier, inc=1, device_id=device, device_id_type=MESH)
    pl.semaphore_wait(barrier, len(devices))


def params(collective_id, megabytes=16):
    return pltpu.CompilerParams(
        collective_id=collective_id, has_side_effects=True, vmem_limit_bytes=megabytes << 20
    )


def link_cost(microseconds, flops=0):
    return pl.CostEstimate(
        flops=0, bytes_accessed=int(microseconds * SCALE), transcendentals=0
    )


class Sender:
    def __init__(self, send_sems, recv_sems):
        self.send_sems, self.recv_sems, self.copies = send_sems, recv_sems, []

    def send(self, src, dst, device):
        copy = self.make(src, dst, device)
        copy.start()
        return copy

    def make(self, src, dst, device):
        index = len(self.copies)
        copy = pltpu.make_async_remote_copy(
            src_ref=src,
            dst_ref=dst,
            send_sem=self.send_sems.at[index],
            recv_sem=self.recv_sems.at[index],
            device_id=device,
            device_id_type=MESH,
        )
        self.copies.append(copy)
        return copy

    def finish(self):
        for copy in self.copies:
            copy.wait_send()


class Bounce:
    def __init__(self, src, dst, room, sems):
        self.fetch = pltpu.make_async_copy(src, room, sems.at[0])
        self.store = pltpu.make_async_copy(room, dst, sems.at[1])

    def start(self):
        self.fetch.start()

    def turn(self):
        self.fetch.wait()
        self.store.start()

    def wait(self):
        self.store.wait()


class Gather:
    def __init__(self, sender, x_ref, out_ref, local_sem, place):
        rep, core, own, across, down, corner = place
        to_across, to_down, to_core = (rep, core, across), (rep, core, down), (rep, 1 - core, own)
        half = x_ref.shape[0] // 2
        low, high, whole = pl.ds(0, half), pl.ds(half, half), pl.ds(0, 2 * half)
        base = core * 4

        def first(rows, device):
            return sender.make(x_ref.at[rows], out_ref.at[base + own, rows], device)

        def forward(block, rows, device):
            ref = out_ref.at[base + block, rows]
            return sender.make(ref, ref, device)

        self.across_low, self.down_high = first(low, to_across), first(high, to_down)
        self.across_high, self.down_low = first(high, to_across), first(low, to_down)
        self.corner_low = forward(across, low, to_down)
        self.corner_high = forward(down, high, to_across)
        self.swap_own = first(whole, to_core)
        self.swap_near = [
            forward(across, low, to_core),
            forward(down, high, to_core),
            forward(across, high, to_core),
            forward(down, low, to_core),
        ]
        self.swap_corner = [forward(corner, low, to_core), forward(corner, high, to_core)]
        self.mine = pltpu.make_async_copy(x_ref, out_ref.at[base + own], local_sem)

    def begin(self):
        for copy in (self.across_low, self.down_high, self.across_high, self.down_low):
            copy.start()
        self.swap_own.start()
        self.mine.start()

    def relay(self):
        self.relay_first()
        self.relay_second()

    def relay_first(self):
        self.across_low.wait_recv()
        self.corner_low.start()
        self.swap_near[0].start()
        self.down_high.wait_recv()
        self.corner_high.start()
        self.swap_near[1].start()

    def relay_second(self):
        self.across_high.wait_recv()
        self.swap_near[2].start()
        self.down_low.wait_recv()
        self.swap_near[3].start()

    def finish(self):
        self.pass_corner()
        self.arrive()

    def pass_corner(self):
        self.corner_low.wait_recv()
        self.swap_corner[0].start()
        self.corner_high.wait_recv()
        self.swap_corner[1].start()

    def arrive(self):
        for swap in [self.swap_own] + self.swap_near + self.swap_corner:
            swap.wait_recv()
        self.mine.wait()


class ExchangeJob:
    climbs = False
    corner = True

    def __init__(self, source):
        self.rows = source.shape[0] // 4
        shape = (self.rows, source.shape[1])
        self.arrays = [source]
        self.outs = [jax.ShapeDtypeStruct((4,) + shape, BF16)]
        self.scratch = [pltpu.SemaphoreType.DMA((3,))] * 2
        self.scratch += [pltpu.VMEM(shape, BF16), pltpu.SemaphoreType.DMA((2,))]

    def open(self, arrays, outs, scratch, place):
        self.source, self.out, self.place = arrays[0], outs[0], place
        own = place[2]
        self.sems = scratch[:2]
        self.keep = Bounce(self.part(own), self.out.at[own], scratch[2], scratch[3])

    def part(self, block):
        return self.source.at[pl.ds(pl.multiple_of(block * self.rows, 16), self.rows)]

    def stage(self, n):
        rep, core, own, across, down, corner = self.place
        if n == 0:
            self.keep.start()
            self.sender = Sender(*self.sems)
            for peer in (corner, across, down):
                self.sender.send(self.part(peer), self.out.at[own], (rep, core, peer))
        if n == 1:
            self.keep.turn()
        if n == 6:
            for copy in self.sender.copies:
                copy.wait()
            self.keep.wait()


class KeepJob:
    climbs = False
    corner = False

    def __init__(self, source):
        self.arrays = [source]
        self.outs = [jax.ShapeDtypeStruct(source.shape, BF16)]
        self.scratch = [pltpu.VMEM(source.shape, BF16), pltpu.SemaphoreType.DMA((2,))]

    def open(self, arrays, outs, scratch, place):
        self.keep = Bounce(arrays[0], outs[0], *scratch)

    def stage(self, n):
        if n == 0:
            self.keep.start()
        if n == 1:
            self.keep.turn()
        if n == 6:
            self.keep.wait()


def column_place(place, reps):
    rep, core, own = place[:3]
    up = (rep == 0, rep == reps - 1, (rep + 1, core, own), (rep - 1, core, own))
    down = (rep == reps - 1, rep == 0, (rep - 1, core, own), (rep + 1, core, own))
    return (up, down)


def skewed(rep, reps, count, act, i):
    for low in (True, False):
        near = 0 if low else 1

        @pl.when((rep * 2 < reps) == low)
        def _(near=near):
            if i < count:
                act(near, i)
            if i >= 1:
                act(1 - near, i - 1)


class SumJob:
    climbs = True

    def __init__(self, sources, blocks, cuts, reps, steps):
        self.blocks, self.cuts, self.reps, self.steps = blocks, cuts, reps, steps
        self.arrays = sources
        self.corner = blocks > 1
        rows = sources[0].shape[0]
        self.span = rows // blocks
        self.half = self.span // 2
        self.size = self.half // cuts
        self.widths = [source.shape[1] for source in sources]
        wide = sum(self.widths)
        self.shape = (2, blocks, self.half, wide)
        self.outs = []
        self.count = blocks * cuts
        sems = pltpu.SemaphoreType.DMA((2, self.count))
        self.scratch = [
            pltpu.VMEM(self.shape, BF16),
            pltpu.VMEM(self.shape, BF16),
            pltpu.VMEM(self.shape, BF16),
            pltpu.SemaphoreType.DMA((2, blocks, len(sources))),
        ] + [sems] * 5

    def open(self, arrays, outs, scratch, place):
        self.sources = arrays
        self.held, self.landed, self.fin, self.load_sems = scratch[:4]
        self.chain_sems, self.give_sems, self.keep_sems = scratch[4:6], scratch[6:8], scratch[8]
        self.rep, self.core, self.own = place[:3]
        self.ways = column_place(place, self.reps)
        for k in range(self.blocks):
            for way in range(2):
                for load in self.loads(way, k):
                    load.start()

    def block(self, k):
        return (self.own + k) % self.blocks

    def loads(self, way, k):
        copies = []
        at = 0
        for n, (source, width) in enumerate(zip(self.sources, self.widths)):
            start = pl.multiple_of(self.block(k) * self.span + way * self.half, 16)
            src = source.at[pl.ds(start, self.half)]
            dst = self.held.at[way, k, :, pl.ds(at, width)]
            copies.append(pltpu.make_async_copy(src, dst, self.load_sems.at[way, k, n]))
            at += width
        return copies

    def rows(self, i):
        return i // self.cuts, pl.ds(i % self.cuts * self.size, self.size)

    def chain(self, way, i):
        k, rows = self.rows(i)
        return pltpu.make_async_remote_copy(
            src_ref=self.held.at[way, k, rows],
            dst_ref=self.landed.at[way, k, rows],
            send_sem=self.chain_sems[0].at[way, i],
            recv_sem=self.chain_sems[1].at[way, i],
            device_id=self.ways[way][2],
            device_id_type=MESH,
        )

    def give(self, way, i):
        k, rows = self.rows(i)
        return pltpu.make_async_remote_copy(
            src_ref=self.held.at[way, k, rows],
            dst_ref=self.fin.at[way, self.own, rows],
            send_sem=self.give_sems[0].at[way, i],
            recv_sem=self.give_sems[1].at[way, i],
            device_id=(self.rep, self.core, self.block(k)),
            device_id_type=MESH,
        )

    def keep(self, way, i):
        k, rows = self.rows(i)
        own = self.own if self.blocks > 1 else 0
        src, dst = self.held.at[way, k, rows], self.fin.at[way, own, rows]
        return pltpu.make_async_copy(src, dst, self.keep_sems.at[way, i])

    def loaded(self, way, i):
        if i % self.cuts == 0:
            for load in self.loads(way, i // self.cuts):
                load.wait()

    def prime(self):
        for way in range(2):

            @pl.when(self.ways[way][0])
            def _(way=way):
                for i in range(self.count):
                    self.loaded(way, i)
                    self.chain(way, i).start()

    def add(self, way, i):
        first, last = self.ways[way][:2]
        k, rows = self.rows(i)

        @pl.when(jnp.logical_not(first))
        def _():
            self.loaded(way, i)
            self.chain(way, i).wait_recv()
            self.held[way, k, rows] = self.held[way, k, rows] + self.landed[way, k, rows]

            @pl.when(jnp.logical_not(last))
            def _():
                self.chain(way, i).start()

            @pl.when(last)
            def _():
                if k == 0:
                    self.keep(way, i).start()
                else:
                    self.give(way, i).start()

    def step(self, i):
        skewed(self.rep, self.reps, self.count, self.add, i)

    def stage(self, n):
        if n == 0:
            self.prime()
        if n in self.steps:
            for i in self.steps[n]:
                self.step(i)
        if n == 7:
            for way in range(2):
                last = self.ways[way][1]
                for i in range(self.count):

                    @pl.when(jnp.logical_not(last))
                    def _(way=way, i=i):
                        self.chain(way, i).wait_send()

                    @pl.when(last)
                    def _(way=way, i=i):
                        if i // self.cuts == 0:
                            self.keep(way, i).wait()
                        else:
                            self.give(way, i).wait()


class HandJob:
    climbs = True

    def __init__(self, sums, reps, cuts):
        self.sums, self.arrays = sums, []
        shape = sums.shape
        self.reps, self.cuts, self.size = reps, cuts, shape[2] // cuts
        self.count = shape[1] * cuts
        self.corner = False
        self.outs = [jax.ShapeDtypeStruct((2, 2) + shape[1:], BF16)]
        self.scratch = [pltpu.SemaphoreType.DMA((2, self.count))] * 5

    def open(self, arrays, outs, scratch, place):
        self.out = outs[0]
        self.hand_sems, self.side_sems, self.keep_sems = scratch[:2], scratch[2:4], scratch[4]
        self.rep, self.core, self.own = place[:3]
        self.ways = column_place(place, self.reps)

    def rows(self, j):
        return j // self.cuts, pl.ds(j % self.cuts * self.size, self.size)

    def place(self, way, j):
        block, rows = self.rows(j)
        return self.out.at[way, self.core, block, rows]

    def remote(self, src, way, j, sems, device):
        return pltpu.make_async_remote_copy(
            src_ref=src,
            dst_ref=self.place(way, j),
            send_sem=sems[0].at[way, j],
            recv_sem=sems[1].at[way, j],
            device_id=device,
            device_id_type=MESH,
        )

    def beside(self):
        return (self.rep, 1 - self.core, self.own)

    def begin(self):
        fin = self.sums.fin
        for j in range(self.count):
            for way in range(2):

                @pl.when(self.ways[way][1])
                def _(way=way, j=j):
                    block, rows = self.rows(j)
                    src = fin.at[way, block, rows]
                    self.remote(src, way, j, self.hand_sems, self.ways[way][3]).start()
                    self.remote(src, way, j, self.side_sems, self.beside()).start()
                    dst = self.place(way, j)
                    pltpu.make_async_copy(src, dst, self.keep_sems.at[way, j]).start()

    def hand(self, way, j):
        first, last = self.ways[way][:2]

        @pl.when(jnp.logical_not(last))
        def _():
            ref = self.place(way, j)
            hand = self.remote(ref, way, j, self.hand_sems, self.ways[way][3])
            hand.wait_recv()

            @pl.when(jnp.logical_not(first))
            def _():
                hand.start()

            self.remote(ref, way, j, self.side_sems, self.beside()).start()

    def pass_on(self):
        for j in range(self.count + 1):
            skewed(self.rep, self.reps, self.count, lambda w, i: self.hand(1 - w, i), j)

    def close(self):
        for j in range(self.count):
            for way in range(2):
                first, last = self.ways[way][:2]
                ref = self.place(way, j)
                self.remote(ref, way, j, self.side_sems, self.beside()).wait()

                @pl.when(jnp.logical_not(first))
                def _(way=way, j=j, ref=ref):
                    self.remote(ref, way, j, self.hand_sems, self.ways[way][3]).wait_send()

                @pl.when(last)
                def _(way=way, j=j, ref=ref):
                    pltpu.make_async_copy(ref, ref, self.keep_sems.at[way, j]).wait()

    def stage(self, n):
        if n == 7:
            self.begin()
        if n == 8:
            self.pass_on()
        if n == 9:
            self.close()


class Jobs:
    def __init__(self, jobs, reps):
        self.jobs, self.reps = jobs, reps
        self.arrays = [a for job in jobs for a in job.arrays]
        self.out_shapes = [o for job in jobs for o in job.outs]
        self.scratch = [x for job in jobs for x in job.scratch]

    def greet(self, place):
        rep, core, own, across, down, corner = place
        devices = [(rep, core, across), (rep, core, down), (rep, 1 - core, own)]
        if any(job.climbs for job in self.jobs):
            devices += [((rep + 1) % self.reps, core, own)]
            devices += [((rep + self.reps - 1) % self.reps, core, own)]
        if any(job.corner for job in self.jobs):
            devices.append((rep, core, corner))
        meet(devices)

    def open(self, arrays, outs, scratch, place):
        arrays, outs, scratch = list(arrays), list(outs), list(scratch)

        def take(refs, count):
            taken = refs[:count]
            del refs[:count]
            return taken

        for job in self.jobs:
            mine = [take(arrays, len(job.arrays)), take(outs, len(job.outs))]
            job.open(*mine, take(scratch, len(job.scratch)), place)

    def stage(self, n):
        for job in self.jobs:
            job.stage(n)


def gather_kernel(count, jobs, *refs):
    arrays, outs = len(jobs.arrays), len(jobs.out_shapes)
    xs, job_arrays = refs[:count], refs[count : count + arrays]
    refs = refs[count + arrays :]
    x_outs, job_outs = refs[:count], refs[count : count + outs]
    refs = refs[count + outs :]
    local_sems, send_sems, recv_sems = refs[:3]
    place = plane_position()
    jobs.greet(place)
    sender = Sender(send_sems, recv_sems)
    moves = [
        Gather(sender, x, out, local_sems.at[i], place)
        for i, (x, out) in enumerate(zip(xs, x_outs))
    ]
    for move in moves:
        move.begin()
    jobs.open(job_arrays, job_outs, refs[3:], place)
    jobs.stage(0)
    jobs.stage(1)
    for move in moves:
        move.relay()
    jobs.stage(5)
    for move in moves:
        move.finish()
    sender.finish()
    for n in (6, 7, 8, 9):
        jobs.stage(n)


def gather_plane(blocks, collective_id, jobs=(), reps=1):
    count = len(blocks)
    jobs = Jobs(jobs, reps)
    return pl.pallas_call(
        functools.partial(gather_kernel, count, jobs),
        out_shape=[jax.ShapeDtypeStruct((8,) + x.shape, x.dtype) for x in blocks]
        + jobs.out_shapes,
        in_specs=[VM] * count + [HBM] * len(jobs.arrays),
        out_specs=[HBM] * (count + len(jobs.out_shapes)),
        scratch_shapes=[
            pltpu.SemaphoreType.DMA((count,)),
            pltpu.SemaphoreType.DMA((13 * count,)),
            pltpu.SemaphoreType.DMA((13 * count,)),
        ]
        + jobs.scratch,
        compiler_params=params(collective_id, 60),
        cost_estimate=link_cost(40 * count),
    )(*blocks, *jobs.arrays)


def column_source(ref, rows, block, width):
    return ref.at[rows, pl.ds(pl.multiple_of(block * width, width), width)]


def quarter_kernel(gate_ref, up_ref, out_ref, room, local_sems, send_sems, recv_sems):
    rep, core, own, across, down, corner = plane_position()
    peers = (corner, across, down)
    meet([(rep, core, peer) for peer in peers])
    rows = out_ref.shape[1]
    width = out_ref.shape[2] // 2
    mine = pl.ds(pl.multiple_of(rep * rows, rows), rows)
    sender = Sender(send_sems, recv_sems)
    local = []
    for k, ref in enumerate((gate_ref, up_ref)):
        columns = pl.ds(k * width, width)
        target = out_ref.at[own, :, columns]
        source = column_source(ref, mine, own * 2 + core, width)
        copy = Bounce(source, target, room.at[:, columns], local_sems.at[k])
        copy.start()
        local.append(copy)
        for peer in peers:
            source = column_source(ref, mine, peer * 2 + core, width)
            sender.send(source, target, (rep, core, peer))
    for copy in local:
        copy.turn()
    for copy in sender.copies:
        copy.wait_recv()
    sender.finish()
    for copy in local:
        copy.wait()


def quarter_columns(w_gate, w_up, reps, collective_id):
    rows, columns = w_gate.shape
    shape = (rows // reps, columns // 4)
    return pl.pallas_call(
        quarter_kernel,
        out_shape=jax.ShapeDtypeStruct((4,) + shape, BF16),
        in_specs=[HBM] * 2,
        out_specs=HBM,
        scratch_shapes=[
            pltpu.VMEM(shape, BF16),
            pltpu.SemaphoreType.DMA((2, 2)),
            pltpu.SemaphoreType.DMA((6,)),
            pltpu.SemaphoreType.DMA((6,)),
        ],
        compiler_params=params(collective_id, 60),
        cost_estimate=link_cost(25),
    )(w_gate, w_up)


def start_kernel(
    x_ref, code_ref, gain_ref, q_ref, k_ref, v_ref, x_out, code_out, gain_out, heads_out,
    room, bounce_sems, local_sems, send_sems, recv_sems,
):
    place = plane_position()
    rep, core, own, across, down, corner = place
    peers = (corner, across, down)
    others = [(rep, core, peer) for peer in peers] + [(rep, 1 - core, peer) for peer in peers]
    others.append((rep, 1 - core, own))
    meet(others)
    sender = Sender(send_sems, recv_sems)
    move = Gather(sender, x_ref, x_out, local_sems.at[0], place)
    direct = [sender.make(gain_ref, gain_out.at[own], (rep, core, peer)) for peer in peers]
    slot = code_out.at[core * 4 + own]
    direct += [sender.make(code_ref, slot, device) for device in others]
    whole = pl.ds(0, q_ref.shape[0])
    q_wide, pair = GROUPS * HD, 2 * HD

    def fetch(ref, at, width, blocks):
        columns = pl.ds(at, width)
        target = heads_out.at[own, :, columns]
        source = column_source(ref, whole, blocks[0], width)
        bounced = Bounce(source, target, room.at[:, columns], bounce_sems.at[min(at, 1)])
        sends = []
        for block, peer in zip(blocks[1:], peers):
            source = column_source(ref, whole, block, width)
            sends.append(sender.make(source, target, (rep, core, peer)))
        return bounced, sends

    def swap(at):
        columns = pl.ds(at, pair)
        copies = [sender.make(room.at[:, columns], heads_out.at[own, :, columns], others[-1])]
        for peer in peers:
            ref = heads_out.at[peer, :, columns]
            copies.append(sender.make(ref, ref, others[-1]))
        return copies

    q_kept, q_sends = fetch(q_ref, 0, q_wide, [block * 2 + core for block in (own,) + peers])
    direct += q_sends
    first = len(sender.copies)
    sides = []
    for ref, at in ((k_ref, q_wide), (v_ref, q_wide + pair)):
        kept, sends = fetch(ref, at, pair, (own,) + peers)
        swaps = swap(at)
        del sender.copies[first + len(sends) :]
        sides.append((kept, sends, swaps, swap(2 * q_wide + pair - at)))
        del sender.copies[first:]
    local = [
        pltpu.make_async_copy(gain_ref, gain_out.at[own], local_sems.at[1]),
        pltpu.make_async_copy(code_ref, slot, local_sems.at[2]),
    ]
    move.begin()
    for copy in direct + local + [q_kept]:
        copy.start()
    for side, (kept, sends, swaps, _) in enumerate(sides):

        @pl.when(core == side)
        def _(kept=kept, sends=sends, swaps=swaps):
            for copy in [kept] + sends:
                copy.start()
            kept.turn()
            swaps[0].start()

    q_kept.turn()
    move.relay()
    for side, (kept, sends, swaps, _) in enumerate(sides):

        @pl.when(core == side)
        def _(kept=kept, sends=sends, swaps=swaps):
            for copy, passed in zip(sends, swaps[1:]):
                copy.wait_recv()
                passed.start()

    move.finish()
    for copy in direct:
        copy.wait_recv()
    for side, (kept, sends, swaps, arrivals) in enumerate(sides):

        @pl.when(core == side)
        def _(kept=kept, sends=sends, swaps=swaps, arrivals=arrivals):
            for copy in arrivals:
                copy.wait_recv()
            for copy in sends + swaps:
                copy.wait_send()
            kept.wait()

    sender.finish()
    for copy in local + [q_kept]:
        copy.wait()


def start_plane(hidden, codes, gains, w_query, w_key, w_value, collective_id):
    heads = (w_query.shape[0], (GROUPS + 4) * HD)
    shapes = [
        ((8,) + hidden.shape, BF16),
        ((8,) + codes.shape, jnp.int32),
        ((4,) + gains.shape, BF16),
        ((4,) + heads, BF16),
    ]
    return pl.pallas_call(
        start_kernel,
        out_shape=[jax.ShapeDtypeStruct(s, d) for s, d in shapes],
        in_specs=[VM] * 3 + [HBM] * 3,
        out_specs=[HBM] * 4,
        scratch_shapes=[
            pltpu.VMEM(heads, BF16),
            pltpu.SemaphoreType.DMA((2, 2)),
            pltpu.SemaphoreType.DMA((3,)),
            pltpu.SemaphoreType.DMA((40,)),
            pltpu.SemaphoreType.DMA((40,)),
        ],
        compiler_params=params(collective_id, 60),
        cost_estimate=link_cost(60),
    )(hidden, codes, gains, w_query, w_key, w_value)


def mlp_kernel(
    x_ref, w_hbm, grad_hbm, x_out, product_out, act_out, down_out,
    x_all, w_ref, product, act, grad, total, down,
    w_sems, grad_sems, store_sems, down_sems, local_sem, send_sems, recv_sems,
):
    place = plane_position()
    rep, core, own, across, down_at, corner = place
    rows = x_ref.shape[0]
    ff = act.shape[2]
    tile, depth = 512, 256
    tiles = ff // tile
    here, there = core * 4, (1 - core) * 4
    order = [here + own, there + own, here + across, here + down_at]
    order += [there + across, there + down_at, here + corner, there + corner]
    loads = []
    for t in range(tiles):
        for k in range(2):
            columns = pl.ds(k * ff + t * tile, tile)
            load = pltpu.make_async_copy(w_hbm.at[:, columns], w_ref.at[:, columns], w_sems.at[t, k])
            load.start()
            loads.append(load)
    grads = [
        pltpu.make_async_copy(grad_hbm.at[block], grad.at[n % 2], grad_sems.at[n])
        for n, block in enumerate(order)
    ]
    grads[0].start()
    grads[1].start()
    meet([(rep, core, across), (rep, core, down_at), (rep, 1 - core, own)])
    sender = Sender(send_sems, recv_sems)
    move = Gather(sender, x_ref, x_all, local_sem, place)
    move.begin()
    pending, finals = [], []

    def piece(x, slot, at):
        gate = dot_f32(x, w_ref[:, pl.ds(at, tile)])
        up = dot_f32(x, w_ref[:, pl.ds(ff + at, tile)])
        product[slot, :, pl.ds(at, tile)] = gate
        product[slot, :, pl.ds(ff + at, tile)] = up
        act[slot, :, pl.ds(at, tile)] = (gate * jax.nn.sigmoid(gate) * up).astype(BF16)

    def compute(n):
        block, slot = order[n], n % 2
        if n >= 2:
            for store in pending[n - 2][:2]:
                store.wait()
        for t in range(tiles):
            if n == 0:
                loads[2 * t].wait()
                loads[2 * t + 1].wait()
            piece(x_all[block], slot, t * tile)
        mine = pl.ds(pl.multiple_of(block * rows, rows), rows)
        stores = [
            pltpu.make_async_copy(product.at[slot], product_out.at[mine], store_sems.at[n, 0]),
            pltpu.make_async_copy(act.at[slot], act_out.at[mine], store_sems.at[n, 1]),
            pltpu.make_async_copy(x_all.at[block], x_out.at[block], store_sems.at[n, 2]),
        ]
        for store in stores:
            store.start()
        pending.append(stores)

    def weigh(n):
        slot = n % 2
        grads[n].wait()

        def term(at):
            return lax.dot_general(
                act[slot, :, pl.ds(at, depth)], grad[slot], (((0,), (0,)), ((), ())),
                preferred_element_type=F32,
            )

        if n == 7:
            for r in range(ff // depth):
                at = pl.ds(r * depth, depth)
                down[at] = (total[at] + term(r * depth)).astype(BF16)
                final = pltpu.make_async_copy(down.at[at], down_out.at[at], down_sems.at[r])
                final.start()
                finals.append(final)
        else:

            @pl.loop(0, ff // depth)
            def _(r):
                start = pl.multiple_of(r * depth, depth)
                at = pl.ds(start, depth)
                total[at] = term(start) if n == 0 else total[at] + term(start)

        if n + 2 < 8:
            grads[n + 2].start()

    move.mine.wait()
    compute(0)
    move.swap_own.wait_recv()
    compute(1)
    move.relay_first()
    weigh(0)
    weigh(1)
    move.relay_second()
    compute(2)
    compute(3)
    for swap in move.swap_near:
        swap.wait_recv()
    weigh(2)
    compute(4)
    move.pass_corner()
    weigh(3)
    compute(5)
    weigh(4)
    compute(6)
    weigh(5)
    for swap in move.swap_corner:
        swap.wait_recv()
    compute(7)
    weigh(6)
    weigh(7)
    for k, stores in enumerate(pending):
        for store in stores if k >= 6 else stores[2:]:
            store.wait()
    for final in finals:
        final.wait()
    sender.finish()


def mlp_plane(x, w, grad, collective_id):
    rows, width = x.shape
    wide = w.shape[1]
    ff = wide // 2
    return pl.pallas_call(
        mlp_kernel,
        out_shape=[
            jax.ShapeDtypeStruct((8, rows, width), BF16),
            jax.ShapeDtypeStruct((8 * rows, wide), F32),
            jax.ShapeDtypeStruct((8 * rows, ff), BF16),
            jax.ShapeDtypeStruct((ff, width), BF16),
        ],
        in_specs=[VM, HBM, HBM],
        out_specs=[HBM] * 4,
        scratch_shapes=[
            pltpu.VMEM((8, rows, width), BF16),
            pltpu.VMEM((width, wide), BF16),
            pltpu.VMEM((2, rows, wide), F32),
            pltpu.VMEM((2, rows, ff), BF16),
            pltpu.VMEM((2, rows, width), BF16),
            pltpu.VMEM((ff, width), F32),
            pltpu.VMEM((ff, width), BF16),
            pltpu.SemaphoreType.DMA((ff // 512, 2)),
            pltpu.SemaphoreType.DMA((8,)),
            pltpu.SemaphoreType.DMA((8, 3)),
            pltpu.SemaphoreType.DMA((ff // 256,)),
            pltpu.SemaphoreType.DMA,
            pltpu.SemaphoreType.DMA((13,)),
            pltpu.SemaphoreType.DMA((13,)),
        ],
        compiler_params=params(collective_id, 60),
        cost_estimate=link_cost(50),
    )(x, w, grad)


def product_scatter_kernel(turned, count, jobs, *refs):
    arrays, outs = len(jobs.arrays), len(jobs.out_shapes)
    x_hbm, w_hbm, job_arrays = refs[:count], refs[count], refs[count + 1 : count + 1 + arrays]
    refs = refs[count + 1 + arrays :]
    out_ref, job_outs = refs[0], refs[1 : 1 + outs]
    refs = refs[1 + outs :]
    x_refs, w_ref = refs[:count], refs[count]
    (
        swap, held, from_core, from_across, from_down, last_across, last_down,
        x_sems, w_sems, core_send, core_recv, send_sems, recv_sems,
    ) = refs[count + 1 : count + 14]
    place = plane_position()
    rep, core, own, across, down, corner = place
    to_across, to_down, to_core = (rep, core, across), (rep, core, down), (rep, 1 - core, own)
    _, rows, wide = held.shape
    depth = x_refs[0].shape[1]
    tile = 512
    tiles = wide // tile
    half = rows // 2
    low, high = pl.ds(0, half), pl.ds(half, half)
    order = []
    for block in (corner, across, down, own):
        order += [(1 - core) * 4 + block, core * 4 + block]

    def rows_of(block):
        return pl.ds(pl.multiple_of(block * rows, rows), rows)

    x_loads = [
        [
            pltpu.make_async_copy(
                x_hbm[i].at[rows_of(block)], x_refs[i].at[rows_of(block)], x_sems.at[i, n]
            )
            for i in range(count)
        ]
        for n, block in enumerate(order)
    ]
    w_loads = []
    for t in range(tiles):
        columns = pl.ds(t * tile, tile)
        if turned:
            src, dst = w_hbm.at[columns], w_ref.at[columns]
        else:
            kept = pl.ds(pl.multiple_of(core * depth, depth), depth)
            src, dst = w_hbm.at[kept, columns], w_ref.at[:, columns]
        w_loads.append(pltpu.make_async_copy(src, dst, w_sems.at[t]))
    for load in x_loads[0]:
        load.start()
    for load in w_loads:
        load.start()
    for loads in x_loads[1:]:
        for load in loads:
            load.start()
    jobs.open(job_arrays, job_outs, refs[count + 14 :], place)
    jobs.greet(place)
    jobs.stage(0)

    def product(dst, mine, columns):
        total = None
        for i in range(count):
            x = x_refs[i][mine, :]
            if turned:
                w = w_ref[columns, pl.ds(i * depth, depth)]
                part = lax.dot_general(
                    x, w, (((1,), (1,)), ((), ())), preferred_element_type=F32
                )
            else:
                part = dot_f32(x, w_ref[:, columns])
            total = part if total is None else total + part
        dst[:, columns] = total.astype(BF16)

    def fill(dst, n):
        for load in x_loads[n]:
            load.wait()
        mine = rows_of(order[n])
        if n == 0:
            for t in range(tiles):
                w_loads[t].wait()
                product(dst, mine, pl.ds(t * tile, tile))
        else:

            @pl.loop(0, tiles)
            def _(t):
                product(dst, mine, pl.ds(pl.multiple_of(t * tile, tile), tile))

    swaps = Sender(core_send, core_recv)
    sender = Sender(send_sems, recv_sems)
    sent = {}
    for k in range(4):
        fill(swap.at[k], 2 * k)
        swaps.send(swap.at[k], from_core.at[k], to_core)
        fill(held.at[k], 2 * k + 1)
        swaps.copies[k].wait_recv()
        held[k] = held[k] + from_core[k]
        if k == 0:
            sent[0] = sender.send(held.at[0, low], from_across.at[0], to_across)
            sent[1] = sender.send(held.at[0, high], from_down.at[0], to_down)
        if k == 1:
            sent[2] = sender.send(held.at[1, low], from_across.at[1], to_across)
        if k == 2:
            sent[3] = sender.send(held.at[2, high], from_down.at[1], to_down)
        jobs.stage(1 + k)
    sent[0].wait_recv()
    held[2, low] = held[2, low] + from_across[0]
    to_last = sender.send(held.at[2, low], last_down, to_down)
    sent[1].wait_recv()
    held[1, high] = held[1, high] + from_down[0]
    across_last = sender.send(held.at[1, high], last_across, to_across)
    jobs.stage(5)
    sent[2].wait_recv()
    sent[3].wait_recv()
    to_last.wait_recv()
    out_ref[low] = (
        held[3, low].astype(F32) + from_across[1].astype(F32) + last_down[...].astype(F32)
    )
    across_last.wait_recv()
    out_ref[high] = (
        held[3, high].astype(F32) + from_down[1].astype(F32) + last_across[...].astype(F32)
    )
    swaps.finish()
    sender.finish()
    for n in (6, 7, 8, 9):
        jobs.stage(n)


def product_scatter(xs, w, turned, collective_id, jobs=(), reps=1):
    count = len(xs)
    jobs = Jobs(jobs, reps)
    tokens, depth = xs[0].shape
    rows = tokens // 8
    wide = w.shape[0] if turned else w.shape[1]
    half = rows // 2
    return pl.pallas_call(
        functools.partial(product_scatter_kernel, turned, count, jobs),
        out_shape=[jax.ShapeDtypeStruct((rows, wide), F32)] + jobs.out_shapes,
        in_specs=[HBM] * (count + 1 + len(jobs.arrays)),
        out_specs=[VM] + [HBM] * len(jobs.out_shapes),
        scratch_shapes=[pltpu.VMEM((tokens, depth), BF16)] * count
        + [
            pltpu.VMEM((wide, depth * count) if turned else (depth, wide), BF16),
            pltpu.VMEM((4, rows, wide), BF16),
            pltpu.VMEM((4, rows, wide), BF16),
            pltpu.VMEM((4, rows, wide), BF16),
            pltpu.VMEM((2, half, wide), BF16),
            pltpu.VMEM((2, half, wide), BF16),
            pltpu.VMEM((half, wide), BF16),
            pltpu.VMEM((half, wide), BF16),
            pltpu.SemaphoreType.DMA((count, 8)),
            pltpu.SemaphoreType.DMA((wide // 512,)),
            pltpu.SemaphoreType.DMA((4,)),
            pltpu.SemaphoreType.DMA((4,)),
            pltpu.SemaphoreType.DMA((6,)),
            pltpu.SemaphoreType.DMA((6,)),
        ]
        + jobs.scratch,
        compiler_params=params(collective_id, 60),
        cost_estimate=link_cost(44, 2 * tokens * depth * count * wide),
    )(*xs, w, *jobs.arrays)


def turn(value, cos_ref, sin_ref, back):
    wide = value.shape[1]
    lanes = lax.broadcasted_iota(jnp.int32, value.shape, 1)
    front = lax.rem(lanes, HD) < HD // 2
    ahead = pltpu.roll(value, wide - HD // 2, 1)
    behind = pltpu.roll(value, HD // 2, 1)
    swapped = jnp.where(front, -ahead, behind) * sin_ref[...]
    turned = value * cos_ref[...]
    return turned - swapped if back else turned + swapped


def allowed_pairs(row_ref, col_ref):
    keys, queries = row_ref[0], col_ref[0]
    length = keys.shape[1]
    row_index = lax.broadcasted_iota(jnp.int32, (length, length), 0)
    col_index = lax.broadcasted_iota(jnp.int32, (length, length), 1)
    same = lax.shift_right_logical(keys, 1) == lax.shift_right_logical(queries, 1)
    valid = jnp.bitwise_and(keys, 1) == 1
    return same & (col_index <= row_index) & (valid | (col_index == row_index))


def head_probs(query, keys, allowed):
    scores = lax.dot_general(
        query, keys, (((1,), (1,)), ((), ())), preferred_element_type=F32
    )
    scores = jnp.where(allowed, scores * SCORE_SCALE, MASKED_SCORE)
    shifted = jnp.exp(scores - jnp.max(scores, axis=-1, keepdims=True))
    return shifted / jnp.sum(shifted, axis=-1, keepdims=True)


def attend_kernel(
    x_ref, gain_ref, w_ref, cos_ref, sin_ref, row_ref, col_ref, cot_ref,
    normed_ref, heads_ref, attended_ref, cot_out,
    local_sem, send_sems, recv_sems,
):
    at = pl.program_id(0)
    place = plane_position()
    rep, core, own, across, down, _ = place
    sender = Sender(send_sems, recv_sems)
    move = Gather(sender, cot_ref, cot_out, local_sem, place)

    @pl.when(at == 0)
    def _():
        meet([(rep, core, across), (rep, core, down), (rep, 1 - core, own)])
        move.begin()

    @pl.when(at == 2)
    def _():
        move.relay_first()

    @pl.when(at == 4)
    def _():
        move.relay_second()

    @pl.when(at == 6)
    def _():
        move.pass_corner()

    @pl.when(at == 7)
    def _():
        move.arrive()
        sender.finish()

    @pl.loop(0, x_ref.shape[1] // 32)
    def _(t):
        rows = pl.ds(pl.multiple_of(t * 32, 32), 32)
        x = x_ref[0, rows].astype(F32)
        normed_ref[0, rows] = (x * row_scale(x) * gain_ref[...]).astype(BF16)

    wide = dot_f32(normed_ref[0], w_ref[...])
    keys_at, values_at = GROUPS * HD, (GROUPS + 2) * HD
    pieces = [wide[:, :keys_at]]
    for at in (keys_at, values_at):
        pieces.append(jnp.where(core == 0, wide[:, at : at + HD], wide[:, at + HD : at + 2 * HD]))
    projected = jnp.concatenate(pieces, axis=1)
    heads = turn(projected, cos_ref, sin_ref, False).astype(BF16)
    heads_ref[0] = heads
    allowed = allowed_pairs(row_ref, col_ref)
    keys = heads[:, GROUPS * HD : (GROUPS + 1) * HD]
    values = heads[:, (GROUPS + 1) * HD :]
    parts = []
    for h in range(GROUPS):
        probs = head_probs(heads[:, h * HD : (h + 1) * HD], keys, allowed)
        parts.append(dot_f32(probs.astype(BF16), values))
    attended_ref[0] = jnp.concatenate(parts, axis=1).astype(BF16)


def attend(hidden, gain, qkv, tables, codes, cotangent, collective_id):
    members, length, width = hidden.shape
    wide, q_wide = (GROUPS + 2) * HD, GROUPS * HD

    def one(columns):
        return pl.BlockSpec((1, length, columns), lambda i: (i, 0, 0))

    def fixed(*shape):
        return pl.BlockSpec(shape, lambda i: (0,) * len(shape))

    return pl.pallas_call(
        attend_kernel,
        grid=(members,),
        out_shape=[
            jax.ShapeDtypeStruct((members, length, width), BF16),
            jax.ShapeDtypeStruct((members, length, wide), BF16),
            jax.ShapeDtypeStruct((members, length, q_wide), BF16),
            jax.ShapeDtypeStruct((8,) + cotangent.shape, BF16),
        ],
        in_specs=[
            one(width), fixed(1, width), fixed(*qkv.shape), fixed(length, wide),
            fixed(length, wide), pl.BlockSpec((1, 1, length), lambda i: (i, 0, 0)), one(1), VM,
        ],
        out_specs=[one(width), one(wide), one(q_wide), HBM],
        scratch_shapes=[
            pltpu.SemaphoreType.DMA,
            pltpu.SemaphoreType.DMA((13,)),
            pltpu.SemaphoreType.DMA((13,)),
        ],
        compiler_params=params(collective_id, 60),
        cost_estimate=link_cost(40),
    )(hidden, gain, qkv, *tables, codes[:, None, :], codes[:, :, None], cotangent)


def attend_back_kernel(
    out_grad_ref, w_ref, heads_ref, attended_ref, cos_ref, sin_ref, row_ref, col_ref,
    grad_ref, w_grad_ref, total,
):
    at = pl.program_id(0)
    out_grad = out_grad_ref[0]
    heads = heads_ref[0]
    attended_grad = lax.dot_general(
        out_grad, w_ref[...], (((1,), (1,)), ((), ())), preferred_element_type=F32
    ).astype(BF16)
    term = lax.dot_general(
        attended_ref[0], out_grad, (((0,), (0,)), ((), ())), preferred_element_type=F32
    )

    @pl.when(at == 0)
    def _():
        total[...] = term

    @pl.when(at > 0)
    def _():
        total[...] = total[...] + term

    @pl.when(at == pl.num_programs(0) - 1)
    def _():
        w_grad_ref[...] = total[...].astype(BF16)

    allowed = allowed_pairs(row_ref, col_ref)
    keys = heads[:, GROUPS * HD : (GROUPS + 1) * HD]
    values = heads[:, (GROUPS + 1) * HD :]
    grads = []
    key_grad, value_grad = None, None
    for h in range(GROUPS):
        lanes = slice(h * HD, (h + 1) * HD)
        query, head_grad = heads[:, lanes], attended_grad[:, lanes]
        probs = head_probs(query, keys, allowed)
        prob_grad = lax.dot_general(
            head_grad, values, (((1,), (1,)), ((), ())), preferred_element_type=F32
        )
        row_dot = jnp.sum(probs * prob_grad, axis=-1, keepdims=True)
        score_grad = (probs * (prob_grad - row_dot)).astype(BF16)
        grads.append(dot_f32(score_grad, keys) * SCORE_SCALE)
        key_part = lax.dot_general(
            score_grad, query, (((0,), (0,)), ((), ())), preferred_element_type=F32
        )
        value_part = lax.dot_general(
            probs.astype(BF16), head_grad, (((0,), (0,)), ((), ())), preferred_element_type=F32
        )
        key_grad = key_part if key_grad is None else key_grad + key_part
        value_grad = value_part if value_grad is None else value_grad + value_part
    grads += [key_grad * SCORE_SCALE, value_grad]
    grad_ref[0] = turn(jnp.concatenate(grads, axis=1), cos_ref, sin_ref, True).astype(BF16)


def attend_back(out_grad, out_rows, heads, attended, tables, codes):
    members, length, width = out_grad.shape
    wide, q_wide = heads.shape[2], attended.shape[2]

    def one(columns):
        return pl.BlockSpec((1, length, columns), lambda i: (i, 0, 0))

    def fixed(*shape):
        return pl.BlockSpec(shape, lambda i: (0,) * len(shape))

    return pl.pallas_call(
        attend_back_kernel,
        grid=(members,),
        out_shape=[
            jax.ShapeDtypeStruct((members, length, wide), BF16),
            jax.ShapeDtypeStruct((q_wide, width), BF16),
        ],
        in_specs=[
            one(width), fixed(q_wide, width), one(wide), one(q_wide), fixed(length, wide),
            fixed(length, wide), pl.BlockSpec((1, 1, length), lambda i: (i, 0, 0)), one(1),
        ],
        out_specs=[one(wide), fixed(q_wide, width)],
        scratch_shapes=[pltpu.VMEM((q_wide, width), F32)],
        compiler_params=pltpu.CompilerParams(vmem_limit_bytes=48 << 20),
        cost_estimate=link_cost(25),
    )(out_grad, out_rows, heads, attended, *tables, codes[:, None, :], codes[:, :, None])


def cast_rows_kernel(x_ref, out_ref):
    out_ref[...] = x_ref[0, 0].astype(F32)


def cast_rows(spread):
    reps, subs, rows, columns = spread.shape
    return pl.pallas_call(
        cast_rows_kernel,
        grid=(subs, reps),
        out_shape=jax.ShapeDtypeStruct((reps * subs * rows, columns), F32),
        in_specs=[pl.BlockSpec((1, 1, rows, columns), lambda s, r: (r, s, 0, 0))],
        out_specs=pl.BlockSpec((rows, columns), lambda s, r: (s * reps + r, 0)),
        cost_estimate=link_cost(8),
    )(spread)


def cast_columns_kernel(x_ref, out_ref):
    _, subs, owners, _, columns = x_ref.shape
    for j in range(owners):
        for s in range(subs):
            at = (j * subs + s) * columns
            out_ref[:, at : at + columns] = x_ref[0, s, j].astype(F32)


def cast_columns(handed, columns):
    parts, subs, owners, rows, _ = handed.shape
    wide = owners * subs * columns
    cuts = max(1, rows // 64)
    block = (1, subs, owners, rows // cuts, columns)
    return pl.pallas_call(
        cast_columns_kernel,
        grid=(parts, cuts),
        out_shape=jax.ShapeDtypeStruct((parts * rows, wide), F32),
        in_specs=[pl.BlockSpec(block, lambda r, h: (r, 0, 0, h, 0))],
        out_specs=pl.BlockSpec((rows // cuts, wide), lambda r, h: (r * cuts + h, 0)),
        compiler_params=pltpu.CompilerParams(vmem_limit_bytes=48 << 20),
        cost_estimate=link_cost(8),
    )(handed)


def cast_heads_kernel(q_ref, kv_ref, q_out, k_out, v_out):
    _, subs, owners, _, columns = q_ref.shape
    for j in range(owners):
        for s in range(subs):
            at = (j * subs + s) * columns
            q_out[:, at : at + columns] = q_ref[0, s, j].astype(F32)
        pair = [kv_ref[0, s, j].astype(F32) for s in range(subs)]
        wide = HD * subs
        at = j * wide
        k_out[:, at : at + wide] = jnp.concatenate([p[:, :HD] for p in pair], axis=1)
        v_out[:, at : at + wide] = jnp.concatenate([p[:, HD:] for p in pair], axis=1)


def cast_heads(handed, skip):
    parts, subs, owners, rows, _ = handed.shape
    q_wide, k_wide = GROUPS * HD, 2 * HD
    members = owners * subs

    def source(wide, at):
        return pl.BlockSpec((1, subs, owners, rows, wide), lambda r: (r, 0, 0, 0, at // wide))

    def shape(wide):
        return jax.ShapeDtypeStruct((parts * rows, wide), F32)

    widths = (members * q_wide, members * HD, members * HD)
    return pl.pallas_call(
        cast_heads_kernel,
        grid=(parts,),
        out_shape=[shape(w) for w in widths],
        in_specs=[source(q_wide, skip), source(k_wide, skip + q_wide)],
        out_specs=[pl.BlockSpec((rows, w), lambda r: (r, 0)) for w in widths],
        compiler_params=pltpu.CompilerParams(vmem_limit_bytes=48 << 20),
        cost_estimate=link_cost(5),
    )(handed, handed)


def tally_kernel(x_ref, out_ref, plane, planes, total, sems, plane_sems):
    rep, core, own, _, _, _ = plane_position()
    reps = planes.shape[0]
    mates = [(c, j) for c in range(2) for j in range(4)][1:]
    others = [(rep, (core + c) % 2, (own + j) % 4) for c, j in mates]
    above = [((rep + r) % reps, core, own) for r in range(1, reps)]
    meet(others + above)
    sender = Sender(sems.at[0], sems.at[1])
    for device in others:
        sender.send(x_ref, plane.at[core * 4 + own], device)
    plane[core * 4 + own] = x_ref[...]
    for copy in sender.copies:
        copy.wait_recv()
    mine = plane[0]
    for k in range(1, 8):
        mine = mine + plane[k]
    total[...] = mine
    climber = Sender(plane_sems.at[0], plane_sems.at[1])
    for device in above:
        climber.send(total, planes.at[rep], device)
    planes[rep] = mine
    for copy in climber.copies:
        copy.wait_recv()
    whole = planes[0]
    for k in range(1, reps):
        whole = whole + planes[k]
    out_ref[...] = whole
    sender.finish()
    climber.finish()


def tally_all(values, reps, collective_id):
    size = values.shape[0]
    rows = -(-size // 1024) * 8
    padded = jnp.pad(values, (0, rows * 128 - size)).reshape(rows, 128)
    block = pltpu.VMEM((rows, 128), F32)
    summed = pl.pallas_call(
        tally_kernel,
        out_shape=jax.ShapeDtypeStruct((rows, 128), F32),
        in_specs=[VM],
        out_specs=VM,
        scratch_shapes=[
            pltpu.VMEM((8, rows, 128), F32),
            pltpu.VMEM((reps, rows, 128), F32),
            block,
            pltpu.SemaphoreType.DMA((2, 7)),
            pltpu.SemaphoreType.DMA((2, reps - 1)),
        ],
        compiler_params=params(collective_id),
        cost_estimate=link_cost(10),
    )(padded)
    return summed.reshape(-1)[:size]


def column_blocks(weight, owners, subs):
    rows, columns = weight.shape
    blocked = weight.reshape(rows, owners, subs, columns // (owners * subs))
    mine = lax.dynamic_index_in_dim(blocked, lax.axis_index("sub"), axis=2, keepdims=False)
    return jnp.swapaxes(mine, 0, 1)


def regroup_columns(weights, owners, subs):
    blocks = jnp.concatenate([column_blocks(w, owners, subs) for w in weights], axis=-1)
    moved = lax.all_to_all(blocks, "fsdp", split_axis=0, concat_axis=0, tiled=True)
    return moved.reshape(-1, moved.shape[-1])


def row_block(weight, subs):
    rows = weight.shape[0] // subs
    return lax.dynamic_slice_in_dim(weight, lax.axis_index("sub") * rows, rows, axis=0)


def gather_tokens(block):
    return lax.all_gather(block, ("sub", "fsdp"), axis=0, tiled=True)


def scatter_tokens(partial):
    return lax.psum_scatter(partial, ("sub", "fsdp"), scatter_dimension=0, tiled=True)


def sum_planes(term):
    return lax.psum_scatter(term, "rep", scatter_dimension=0, tiled=True)


def spread_planes(piece):
    rep, subs = lax.axis_size("rep"), lax.axis_size("sub")
    spread = lax.all_gather(piece, ("rep", "sub"), axis=0, tiled=False)
    return spread.reshape((rep, subs) + piece.shape)


def owner_major(term):
    owners, rep = lax.axis_size("fsdp"), lax.axis_size("rep")
    rows, columns = term.shape
    blocked = jnp.swapaxes(term.reshape(owners, rep, rows // (owners * rep), columns), 0, 1)
    return blocked.reshape(rows, columns)


def to_owners(piece):
    blocked = piece.reshape(lax.axis_size("fsdp"), -1, piece.shape[1])
    return lax.all_to_all(blocked, "fsdp", split_axis=0, concat_axis=0, tiled=True)


def place_columns(spread):
    reps, subs, owners, rows, columns = spread.shape
    part = jnp.transpose(spread, (0, 3, 2, 1, 4))
    return part.reshape(reps * rows, owners * subs * columns).astype(F32)


def shards(
    kernels,
    hidden_in,
    segment_ids,
    valid_mask,
    cotangent,
    norm_attn,
    w_query,
    w_key,
    w_value,
    w_output,
    norm_mlp,
    w_gate,
    w_up,
    w_down,
):
    owners, subs, reps = lax.axis_size("fsdp"), lax.axis_size("sub"), lax.axis_size("rep")
    members = owners * subs
    length, width = hidden_in.shape[1:]
    tokens = members * length
    q_width, k_width = GROUPS * HD, HD

    def gathered(blocks, collective_id, jobs=()):
        if kernels:
            outs = list(gather_plane(blocks, collective_id, jobs, reps))
        else:
            outs = [gather_tokens(block) for block in blocks]
        return [o.reshape(tokens, -1) for o in outs[: len(blocks)]] + outs[len(blocks) :]

    def scattered(xs, w, turned, collective_id, jobs=()):
        if kernels:
            return product_scatter(xs, w, turned, collective_id, jobs, reps)
        x = jnp.concatenate(xs, axis=1)
        product = contract_cols(x, w) if turned else dot_f32(x, row_block(w, subs))
        return [scatter_tokens(product.astype(BF16)).astype(F32)]

    codes = segment_ids * 2 + valid_mask
    gains = jnp.stack([norm_attn, norm_mlp])
    result_grad = cotangent[0].astype(F32)
    mlp_out_low = (RESIDUAL_SCALE * result_grad).astype(BF16)
    if kernels:
        quarter = quarter_columns(w_gate, w_up, reps, 0)
        gate_up = lax.all_gather(quarter, "rep", axis=1, tiled=True).reshape(width, -1)
        hidden_tied = after(hidden_in[0], quarter)
        hidden_low, codes, gains, heads_all = start_plane(
            hidden_tied, codes, gains, w_query, w_key, w_value, 1
        )
        hidden_low = hidden_low.reshape(tokens, width)
        codes = codes.reshape(members, length)
        gains = jnp.swapaxes(gains, 0, 1).reshape(2, width)
        heads_all = heads_all.reshape(width, -1)
    else:
        gains = lax.all_gather(gains, "fsdp", axis=1, tiled=True)
        codes = gather_tokens(codes)
        hidden_low = gather_tokens(hidden_in[0])
        qkv = regroup_columns((w_query, w_key, w_value), owners, subs)
        gate_up = regroup_columns((w_gate, w_up), owners, subs)
    gain_attn = gains[0].astype(F32)
    gain_mlp = gains[1].astype(F32)
    ff = gate_up.shape[1] // 2

    if kernels:
        tables = turn_tables(length)
        normed_one, heads, attended, mlp_out_grad = attend(
            hidden_low.reshape(members, length, width), gain_attn[None], heads_all, tables, codes,
            mlp_out_low, 9,
        )
        normed_one = normed_one.reshape(tokens, width)
        mlp_out_grad = mlp_out_grad.reshape(tokens, width)
        attended = attended.reshape(tokens, q_width)
        heads_all = after(heads_all, normed_one)
        core_at = lax.axis_index("sub") * HD
        key_cols = lax.dynamic_slice_in_dim(heads_all, q_width + core_at, HD, axis=1)
        value_cols = lax.dynamic_slice_in_dim(heads_all, q_width + 2 * HD + core_at, HD, axis=1)
        qkv = jnp.concatenate([heads_all[:, :q_width], key_cols, value_cols], axis=1)
    else:
        cos_table, sin_table = rope_tables(length, HD)
        hidden_all = hidden_low.astype(F32)
        normed_one = (hidden_all * row_scale(hidden_all) * gain_attn).astype(BF16)
        projected = dot_f32(normed_one, qkv)
        cos_heads = cos_table[None, :, None, :]
        sin_heads = sin_table[None, :, None, :]
        per_seq = projected.reshape(members, length, GROUPS + 2, HD)
        queries = rotate(per_seq[:, :, :GROUPS], cos_heads, sin_heads).astype(BF16)
        keys = rotate(per_seq[:, :, GROUPS : GROUPS + 1], cos_heads, sin_heads).astype(BF16)[:, :, 0]
        values = per_seq[:, :, GROUPS + 1].astype(BF16)

        segments, validity = codes // 2, codes % 2
        row_index = jnp.arange(length, dtype=jnp.int32)[:, None]
        col_index = jnp.arange(length, dtype=jnp.int32)[None, :]
        allowed = (
            (segments[:, :, None] == segments[:, None, :])
            & (col_index <= row_index)
            & ((validity[:, None, :] == 1) | (col_index == row_index))
        )[:, None]
        scores = jnp.einsum("stgd,sud->sgtu", queries, keys, preferred_element_type=F32) * SCORE_SCALE
        scores = jnp.where(allowed, scores, MASKED_SCORE)
        shifted = jnp.exp(scores - jnp.max(scores, axis=-1, keepdims=True))
        probs = shifted / jnp.sum(shifted, axis=-1, keepdims=True)
        probs_low = probs.astype(BF16)
        attended = jnp.einsum("sgtu,sud->stgd", probs_low, values, preferred_element_type=F32)
        attended = attended.reshape(tokens, q_width).astype(BF16)
    (attn_branch,) = scattered([attended], w_output, False, 2)

    hidden = hidden_in[0].astype(F32)
    scale_one = row_scale(hidden)
    unit_one = hidden * scale_one
    middle = hidden + RESIDUAL_SCALE * attn_branch
    scale_two = row_scale(middle)
    unit_two = middle * scale_two
    normed_own = (unit_two * gain_mlp).astype(BF16)
    if kernels:
        normed_two, gate_up_proj, mixed_act, down_w_grad = mlp_plane(
            normed_own, gate_up, mlp_out_grad.reshape(members, length, width), 3
        )
        normed_two = normed_two.reshape(tokens, width)
    else:
        normed_two, mlp_out_grad = gathered([normed_own, mlp_out_low], 3)
        gate_up_proj = dot_f32(normed_two, gate_up)
    gate_proj, up_proj = gate_up_proj[:, :ff], gate_up_proj[:, ff:]
    sigma = jax.nn.sigmoid(gate_proj)
    silu_gate = gate_proj * sigma
    if not kernels:
        mixed_act = (silu_gate * up_proj).astype(BF16)
        down_w_grad = contract_rows(mixed_act, mlp_out_grad).astype(BF16)
    down_w_piece = sum_planes(down_w_grad)
    mixed_grad = contract_cols(after(mlp_out_grad, down_w_grad), row_block(w_down, subs))
    slope = sigma * (1.0 + gate_proj * (1.0 - sigma))
    gate_grad = (mixed_grad * up_proj * slope).astype(BF16)
    up_grad = (mixed_grad * silu_gate).astype(BF16)
    gate_w_grad = contract_rows(normed_two, gate_grad).astype(BF16)
    up_w_grad = contract_rows(normed_two, up_grad).astype(BF16)
    gate_sum = sum_planes(owner_major(gate_w_grad))
    gate_up_grad = [after(gate_grad, gate_w_grad, up_w_grad), up_grad]
    (normed_two_grad,) = scattered(gate_up_grad, gate_up, True, 4)
    gain_mlp_grad, middle_part = norm_backward(normed_two_grad, scale_two, unit_two, gain_mlp)
    middle_grad = result_grad + middle_part

    attn_out_low = (RESIDUAL_SCALE * middle_grad).astype(BF16)
    passed = [KeepJob(down_w_piece)] if kernels else []
    attn_out_grad, *passed = gathered([attn_out_low], 5, passed)
    down_spread = spread_planes(passed[0] if kernels else down_w_piece)
    if kernels:
        qkv_grad, output_w_grad = attend_back(
            attn_out_grad.reshape(members, length, width), row_block(w_output, subs), heads,
            attended.reshape(members, length, q_width), tables, codes,
        )
        qkv_grad = qkv_grad.reshape(tokens, q_width + 2 * k_width)
    else:
        attended_grad = contract_cols(attn_out_grad, row_block(w_output, subs)).astype(BF16)
        output_w_grad = contract_rows(attended, attn_out_grad).astype(BF16)
        heads_grad = attended_grad.reshape(members, length, GROUPS, HD)
        prob_grad = jnp.einsum("stgd,sud->sgtu", heads_grad, values, preferred_element_type=F32)
        row_dot = jnp.sum(probs * prob_grad, axis=-1, keepdims=True)
        score_grad = (probs * (prob_grad - row_dot)).astype(BF16)
        query_grad = (
            jnp.einsum("sgtu,sud->stgd", score_grad, keys, preferred_element_type=F32) * SCORE_SCALE
        )
        key_grad = (
            jnp.einsum("sgtu,stgd->sud", score_grad, queries, preferred_element_type=F32) * SCORE_SCALE
        )
        value_grad = jnp.einsum("sgtu,stgd->sud", probs_low, heads_grad, preferred_element_type=F32)
        qkv_grad = jnp.concatenate(
            [
                rotate(query_grad, cos_heads, -sin_heads),
                rotate(key_grad[:, :, None], cos_heads, -sin_heads),
                value_grad[:, :, None],
            ],
            axis=2,
        )
        qkv_grad = qkv_grad.reshape(tokens, q_width + 2 * k_width).astype(BF16)
    qkv_tied = after(qkv_grad, output_w_grad)
    gate_job = [KeepJob(gate_sum)] if kernels else []
    normed_one_grad, *gate_kept = scattered([qkv_tied], qkv, True, 6, gate_job)
    qkv_grad = after(qkv_grad, normed_one_grad)
    qkv_w_grad = contract_rows(normed_one, qkv_grad).astype(BF16)
    gain_attn_grad, hidden_part = norm_backward(normed_one_grad, scale_one, unit_one, gain_attn)
    input_grad = (middle_grad + hidden_part).astype(BF16)

    mixed_tied = after(mixed_act, normed_one_grad, qkv_w_grad, down_spread)
    last_jobs = []
    if kernels:
        up_job = SumJob(
            [up_w_grad, qkv_w_grad], 4, 4, reps,
            {1: range(4), 2: range(4, 8), 3: range(8, 12), 4: range(12, 17)},
        )
        output_job = SumJob([output_w_grad], 1, 2, reps, {4: range(3)})
        last_jobs = [up_job, output_job, ExchangeJob(gate_kept[0])]
        last_jobs += [HandJob(up_job, reps, 4), HandJob(output_job, reps, 2)]
    mlp_branch, *last = scattered([mixed_tied], w_down, False, 7, last_jobs)
    result = middle + RESIDUAL_SCALE * mlp_branch

    validity_own = valid_mask[0].astype(F32)[:, None]
    squares = [
        jnp.sum(tensor * tensor * validity_own)
        for tensor in (hidden, middle, result, attn_branch, mlp_branch)
    ]
    tally = jnp.concatenate(
        [gain_attn_grad, gain_mlp_grad, jnp.stack(squares + [jnp.sum(validity_own)])]
    )
    tally = tally_all(tally, reps, 8) if kernels else lax.psum(tally, ("rep", "sub", "fsdp"))
    part = width // owners
    start = lax.axis_index("fsdp") * part
    gain_attn_out = lax.dynamic_slice_in_dim(tally, start, part)
    gain_mlp_out = lax.dynamic_slice_in_dim(tally, width + start, part)
    statistics = jnp.sqrt(tally[2 * width : 2 * width + 5] / (tally[2 * width + 5] * width))

    if kernels:
        gate_piece, up_handed, output_handed = last
        gate_spread = spread_planes(gate_piece)
        down_out = cast_rows(down_spread)
        output_out = cast_rows(output_handed.reshape((2, 2) + output_handed.shape[3:]))
        gate_out, up_out = cast_columns(gate_spread, ff), cast_columns(up_handed, ff)
        query_out, key_out, value_out = cast_heads(up_handed, ff)
    else:
        down_out, output_out = (
            jnp.swapaxes(s, 0, 1).reshape(-1, width).astype(F32)
            for s in (down_spread, spread_planes(sum_planes(output_w_grad)))
        )
        gate_spread, up_spread, qkv_spread = (
            spread_planes(to_owners(g))
            for g in (
                gate_sum,
                sum_planes(owner_major(up_w_grad)),
                sum_planes(owner_major(qkv_w_grad)),
            )
        )
        gate_out, up_out = place_columns(gate_spread), place_columns(up_spread)
        query_out = place_columns(qkv_spread[..., :q_width])
        key_out = place_columns(qkv_spread[..., q_width : q_width + k_width])
        value_out = place_columns(qkv_spread[..., q_width + k_width :])
    return (
        result.astype(BF16)[None],
        input_grad[None],
        gain_attn_out,
        query_out,
        key_out,
        value_out,
        output_out,
        gain_mlp_out,
        gate_out,
        up_out,
        down_out,
        statistics,
    )


def solution(mesh):
    fsdp = mesh.shape["fsdp"]
    subs = max(1, KV // fsdp)
    rep = mesh.shape["dp"] // subs
    kernels = fsdp == 4 and subs == 2 and rep >= 3
    plane_mesh = Mesh(mesh.devices.reshape(rep, subs, fsdp), ("rep", "sub", "fsdp"))
    batch = ("rep", "sub", "fsdp")
    return jax.shard_map(
        functools.partial(shards, kernels),
        mesh=plane_mesh,
        in_specs=(
            P(batch, None, None),
            P(batch, None),
            P(batch, None),
            P(batch, None, None),
            P("fsdp"),
            P("fsdp", None),
            P("fsdp", None),
            P("fsdp", None),
            P("fsdp", None),
            P("fsdp"),
            P("fsdp", None),
            P("fsdp", None),
            P("fsdp", None),
        ),
        out_specs=(
            P(batch, None, None),
            P(batch, None, None),
            P("fsdp"),
            P("fsdp", None),
            P("fsdp", None),
            P("fsdp", None),
            P("fsdp", None),
            P("fsdp"),
            P("fsdp", None),
            P("fsdp", None),
            P("fsdp", None),
            P(),
        ),
        check_vma=False,
    )
```

```python
import functools

import jax
import jax.numpy as jnp
import numpy as np
from jax import lax
from jax.experimental import pallas as pl
from jax.experimental.pallas import tpu as pltpu
from jax.sharding import Mesh
from jax.sharding import PartitionSpec as P

H = 32
KV = 8
HD = 64
GROUPS = H // KV

EPSILON = 1e-05
RESIDUAL_SCALE = 0.22
SCORE_SCALE = 1.0 / 64.0
MASKED_SCORE = -1e30
ROPE_BASE = 10000000.0

BF16 = jnp.bfloat16
F32 = jnp.float32
MESH = pl.DeviceIdType.MESH
SCALE = 3_300_000
HBM = pl.BlockSpec(memory_space=pltpu.HBM)
VM = pl.BlockSpec(memory_space=pltpu.VMEM)


def rope_tables(length, head_size):
    half_size = head_size // 2
    frequency = ROPE_BASE ** (-(jnp.arange(half_size, dtype=F32) * 2.0 / head_size))
    angles = jnp.arange(length, dtype=F32)[:, None] * frequency[None, :]
    return (jnp.cos(angles), jnp.sin(angles))


def turn_tables(length):
    half = HD // 2
    frequency = (ROPE_BASE ** (-2.0 * np.arange(half) / HD)).astype(np.float32)
    angles = np.arange(length, dtype=np.float32)[:, None] * frequency[None, :]
    plain = np.zeros((length, HD))
    angles = np.concatenate([angles] * (2 * (GROUPS + 1)) + [plain], axis=1).astype(np.float64)
    return jnp.asarray(np.cos(angles), F32), jnp.asarray(np.sin(angles), F32)


def rotate(tensor, cos_table, sin_table):
    half_size = tensor.shape[-1] // 2
    front_half = tensor[..., :half_size]
    back_half = tensor[..., half_size:]
    return jnp.concatenate(
        [
            front_half * cos_table - back_half * sin_table,
            back_half * cos_table + front_half * sin_table,
        ],
        axis=-1,
    )


def dot_f32(left, right):
    return jnp.dot(left, right, preferred_element_type=F32)


def contract_rows(left, right):
    return jnp.einsum("sa,sb->ab", left, right, preferred_element_type=F32)


def contract_cols(left, right):
    return jnp.einsum("sb,ab->sa", left, right, preferred_element_type=F32)


def row_scale(source):
    return lax.rsqrt(jnp.mean(source * source, axis=-1, keepdims=True) + EPSILON)


def norm_backward(grad_norm, scale_row, unit_rows, gain):
    gain_grad = jnp.sum(grad_norm * unit_rows, axis=0)
    scaled = grad_norm * gain
    source_grad = scale_row * (
        scaled - unit_rows * jnp.mean(scaled * unit_rows, axis=-1, keepdims=True)
    )
    return (gain_grad, source_grad)


def after(value, *others):
    return lax.optimization_barrier((value,) + others)[0]


def plane_position():
    rep, core, own = lax.axis_index("rep"), lax.axis_index("sub"), lax.axis_index("fsdp")
    row, col = own // 2, own % 2
    across = row * 2 + (1 - col)
    down = (1 - row) * 2 + col
    corner = (1 - row) * 2 + (1 - col)
    return rep, core, own, across, down, corner


def meet(devices):
    barrier = pltpu.get_barrier_semaphore()
    for device in devices:
        pl.semaphore_signal(barrier, inc=1, device_id=device, device_id_type=MESH)
    pl.semaphore_wait(barrier, len(devices))


def params(collective_id, megabytes=16):
    return pltpu.CompilerParams(
        collective_id=collective_id, has_side_effects=True, vmem_limit_bytes=megabytes << 20
    )


def link_cost(microseconds, flops=0):
    return pl.CostEstimate(
        flops=0, bytes_accessed=int(microseconds * SCALE), transcendentals=0
    )


class Sender:
    def __init__(self, send_sems, recv_sems):
        self.send_sems, self.recv_sems, self.copies = send_sems, recv_sems, []

    def send(self, src, dst, device):
        copy = self.make(src, dst, device)
        copy.start()
        return copy

    def make(self, src, dst, device):
        index = len(self.copies)
        copy = pltpu.make_async_remote_copy(
            src_ref=src,
            dst_ref=dst,
            send_sem=self.send_sems.at[index],
            recv_sem=self.recv_sems.at[index],
            device_id=device,
            device_id_type=MESH,
        )
        self.copies.append(copy)
        return copy

    def finish(self):
        for copy in self.copies:
            copy.wait_send()


class Bounce:
    def __init__(self, src, dst, room, sems):
        self.fetch = pltpu.make_async_copy(src, room, sems.at[0])
        self.store = pltpu.make_async_copy(room, dst, sems.at[1])

    def start(self):
        self.fetch.start()

    def turn(self):
        self.fetch.wait()
        self.store.start()

    def wait(self):
        self.store.wait()


class Gather:
    def __init__(self, sender, x_ref, out_ref, local_sem, place):
        rep, core, own, across, down, corner = place
        to_across, to_down, to_core = (rep, core, across), (rep, core, down), (rep, 1 - core, own)
        half = x_ref.shape[0] // 2
        low, high, whole = pl.ds(0, half), pl.ds(half, half), pl.ds(0, 2 * half)
        base = core * 4

        def first(rows, device):
            return sender.make(x_ref.at[rows], out_ref.at[base + own, rows], device)

        def forward(block, rows, device):
            ref = out_ref.at[base + block, rows]
            return sender.make(ref, ref, device)

        self.across_low, self.down_high = first(low, to_across), first(high, to_down)
        self.across_high, self.down_low = first(high, to_across), first(low, to_down)
        self.corner_low = forward(across, low, to_down)
        self.corner_high = forward(down, high, to_across)
        self.swap_own = first(whole, to_core)
        self.swap_near = [
            forward(across, low, to_core),
            forward(down, high, to_core),
            forward(across, high, to_core),
            forward(down, low, to_core),
        ]
        self.swap_corner = [forward(corner, low, to_core), forward(corner, high, to_core)]
        self.mine = pltpu.make_async_copy(x_ref, out_ref.at[base + own], local_sem)

    def begin(self):
        for copy in (self.across_low, self.down_high, self.across_high, self.down_low):
            copy.start()
        self.swap_own.start()
        self.mine.start()

    def relay(self):
        self.relay_first()
        self.relay_second()

    def relay_first(self):
        self.across_low.wait_recv()
        self.corner_low.start()
        self.swap_near[0].start()
        self.down_high.wait_recv()
        self.corner_high.start()
        self.swap_near[1].start()

    def relay_second(self):
        self.across_high.wait_recv()
        self.swap_near[2].start()
        self.down_low.wait_recv()
        self.swap_near[3].start()

    def finish(self):
        self.pass_corner()
        self.arrive()

    def pass_corner(self):
        self.corner_low.wait_recv()
        self.swap_corner[0].start()
        self.corner_high.wait_recv()
        self.swap_corner[1].start()

    def arrive(self):
        for swap in [self.swap_own] + self.swap_near + self.swap_corner:
            swap.wait_recv()
        self.mine.wait()


class ExchangeJob:
    climbs = False
    corner = True

    def __init__(self, source):
        self.rows = source.shape[0] // 4
        shape = (self.rows, source.shape[1])
        self.arrays = [source]
        self.outs = [jax.ShapeDtypeStruct((4,) + shape, BF16)]
        self.scratch = [pltpu.SemaphoreType.DMA((3,))] * 2
        self.scratch += [pltpu.VMEM(shape, BF16), pltpu.SemaphoreType.DMA((2,))]

    def open(self, arrays, outs, scratch, place):
        self.source, self.out, self.place = arrays[0], outs[0], place
        own = place[2]
        self.sems = scratch[:2]
        self.keep = Bounce(self.part(own), self.out.at[own], scratch[2], scratch[3])

    def part(self, block):
        return self.source.at[pl.ds(pl.multiple_of(block * self.rows, 16), self.rows)]

    def stage(self, n):
        rep, core, own, across, down, corner = self.place
        if n == 0:
            self.keep.start()
            self.sender = Sender(*self.sems)
            for peer in (corner, across, down):
                self.sender.send(self.part(peer), self.out.at[own], (rep, core, peer))
        if n == 1:
            self.keep.turn()
        if n == 6:
            for copy in self.sender.copies:
                copy.wait()
            self.keep.wait()


class KeepJob:
    climbs = False
    corner = False

    def __init__(self, source):
        self.arrays = [source]
        self.outs = [jax.ShapeDtypeStruct(source.shape, BF16)]
        self.scratch = [pltpu.VMEM(source.shape, BF16), pltpu.SemaphoreType.DMA((2,))]

    def open(self, arrays, outs, scratch, place):
        self.keep = Bounce(arrays[0], outs[0], *scratch)

    def stage(self, n):
        if n == 0:
            self.keep.start()
        if n == 1:
            self.keep.turn()
        if n == 6:
            self.keep.wait()


def column_place(place, reps):
    rep, core, own = place[:3]
    up = (rep == 0, rep == reps - 1, (rep + 1, core, own), (rep - 1, core, own))
    down = (rep == reps - 1, rep == 0, (rep - 1, core, own), (rep + 1, core, own))
    return (up, down)


def skewed(rep, reps, count, act, i):
    for low in (True, False):
        near = 0 if low else 1

        @pl.when((rep * 2 < reps) == low)
        def _(near=near):
            if i < count:
                act(near, i)
            if i >= 1:
                act(1 - near, i - 1)


class SumJob:
    climbs = True

    def __init__(self, sources, blocks, cuts, reps, steps):
        self.blocks, self.cuts, self.reps, self.steps = blocks, cuts, reps, steps
        self.arrays = sources
        self.corner = blocks > 1
        rows = sources[0].shape[0]
        self.span = rows // blocks
        self.half = self.span // 2
        self.size = self.half // cuts
        self.widths = [source.shape[1] for source in sources]
        wide = sum(self.widths)
        self.shape = (2, blocks, self.half, wide)
        self.outs = []
        self.count = blocks * cuts
        sems = pltpu.SemaphoreType.DMA((2, self.count))
        self.scratch = [
            pltpu.VMEM(self.shape, BF16),
            pltpu.VMEM(self.shape, BF16),
            pltpu.VMEM(self.shape, BF16),
            pltpu.SemaphoreType.DMA((2, blocks, len(sources))),
        ] + [sems] * 5

    def open(self, arrays, outs, scratch, place):
        self.sources = arrays
        self.held, self.landed, self.fin, self.load_sems = scratch[:4]
        self.chain_sems, self.give_sems, self.keep_sems = scratch[4:6], scratch[6:8], scratch[8]
        self.rep, self.core, self.own = place[:3]
        self.ways = column_place(place, self.reps)
        for k in range(self.blocks):
            for way in range(2):
                for load in self.loads(way, k):
                    load.start()

    def block(self, k):
        return (self.own + k) % self.blocks

    def loads(self, way, k):
        copies = []
        at = 0
        for n, (source, width) in enumerate(zip(self.sources, self.widths)):
            start = pl.multiple_of(self.block(k) * self.span + way * self.half, 16)
            src = source.at[pl.ds(start, self.half)]
            dst = self.held.at[way, k, :, pl.ds(at, width)]
            copies.append(pltpu.make_async_copy(src, dst, self.load_sems.at[way, k, n]))
            at += width
        return copies

    def rows(self, i):
        return i // self.cuts, pl.ds(i % self.cuts * self.size, self.size)

    def chain(self, way, i):
        k, rows = self.rows(i)
        return pltpu.make_async_remote_copy(
            src_ref=self.held.at[way, k, rows],
            dst_ref=self.landed.at[way, k, rows],
            send_sem=self.chain_sems[0].at[way, i],
            recv_sem=self.chain_sems[1].at[way, i],
            device_id=self.ways[way][2],
            device_id_type=MESH,
        )

    def give(self, way, i):
        k, rows = self.rows(i)
        return pltpu.make_async_remote_copy(
            src_ref=self.held.at[way, k, rows],
            dst_ref=self.fin.at[way, self.own, rows],
            send_sem=self.give_sems[0].at[way, i],
            recv_sem=self.give_sems[1].at[way, i],
            device_id=(self.rep, self.core, self.block(k)),
            device_id_type=MESH,
        )

    def keep(self, way, i):
        k, rows = self.rows(i)
        own = self.own if self.blocks > 1 else 0
        src, dst = self.held.at[way, k, rows], self.fin.at[way, own, rows]
        return pltpu.make_async_copy(src, dst, self.keep_sems.at[way, i])

    def loaded(self, way, i):
        if i % self.cuts == 0:
            for load in self.loads(way, i // self.cuts):
                load.wait()

    def prime(self):
        for way in range(2):

            @pl.when(self.ways[way][0])
            def _(way=way):
                for i in range(self.count):
                    self.loaded(way, i)
                    self.chain(way, i).start()

    def add(self, way, i):
        first, last = self.ways[way][:2]
        k, rows = self.rows(i)

        @pl.when(jnp.logical_not(first))
        def _():
            self.loaded(way, i)
            self.chain(way, i).wait_recv()
            self.held[way, k, rows] = self.held[way, k, rows] + self.landed[way, k, rows]

            @pl.when(jnp.logical_not(last))
            def _():
                self.chain(way, i).start()

            @pl.when(last)
            def _():
                if k == 0:
                    self.keep(way, i).start()
                else:
                    self.give(way, i).start()

    def step(self, i):
        skewed(self.rep, self.reps, self.count, self.add, i)

    def stage(self, n):
        if n == 0:
            self.prime()
        if n in self.steps:
            for i in self.steps[n]:
                self.step(i)
        if n == 7:
            for way in range(2):
                last = self.ways[way][1]
                for i in range(self.count):

                    @pl.when(jnp.logical_not(last))
                    def _(way=way, i=i):
                        self.chain(way, i).wait_send()

                    @pl.when(last)
                    def _(way=way, i=i):
                        if i // self.cuts == 0:
                            self.keep(way, i).wait()
                        else:
                            self.give(way, i).wait()


class HandJob:
    climbs = True

    def __init__(self, sums, reps, cuts):
        self.sums, self.arrays = sums, []
        shape = sums.shape
        self.reps, self.cuts, self.size = reps, cuts, shape[2] // cuts
        self.count = shape[1] * cuts
        self.corner = False
        self.outs = [jax.ShapeDtypeStruct((2, 2) + shape[1:], BF16)]
        self.scratch = [pltpu.SemaphoreType.DMA((2, self.count))] * 5

    def open(self, arrays, outs, scratch, place):
        self.out = outs[0]
        self.hand_sems, self.side_sems, self.keep_sems = scratch[:2], scratch[2:4], scratch[4]
        self.rep, self.core, self.own = place[:3]
        self.ways = column_place(place, self.reps)

    def rows(self, j):
        return j // self.cuts, pl.ds(j % self.cuts * self.size, self.size)

    def place(self, way, j):
        block, rows = self.rows(j)
        return self.out.at[way, self.core, block, rows]

    def remote(self, src, way, j, sems, device):
        return pltpu.make_async_remote_copy(
            src_ref=src,
            dst_ref=self.place(way, j),
            send_sem=sems[0].at[way, j],
            recv_sem=sems[1].at[way, j],
            device_id=device,
            device_id_type=MESH,
        )

    def beside(self):
        return (self.rep, 1 - self.core, self.own)

    def begin(self):
        fin = self.sums.fin
        for j in range(self.count):
            for way in range(2):

                @pl.when(self.ways[way][1])
                def _(way=way, j=j):
                    block, rows = self.rows(j)
                    src = fin.at[way, block, rows]
                    self.remote(src, way, j, self.hand_sems, self.ways[way][3]).start()
                    self.remote(src, way, j, self.side_sems, self.beside()).start()
                    dst = self.place(way, j)
                    pltpu.make_async_copy(src, dst, self.keep_sems.at[way, j]).start()

    def hand(self, way, j):
        first, last = self.ways[way][:2]

        @pl.when(jnp.logical_not(last))
        def _():
            ref = self.place(way, j)
            hand = self.remote(ref, way, j, self.hand_sems, self.ways[way][3])
            hand.wait_recv()

            @pl.when(jnp.logical_not(first))
            def _():
                hand.start()

            self.remote(ref, way, j, self.side_sems, self.beside()).start()

    def pass_on(self):
        for j in range(self.count + 1):
            skewed(self.rep, self.reps, self.count, lambda w, i: self.hand(1 - w, i), j)

    def close(self):
        for j in range(self.count):
            for way in range(2):
                first, last = self.ways[way][:2]
                ref = self.place(way, j)
                self.remote(ref, way, j, self.side_sems, self.beside()).wait()

                @pl.when(jnp.logical_not(first))
                def _(way=way, j=j, ref=ref):
                    self.remote(ref, way, j, self.hand_sems, self.ways[way][3]).wait_send()

                @pl.when(last)
                def _(way=way, j=j, ref=ref):
                    pltpu.make_async_copy(ref, ref, self.keep_sems.at[way, j]).wait()

    def stage(self, n):
        if n == 7:
            self.begin()
        if n == 8:
            self.pass_on()
        if n == 9:
            self.close()


class Jobs:
    def __init__(self, jobs, reps):
        self.jobs, self.reps = jobs, reps
        self.arrays = [a for job in jobs for a in job.arrays]
        self.out_shapes = [o for job in jobs for o in job.outs]
        self.scratch = [x for job in jobs for x in job.scratch]

    def greet(self, place):
        rep, core, own, across, down, corner = place
        devices = [(rep, core, across), (rep, core, down), (rep, 1 - core, own)]
        if any(job.climbs for job in self.jobs):
            devices += [((rep + 1) % self.reps, core, own)]
            devices += [((rep + self.reps - 1) % self.reps, core, own)]
        if any(job.corner for job in self.jobs):
            devices.append((rep, core, corner))
        meet(devices)

    def open(self, arrays, outs, scratch, place):
        arrays, outs, scratch = list(arrays), list(outs), list(scratch)

        def take(refs, count):
            taken = refs[:count]
            del refs[:count]
            return taken

        for job in self.jobs:
            mine = [take(arrays, len(job.arrays)), take(outs, len(job.outs))]
            job.open(*mine, take(scratch, len(job.scratch)), place)

    def stage(self, n):
        for job in self.jobs:
            job.stage(n)


def gather_kernel(count, jobs, *refs):
    arrays, outs = len(jobs.arrays), len(jobs.out_shapes)
    xs, job_arrays = refs[:count], refs[count : count + arrays]
    refs = refs[count + arrays :]
    x_outs, job_outs = refs[:count], refs[count : count + outs]
    refs = refs[count + outs :]
    local_sems, send_sems, recv_sems = refs[:3]
    place = plane_position()
    jobs.greet(place)
    sender = Sender(send_sems, recv_sems)
    moves = [
        Gather(sender, x, out, local_sems.at[i], place)
        for i, (x, out) in enumerate(zip(xs, x_outs))
    ]
    for move in moves:
        move.begin()
    jobs.open(job_arrays, job_outs, refs[3:], place)
    jobs.stage(0)
    jobs.stage(1)
    for move in moves:
        move.relay()
    jobs.stage(5)
    for move in moves:
        move.finish()
    sender.finish()
    for n in (6, 7, 8, 9):
        jobs.stage(n)


def gather_plane(blocks, collective_id, jobs=(), reps=1):
    count = len(blocks)
    jobs = Jobs(jobs, reps)
    return pl.pallas_call(
        functools.partial(gather_kernel, count, jobs),
        out_shape=[jax.ShapeDtypeStruct((8,) + x.shape, x.dtype) for x in blocks]
        + jobs.out_shapes,
        in_specs=[VM] * count + [HBM] * len(jobs.arrays),
        out_specs=[HBM] * (count + len(jobs.out_shapes)),
        scratch_shapes=[
            pltpu.SemaphoreType.DMA((count,)),
            pltpu.SemaphoreType.DMA((13 * count,)),
            pltpu.SemaphoreType.DMA((13 * count,)),
        ]
        + jobs.scratch,
        compiler_params=params(collective_id, 60),
        cost_estimate=link_cost(40 * count),
    )(*blocks, *jobs.arrays)


def column_source(ref, rows, block, width):
    return ref.at[rows, pl.ds(pl.multiple_of(block * width, width), width)]


def quarter_kernel(gate_ref, up_ref, out_ref, room, local_sems, send_sems, recv_sems):
    rep, core, own, across, down, corner = plane_position()
    peers = (corner, across, down)
    meet([(rep, core, peer) for peer in peers])
    rows = out_ref.shape[1]
    width = out_ref.shape[2] // 2
    mine = pl.ds(pl.multiple_of(rep * rows, rows), rows)
    sender = Sender(send_sems, recv_sems)
    local = []
    for k, ref in enumerate((gate_ref, up_ref)):
        columns = pl.ds(k * width, width)
        target = out_ref.at[own, :, columns]
        source = column_source(ref, mine, own * 2 + core, width)
        copy = Bounce(source, target, room.at[:, columns], local_sems.at[k])
        copy.start()
        local.append(copy)
        for peer in peers:
            source = column_source(ref, mine, peer * 2 + core, width)
            sender.send(source, target, (rep, core, peer))
    for copy in local:
        copy.turn()
    for copy in sender.copies:
        copy.wait_recv()
    sender.finish()
    for copy in local:
        copy.wait()


def quarter_columns(w_gate, w_up, reps, collective_id):
    rows, columns = w_gate.shape
    shape = (rows // reps, columns // 4)
    return pl.pallas_call(
        quarter_kernel,
        out_shape=jax.ShapeDtypeStruct((4,) + shape, BF16),
        in_specs=[HBM] * 2,
        out_specs=HBM,
        scratch_shapes=[
            pltpu.VMEM(shape, BF16),
            pltpu.SemaphoreType.DMA((2, 2)),
            pltpu.SemaphoreType.DMA((6,)),
            pltpu.SemaphoreType.DMA((6,)),
        ],
        compiler_params=params(collective_id, 60),
        cost_estimate=link_cost(25),
    )(w_gate, w_up)


def start_kernel(
    x_ref, code_ref, gain_ref, q_ref, k_ref, v_ref, x_out, code_out, gain_out, heads_out,
    room, bounce_sems, local_sems, send_sems, recv_sems,
):
    place = plane_position()
    rep, core, own, across, down, corner = place
    peers = (corner, across, down)
    others = [(rep, core, peer) for peer in peers] + [(rep, 1 - core, peer) for peer in peers]
    others.append((rep, 1 - core, own))
    meet(others)
    sender = Sender(send_sems, recv_sems)
    move = Gather(sender, x_ref, x_out, local_sems.at[0], place)
    direct = [sender.make(gain_ref, gain_out.at[own], (rep, core, peer)) for peer in peers]
    slot = code_out.at[core * 4 + own]
    direct += [sender.make(code_ref, slot, device) for device in others]
    whole = pl.ds(0, q_ref.shape[0])
    q_wide, pair = GROUPS * HD, 2 * HD

    def fetch(ref, at, width, blocks):
        columns = pl.ds(at, width)
        target = heads_out.at[own, :, columns]
        source = column_source(ref, whole, blocks[0], width)
        bounced = Bounce(source, target, room.at[:, columns], bounce_sems.at[min(at, 1)])
        sends = []
        for block, peer in zip(blocks[1:], peers):
            source = column_source(ref, whole, block, width)
            sends.append(sender.make(source, target, (rep, core, peer)))
        return bounced, sends

    def swap(at):
        columns = pl.ds(at, pair)
        copies = [sender.make(room.at[:, columns], heads_out.at[own, :, columns], others[-1])]
        for peer in peers:
            ref = heads_out.at[peer, :, columns]
            copies.append(sender.make(ref, ref, others[-1]))
        return copies

    q_kept, q_sends = fetch(q_ref, 0, q_wide, [block * 2 + core for block in (own,) + peers])
    direct += q_sends
    first = len(sender.copies)
    sides = []
    for ref, at in ((k_ref, q_wide), (v_ref, q_wide + pair)):
        kept, sends = fetch(ref, at, pair, (own,) + peers)
        swaps = swap(at)
        del sender.copies[first + len(sends) :]
        sides.append((kept, sends, swaps, swap(2 * q_wide + pair - at)))
        del sender.copies[first:]
    local = [
        pltpu.make_async_copy(gain_ref, gain_out.at[own], local_sems.at[1]),
        pltpu.make_async_copy(code_ref, slot, local_sems.at[2]),
    ]
    move.begin()
    for copy in direct + local + [q_kept]:
        copy.start()
    for side, (kept, sends, swaps, _) in enumerate(sides):

        @pl.when(core == side)
        def _(kept=kept, sends=sends, swaps=swaps):
            for copy in [kept] + sends:
                copy.start()
            kept.turn()
            swaps[0].start()

    q_kept.turn()
    move.relay()
    for side, (kept, sends, swaps, _) in enumerate(sides):

        @pl.when(core == side)
        def _(kept=kept, sends=sends, swaps=swaps):
            for copy, passed in zip(sends, swaps[1:]):
                copy.wait_recv()
                passed.start()

    move.finish()
    for copy in direct:
        copy.wait_recv()
    for side, (kept, sends, swaps, arrivals) in enumerate(sides):

        @pl.when(core == side)
        def _(kept=kept, sends=sends, swaps=swaps, arrivals=arrivals):
            for copy in arrivals:
                copy.wait_recv()
            for copy in sends + swaps:
                copy.wait_send()
            kept.wait()

    sender.finish()
    for copy in local + [q_kept]:
        copy.wait()


def start_plane(hidden, codes, gains, w_query, w_key, w_value, collective_id):
    heads = (w_query.shape[0], (GROUPS + 4) * HD)
    shapes = [
        ((8,) + hidden.shape, BF16),
        ((8,) + codes.shape, jnp.int32),
        ((4,) + gains.shape, BF16),
        ((4,) + heads, BF16),
    ]
    return pl.pallas_call(
        start_kernel,
        out_shape=[jax.ShapeDtypeStruct(s, d) for s, d in shapes],
        in_specs=[VM] * 3 + [HBM] * 3,
        out_specs=[HBM] * 4,
        scratch_shapes=[
            pltpu.VMEM(heads, BF16),
            pltpu.SemaphoreType.DMA((2, 2)),
            pltpu.SemaphoreType.DMA((3,)),
            pltpu.SemaphoreType.DMA((40,)),
            pltpu.SemaphoreType.DMA((40,)),
        ],
        compiler_params=params(collective_id, 60),
        cost_estimate=link_cost(60),
    )(hidden, codes, gains, w_query, w_key, w_value)


def mlp_kernel(
    x_ref, w_hbm, grad_hbm, x_out, product_out, act_out, down_out,
    x_all, w_ref, product, act, grad, total, down,
    w_sems, grad_sems, store_sems, down_sems, local_sem, send_sems, recv_sems,
):
    place = plane_position()
    rep, core, own, across, down_at, corner = place
    rows = x_ref.shape[0]
    ff = act.shape[2]
    tile, depth = 512, 256
    tiles = ff // tile
    here, there = core * 4, (1 - core) * 4
    order = [here + own, there + own, here + across, here + down_at]
    order += [there + across, there + down_at, here + corner, there + corner]
    loads = []
    for t in range(tiles):
        for k in range(2):
            columns = pl.ds(k * ff + t * tile, tile)
            load = pltpu.make_async_copy(w_hbm.at[:, columns], w_ref.at[:, columns], w_sems.at[t, k])
            load.start()
            loads.append(load)
    grads = [
        pltpu.make_async_copy(grad_hbm.at[block], grad.at[n % 2], grad_sems.at[n])
        for n, block in enumerate(order)
    ]
    grads[0].start()
    grads[1].start()
    meet([(rep, core, across), (rep, core, down_at), (rep, 1 - core, own)])
    sender = Sender(send_sems, recv_sems)
    move = Gather(sender, x_ref, x_all, local_sem, place)
    move.begin()
    pending, finals = [], []

    def piece(x, slot, at):
        gate = dot_f32(x, w_ref[:, pl.ds(at, tile)])
        up = dot_f32(x, w_ref[:, pl.ds(ff + at, tile)])
        product[slot, :, pl.ds(at, tile)] = gate
        product[slot, :, pl.ds(ff + at, tile)] = up
        act[slot, :, pl.ds(at, tile)] = (gate * jax.nn.sigmoid(gate) * up).astype(BF16)

    def compute(n):
        block, slot = order[n], n % 2
        if n >= 2:
            for store in pending[n - 2][:2]:
                store.wait()
        for t in range(tiles):
            if n == 0:
                loads[2 * t].wait()
                loads[2 * t + 1].wait()
            piece(x_all[block], slot, t * tile)
        mine = pl.ds(pl.multiple_of(block * rows, rows), rows)
        stores = [
            pltpu.make_async_copy(product.at[slot], product_out.at[mine], store_sems.at[n, 0]),
            pltpu.make_async_copy(act.at[slot], act_out.at[mine], store_sems.at[n, 1]),
            pltpu.make_async_copy(x_all.at[block], x_out.at[block], store_sems.at[n, 2]),
        ]
        for store in stores:
            store.start()
        pending.append(stores)

    def weigh(n):
        slot = n % 2
        grads[n].wait()

        def term(at):
            return lax.dot_general(
                act[slot, :, pl.ds(at, depth)], grad[slot], (((0,), (0,)), ((), ())),
                preferred_element_type=F32,
            )

        if n == 7:
            for r in range(ff // depth):
                at = pl.ds(r * depth, depth)
                down[at] = (total[at] + term(r * depth)).astype(BF16)
                final = pltpu.make_async_copy(down.at[at], down_out.at[at], down_sems.at[r])
                final.start()
                finals.append(final)
        else:

            @pl.loop(0, ff // depth)
            def _(r):
                start = pl.multiple_of(r * depth, depth)
                at = pl.ds(start, depth)
                total[at] = term(start) if n == 0 else total[at] + term(start)

        if n + 2 < 8:
            grads[n + 2].start()

    move.mine.wait()
    compute(0)
    move.swap_own.wait_recv()
    compute(1)
    move.relay_first()
    weigh(0)
    weigh(1)
    move.relay_second()
    compute(2)
    compute(3)
    for swap in move.swap_near:
        swap.wait_recv()
    weigh(2)
    compute(4)
    move.pass_corner()
    weigh(3)
    compute(5)
    weigh(4)
    compute(6)
    weigh(5)
    for swap in move.swap_corner:
        swap.wait_recv()
    compute(7)
    weigh(6)
    weigh(7)
    for k, stores in enumerate(pending):
        for store in stores if k >= 6 else stores[2:]:
            store.wait()
    for final in finals:
        final.wait()
    sender.finish()


def mlp_plane(x, w, grad, collective_id):
    rows, width = x.shape
    wide = w.shape[1]
    ff = wide // 2
    return pl.pallas_call(
        mlp_kernel,
        out_shape=[
            jax.ShapeDtypeStruct((8, rows, width), BF16),
            jax.ShapeDtypeStruct((8 * rows, wide), F32),
            jax.ShapeDtypeStruct((8 * rows, ff), BF16),
            jax.ShapeDtypeStruct((ff, width), BF16),
        ],
        in_specs=[VM, HBM, HBM],
        out_specs=[HBM] * 4,
        scratch_shapes=[
            pltpu.VMEM((8, rows, width), BF16),
            pltpu.VMEM((width, wide), BF16),
            pltpu.VMEM((2, rows, wide), F32),
            pltpu.VMEM((2, rows, ff), BF16),
            pltpu.VMEM((2, rows, width), BF16),
            pltpu.VMEM((ff, width), F32),
            pltpu.VMEM((ff, width), BF16),
            pltpu.SemaphoreType.DMA((ff // 512, 2)),
            pltpu.SemaphoreType.DMA((8,)),
            pltpu.SemaphoreType.DMA((8, 3)),
            pltpu.SemaphoreType.DMA((ff // 256,)),
            pltpu.SemaphoreType.DMA,
            pltpu.SemaphoreType.DMA((13,)),
            pltpu.SemaphoreType.DMA((13,)),
        ],
        compiler_params=params(collective_id, 60),
        cost_estimate=link_cost(50),
    )(x, w, grad)


def product_scatter_kernel(turned, count, jobs, *refs):
    arrays, outs = len(jobs.arrays), len(jobs.out_shapes)
    x_hbm, w_hbm, job_arrays = refs[:count], refs[count], refs[count + 1 : count + 1 + arrays]
    refs = refs[count + 1 + arrays :]
    out_ref, job_outs = refs[0], refs[1 : 1 + outs]
    refs = refs[1 + outs :]
    x_refs, w_ref = refs[:count], refs[count]
    (
        swap, held, from_core, from_across, from_down, last_across, last_down,
        x_sems, w_sems, core_send, core_recv, send_sems, recv_sems,
    ) = refs[count + 1 : count + 14]
    place = plane_position()
    rep, core, own, across, down, corner = place
    to_across, to_down, to_core = (rep, core, across), (rep, core, down), (rep, 1 - core, own)
    _, rows, wide = held.shape
    depth = x_refs[0].shape[1]
    tile = 512
    tiles = wide // tile
    half = rows // 2
    low, high = pl.ds(0, half), pl.ds(half, half)
    order = []
    for block in (corner, across, down, own):
        order += [(1 - core) * 4 + block, core * 4 + block]

    def rows_of(block):
        return pl.ds(pl.multiple_of(block * rows, rows), rows)

    x_loads = [
        [
            pltpu.make_async_copy(
                x_hbm[i].at[rows_of(block)], x_refs[i].at[rows_of(block)], x_sems.at[i, n]
            )
            for i in range(count)
        ]
        for n, block in enumerate(order)
    ]
    w_loads = []
    for t in range(tiles):
        columns = pl.ds(t * tile, tile)
        if turned:
            src, dst = w_hbm.at[columns], w_ref.at[columns]
        else:
            kept = pl.ds(pl.multiple_of(core * depth, depth), depth)
            src, dst = w_hbm.at[kept, columns], w_ref.at[:, columns]
        w_loads.append(pltpu.make_async_copy(src, dst, w_sems.at[t]))
    for load in x_loads[0]:
        load.start()
    for load in w_loads:
        load.start()
    for loads in x_loads[1:]:
        for load in loads:
            load.start()
    jobs.open(job_arrays, job_outs, refs[count + 14 :], place)
    jobs.greet(place)
    jobs.stage(0)

    def product(dst, mine, columns):
        total = None
        for i in range(count):
            x = x_refs[i][mine, :]
            if turned:
                w = w_ref[columns, pl.ds(i * depth, depth)]
                part = lax.dot_general(
                    x, w, (((1,), (1,)), ((), ())), preferred_element_type=F32
                )
            else:
                part = dot_f32(x, w_ref[:, columns])
            total = part if total is None else total + part
        dst[:, columns] = total.astype(BF16)

    def fill(dst, n):
        for load in x_loads[n]:
            load.wait()
        mine = rows_of(order[n])
        if n == 0:
            for t in range(tiles):
                w_loads[t].wait()
                product(dst, mine, pl.ds(t * tile, tile))
        else:

            @pl.loop(0, tiles)
            def _(t):
                product(dst, mine, pl.ds(pl.multiple_of(t * tile, tile), tile))

    swaps = Sender(core_send, core_recv)
    sender = Sender(send_sems, recv_sems)
    sent = {}
    for k in range(4):
        fill(swap.at[k], 2 * k)
        swaps.send(swap.at[k], from_core.at[k], to_core)
        fill(held.at[k], 2 * k + 1)
        swaps.copies[k].wait_recv()
        held[k] = held[k] + from_core[k]
        if k == 0:
            sent[0] = sender.send(held.at[0, low], from_across.at[0], to_across)
            sent[1] = sender.send(held.at[0, high], from_down.at[0], to_down)
        if k == 1:
            sent[2] = sender.send(held.at[1, low], from_across.at[1], to_across)
        if k == 2:
            sent[3] = sender.send(held.at[2, high], from_down.at[1], to_down)
        jobs.stage(1 + k)
    sent[0].wait_recv()
    held[2, low] = held[2, low] + from_across[0]
    to_last = sender.send(held.at[2, low], last_down, to_down)
    sent[1].wait_recv()
    held[1, high] = held[1, high] + from_down[0]
    across_last = sender.send(held.at[1, high], last_across, to_across)
    jobs.stage(5)
    sent[2].wait_recv()
    sent[3].wait_recv()
    to_last.wait_recv()
    out_ref[low] = (
        held[3, low].astype(F32) + from_across[1].astype(F32) + last_down[...].astype(F32)
    )
    across_last.wait_recv()
    out_ref[high] = (
        held[3, high].astype(F32) + from_down[1].astype(F32) + last_across[...].astype(F32)
    )
    swaps.finish()
    sender.finish()
    for n in (6, 7, 8, 9):
        jobs.stage(n)


def product_scatter(xs, w, turned, collective_id, jobs=(), reps=1):
    count = len(xs)
    jobs = Jobs(jobs, reps)
    tokens, depth = xs[0].shape
    rows = tokens // 8
    wide = w.shape[0] if turned else w.shape[1]
    half = rows // 2
    return pl.pallas_call(
        functools.partial(product_scatter_kernel, turned, count, jobs),
        out_shape=[jax.ShapeDtypeStruct((rows, wide), F32)] + jobs.out_shapes,
        in_specs=[HBM] * (count + 1 + len(jobs.arrays)),
        out_specs=[VM] + [HBM] * len(jobs.out_shapes),
        scratch_shapes=[pltpu.VMEM((tokens, depth), BF16)] * count
        + [
            pltpu.VMEM((wide, depth * count) if turned else (depth, wide), BF16),
            pltpu.VMEM((4, rows, wide), BF16),
            pltpu.VMEM((4, rows, wide), BF16),
            pltpu.VMEM((4, rows, wide), BF16),
            pltpu.VMEM((2, half, wide), BF16),
            pltpu.VMEM((2, half, wide), BF16),
            pltpu.VMEM((half, wide), BF16),
            pltpu.VMEM((half, wide), BF16),
            pltpu.SemaphoreType.DMA((count, 8)),
            pltpu.SemaphoreType.DMA((wide // 512,)),
            pltpu.SemaphoreType.DMA((4,)),
            pltpu.SemaphoreType.DMA((4,)),
            pltpu.SemaphoreType.DMA((6,)),
            pltpu.SemaphoreType.DMA((6,)),
        ]
        + jobs.scratch,
        compiler_params=params(collective_id, 60),
        cost_estimate=link_cost(44, 2 * tokens * depth * count * wide),
    )(*xs, w, *jobs.arrays)


def turn(value, cos_ref, sin_ref, back):
    wide = value.shape[1]
    lanes = lax.broadcasted_iota(jnp.int32, value.shape, 1)
    front = lax.rem(lanes, HD) < HD // 2
    ahead = pltpu.roll(value, wide - HD // 2, 1)
    behind = pltpu.roll(value, HD // 2, 1)
    swapped = jnp.where(front, -ahead, behind) * sin_ref[...]
    turned = value * cos_ref[...]
    return turned - swapped if back else turned + swapped


def allowed_pairs(row_ref, col_ref):
    keys, queries = row_ref[...], col_ref[...]
    length = keys.shape[1]
    row_index = lax.broadcasted_iota(jnp.int32, (length, length), 0)
    col_index = lax.broadcasted_iota(jnp.int32, (length, length), 1)
    same = lax.shift_right_logical(keys, 1) == lax.shift_right_logical(queries, 1)
    valid = jnp.bitwise_and(keys, 1) == 1
    return same & (col_index <= row_index) & (valid | (col_index == row_index))


def head_probs(query, keys, allowed):
    scores = lax.dot_general(
        query, keys, (((1,), (1,)), ((), ())), preferred_element_type=F32
    )
    scores = jnp.where(allowed, scores * SCORE_SCALE, MASKED_SCORE)
    shifted = jnp.exp(scores - jnp.max(scores, axis=-1, keepdims=True))
    return shifted / jnp.sum(shifted, axis=-1, keepdims=True)


def attend_kernel(
    x_hbm, gain_ref, w_ref, cos_ref, sin_ref, row_ref, col_ref, cot_ref, out_w_hbm,
    out_ref, normed_hbm, heads_hbm, attended_hbm, cot_out,
    x_buf, normed, heads_buf, attended, out_w, parts, from_core, from_across, from_down,
    last_across, last_down, x_sems, w_sem, store_sems, local_sem,
    core_send, core_recv, send_sems, recv_sems, cot_send, cot_recv,
):
    place = plane_position()
    rep, core, own, across, down, corner = place
    row, col = own // 2, own % 2
    to_across, to_down, to_core = (rep, core, across), (rep, core, down), (rep, 1 - core, own)
    length, wide = out_ref.shape
    half = length // 2
    low, high = pl.ds(0, half), pl.ds(half, half)
    depth = out_w.shape[0]
    tile = 512

    def block_of(n):
        k = n // 2
        far_row = row + (k + 1) % 2 * (1 - 2 * row)
        far_col = col + (1 - k // 2) * (1 - 2 * col)
        near = n % 2
        return (near * core + (1 - near) * (1 - core)) * 4 + far_row * 2 + far_col

    def fetch(n):
        slot = n % 2
        return pltpu.make_async_copy(x_hbm.at[block_of(n)], x_buf.at[slot], x_sems.at[slot])

    def stores(n):
        slot, block = n % 2, block_of(n)
        pairs = ((normed, normed_hbm), (heads_buf, heads_hbm), (attended, attended_hbm))
        return [
            pltpu.make_async_copy(src.at[slot], dst.at[block], store_sems.at[slot, i])
            for i, (src, dst) in enumerate(pairs)
        ]

    def swap(k):
        return pltpu.make_async_remote_copy(
            src_ref=parts.at[0, k],
            dst_ref=from_core.at[k],
            send_sem=core_send.at[k],
            recv_sem=core_recv.at[k],
            device_id=to_core,
            device_id_type=MESH,
        )

    rows_kept = pl.ds(pl.multiple_of(core * depth, depth), depth)
    out_w_load = pltpu.make_async_copy(out_w_hbm.at[rows_kept], out_w, w_sem)
    out_w_load.start()
    fetch(0).start()
    meet([to_across, to_down, to_core])
    cot_sender = Sender(cot_send, cot_recv)
    move = Gather(cot_sender, cot_ref, cot_out, local_sem, place)
    move.begin()
    sender = Sender(send_sems, recv_sems)
    sent = [
        sender.make(parts.at[1, 0, low], from_across.at[0], to_across),
        sender.make(parts.at[1, 0, high], from_down.at[0], to_down),
        sender.make(parts.at[1, 1, low], from_across.at[1], to_across),
        sender.make(parts.at[1, 2, high], from_down.at[1], to_down),
        sender.make(parts.at[1, 2, low], last_down, to_down),
        sender.make(parts.at[1, 1, high], last_across, to_across),
    ]
    out_w_load.wait()

    @pl.loop(0, 8)
    def _(n):
        slot, k = n % 2, n // 2
        block = block_of(n)
        fetch(n).wait()

        @pl.when(n < 7)
        def _():
            fetch(n + 1).start()

        @pl.when(n >= 2)
        def _():
            for store in stores(n - 2):
                store.wait()

        @pl.when(n == 3)
        def _():
            move.relay_first()

        @pl.when(n == 5)
        def _():
            move.relay_second()

        @pl.loop(0, length // 32)
        def _(t):
            rows = pl.ds(pl.multiple_of(t * 32, 32), 32)
            x = x_buf[slot, rows].astype(F32)
            normed[slot, rows] = (x * row_scale(x) * gain_ref[...]).astype(BF16)

        projected = dot_f32(normed[slot], w_ref[...])
        keys_at, values_at = GROUPS * HD, (GROUPS + 2) * HD
        pieces = [projected[:, :keys_at]]
        for at in (keys_at, values_at):
            mine, other = projected[:, at : at + HD], projected[:, at + HD : at + 2 * HD]
            pieces.append(jnp.where(core == 0, mine, other))
        heads = turn(jnp.concatenate(pieces, axis=1), cos_ref, sin_ref, False).astype(BF16)
        heads_buf[slot] = heads
        allowed = allowed_pairs(row_ref.at[block], col_ref.at[block])
        keys = heads[:, GROUPS * HD : (GROUPS + 1) * HD]
        values = heads[:, (GROUPS + 1) * HD :]
        outs = []
        for h in range(GROUPS):
            probs = head_probs(heads[:, h * HD : (h + 1) * HD], keys, allowed)
            outs.append(dot_f32(probs.astype(BF16), values))
        attended[slot] = jnp.concatenate(outs, axis=1).astype(BF16)
        for store in stores(n):
            store.start()

        @pl.loop(0, wide // tile)
        def _(t):
            columns = pl.ds(pl.multiple_of(t * tile, tile), tile)
            parts[slot, k, :, columns] = dot_f32(attended[slot], out_w[:, columns]).astype(BF16)

        @pl.when(slot == 0)
        def _():
            swap(k).start()

        @pl.when(slot == 1)
        def _():
            swap(k).wait_recv()
            parts[1, k] = parts[1, k] + from_core[k]

        @pl.when(n == 1)
        def _():
            sent[0].start()
            sent[1].start()

        @pl.when(n == 3)
        def _():
            sent[2].start()

        @pl.when(n == 5)
        def _():
            sent[3].start()

    sent[0].wait_recv()
    parts[1, 2, low] = parts[1, 2, low] + from_across[0]
    sent[4].start()
    sent[1].wait_recv()
    parts[1, 1, high] = parts[1, 1, high] + from_down[0]
    sent[5].start()
    move.pass_corner()
    sent[2].wait_recv()
    sent[3].wait_recv()
    sent[4].wait_recv()
    out_ref[low] = (
        parts[1, 3, low].astype(F32) + from_across[1].astype(F32) + last_down[...].astype(F32)
    )
    sent[5].wait_recv()
    out_ref[high] = (
        parts[1, 3, high].astype(F32) + from_down[1].astype(F32) + last_across[...].astype(F32)
    )
    move.arrive()
    cot_sender.finish()
    for k in range(4):
        swap(k).wait_send()
    sender.finish()
    for n in (6, 7):
        for store in stores(n):
            store.wait()


def attend(hidden, gain, qkv, tables, codes, cotangent, w_output, collective_id):
    members, length, width = hidden.shape
    wide, q_wide = (GROUPS + 2) * HD, GROUPS * HD
    half = length // 2
    three = [(length, width), (length, wide), (length, q_wide)]
    return pl.pallas_call(
        attend_kernel,
        out_shape=[jax.ShapeDtypeStruct((length, width), F32)]
        + [jax.ShapeDtypeStruct((members,) + shape, BF16) for shape in three]
        + [jax.ShapeDtypeStruct((8,) + cotangent.shape, BF16)],
        in_specs=[HBM] + [VM] * 7 + [HBM],
        out_specs=[VM] + [HBM] * 4,
        scratch_shapes=[pltpu.VMEM((2, length, width), BF16)]
        + [pltpu.VMEM((2,) + shape, BF16) for shape in three]
        + [
            pltpu.VMEM((q_wide, width), BF16),
            pltpu.VMEM((2, 4, length, width), BF16),
            pltpu.VMEM((4, length, width), BF16),
            pltpu.VMEM((2, half, width), BF16),
            pltpu.VMEM((2, half, width), BF16),
            pltpu.VMEM((half, width), BF16),
            pltpu.VMEM((half, width), BF16),
            pltpu.SemaphoreType.DMA((2,)),
            pltpu.SemaphoreType.DMA,
            pltpu.SemaphoreType.DMA((2, 3)),
            pltpu.SemaphoreType.DMA,
            pltpu.SemaphoreType.DMA((4,)),
            pltpu.SemaphoreType.DMA((4,)),
            pltpu.SemaphoreType.DMA((6,)),
            pltpu.SemaphoreType.DMA((6,)),
            pltpu.SemaphoreType.DMA((13,)),
            pltpu.SemaphoreType.DMA((13,)),
        ],
        compiler_params=params(collective_id, 60),
        cost_estimate=link_cost(70),
    )(
        hidden, gain, qkv, *tables, codes[:, None, :], codes[:, :, None], cotangent, w_output
    )


def attend_back_kernel(
    out_grad_ref, w_ref, heads_ref, attended_ref, cos_ref, sin_ref, row_ref, col_ref,
    grad_ref, w_grad_ref, total,
):
    at = pl.program_id(0)
    out_grad = out_grad_ref[0]
    heads = heads_ref[0]
    attended_grad = lax.dot_general(
        out_grad, w_ref[...], (((1,), (1,)), ((), ())), preferred_element_type=F32
    ).astype(BF16)
    term = lax.dot_general(
        attended_ref[0], out_grad, (((0,), (0,)), ((), ())), preferred_element_type=F32
    )

    @pl.when(at == 0)
    def _():
        total[...] = term

    @pl.when(at > 0)
    def _():
        total[...] = total[...] + term

    @pl.when(at == pl.num_programs(0) - 1)
    def _():
        w_grad_ref[...] = total[...].astype(BF16)

    allowed = allowed_pairs(row_ref.at[0], col_ref.at[0])
    keys = heads[:, GROUPS * HD : (GROUPS + 1) * HD]
    values = heads[:, (GROUPS + 1) * HD :]
    grads = []
    key_grad, value_grad = None, None
    for h in range(GROUPS):
        lanes = slice(h * HD, (h + 1) * HD)
        query, head_grad = heads[:, lanes], attended_grad[:, lanes]
        probs = head_probs(query, keys, allowed)
        prob_grad = lax.dot_general(
            head_grad, values, (((1,), (1,)), ((), ())), preferred_element_type=F32
        )
        row_dot = jnp.sum(probs * prob_grad, axis=-1, keepdims=True)
        score_grad = (probs * (prob_grad - row_dot)).astype(BF16)
        grads.append(dot_f32(score_grad, keys) * SCORE_SCALE)
        key_part = lax.dot_general(
            score_grad, query, (((0,), (0,)), ((), ())), preferred_element_type=F32
        )
        value_part = lax.dot_general(
            probs.astype(BF16), head_grad, (((0,), (0,)), ((), ())), preferred_element_type=F32
        )
        key_grad = key_part if key_grad is None else key_grad + key_part
        value_grad = value_part if value_grad is None else value_grad + value_part
    grads += [key_grad * SCORE_SCALE, value_grad]
    grad_ref[0] = turn(jnp.concatenate(grads, axis=1), cos_ref, sin_ref, True).astype(BF16)


def attend_back(out_grad, out_rows, heads, attended, tables, codes):
    members, length, width = out_grad.shape
    wide, q_wide = heads.shape[2], attended.shape[2]

    def one(columns):
        return pl.BlockSpec((1, length, columns), lambda i: (i, 0, 0))

    def fixed(*shape):
        return pl.BlockSpec(shape, lambda i: (0,) * len(shape))

    return pl.pallas_call(
        attend_back_kernel,
        grid=(members,),
        out_shape=[
            jax.ShapeDtypeStruct((members, length, wide), BF16),
            jax.ShapeDtypeStruct((q_wide, width), BF16),
        ],
        in_specs=[
            one(width), fixed(q_wide, width), one(wide), one(q_wide), fixed(length, wide),
            fixed(length, wide), pl.BlockSpec((1, 1, length), lambda i: (i, 0, 0)), one(1),
        ],
        out_specs=[one(wide), fixed(q_wide, width)],
        scratch_shapes=[pltpu.VMEM((q_wide, width), F32)],
        compiler_params=pltpu.CompilerParams(vmem_limit_bytes=48 << 20),
        cost_estimate=link_cost(25),
    )(out_grad, out_rows, heads, attended, *tables, codes[:, None, :], codes[:, :, None])


def cast_rows_kernel(x_ref, out_ref):
    out_ref[...] = x_ref[0, 0].astype(F32)


def cast_rows(spread):
    reps, subs, rows, columns = spread.shape
    return pl.pallas_call(
        cast_rows_kernel,
        grid=(subs, reps),
        out_shape=jax.ShapeDtypeStruct((reps * subs * rows, columns), F32),
        in_specs=[pl.BlockSpec((1, 1, rows, columns), lambda s, r: (r, s, 0, 0))],
        out_specs=pl.BlockSpec((rows, columns), lambda s, r: (s * reps + r, 0)),
        cost_estimate=link_cost(8),
    )(spread)


def cast_columns_kernel(x_ref, out_ref):
    _, subs, owners, _, columns = x_ref.shape
    for j in range(owners):
        for s in range(subs):
            at = (j * subs + s) * columns
            out_ref[:, at : at + columns] = x_ref[0, s, j].astype(F32)


def cast_columns(handed, columns):
    parts, subs, owners, rows, _ = handed.shape
    wide = owners * subs * columns
    cuts = max(1, rows // 64)
    block = (1, subs, owners, rows // cuts, columns)
    return pl.pallas_call(
        cast_columns_kernel,
        grid=(parts, cuts),
        out_shape=jax.ShapeDtypeStruct((parts * rows, wide), F32),
        in_specs=[pl.BlockSpec(block, lambda r, h: (r, 0, 0, h, 0))],
        out_specs=pl.BlockSpec((rows // cuts, wide), lambda r, h: (r * cuts + h, 0)),
        compiler_params=pltpu.CompilerParams(vmem_limit_bytes=48 << 20),
        cost_estimate=link_cost(8),
    )(handed)


def cast_heads_kernel(q_ref, kv_ref, q_out, k_out, v_out):
    _, subs, owners, _, columns = q_ref.shape
    for j in range(owners):
        for s in range(subs):
            at = (j * subs + s) * columns
            q_out[:, at : at + columns] = q_ref[0, s, j].astype(F32)
        pair = [kv_ref[0, s, j].astype(F32) for s in range(subs)]
        wide = HD * subs
        at = j * wide
        k_out[:, at : at + wide] = jnp.concatenate([p[:, :HD] for p in pair], axis=1)
        v_out[:, at : at + wide] = jnp.concatenate([p[:, HD:] for p in pair], axis=1)


def cast_heads(handed, skip):
    parts, subs, owners, rows, _ = handed.shape
    q_wide, k_wide = GROUPS * HD, 2 * HD
    members = owners * subs

    def source(wide, at):
        return pl.BlockSpec((1, subs, owners, rows, wide), lambda r: (r, 0, 0, 0, at // wide))

    def shape(wide):
        return jax.ShapeDtypeStruct((parts * rows, wide), F32)

    widths = (members * q_wide, members * HD, members * HD)
    return pl.pallas_call(
        cast_heads_kernel,
        grid=(parts,),
        out_shape=[shape(w) for w in widths],
        in_specs=[source(q_wide, skip), source(k_wide, skip + q_wide)],
        out_specs=[pl.BlockSpec((rows, w), lambda r: (r, 0)) for w in widths],
        compiler_params=pltpu.CompilerParams(vmem_limit_bytes=48 << 20),
        cost_estimate=link_cost(5),
    )(handed, handed)


def tally_kernel(x_ref, out_ref, plane, planes, total, sems, plane_sems):
    rep, core, own, _, _, _ = plane_position()
    reps = planes.shape[0]
    mates = [(c, j) for c in range(2) for j in range(4)][1:]
    others = [(rep, (core + c) % 2, (own + j) % 4) for c, j in mates]
    above = [((rep + r) % reps, core, own) for r in range(1, reps)]
    meet(others + above)
    sender = Sender(sems.at[0], sems.at[1])
    for device in others:
        sender.send(x_ref, plane.at[core * 4 + own], device)
    plane[core * 4 + own] = x_ref[...]
    for copy in sender.copies:
        copy.wait_recv()
    mine = plane[0]
    for k in range(1, 8):
        mine = mine + plane[k]
    total[...] = mine
    climber = Sender(plane_sems.at[0], plane_sems.at[1])
    for device in above:
        climber.send(total, planes.at[rep], device)
    planes[rep] = mine
    for copy in climber.copies:
        copy.wait_recv()
    whole = planes[0]
    for k in range(1, reps):
        whole = whole + planes[k]
    out_ref[...] = whole
    sender.finish()
    climber.finish()


def tally_all(values, reps, collective_id):
    size = values.shape[0]
    rows = -(-size // 1024) * 8
    padded = jnp.pad(values, (0, rows * 128 - size)).reshape(rows, 128)
    block = pltpu.VMEM((rows, 128), F32)
    summed = pl.pallas_call(
        tally_kernel,
        out_shape=jax.ShapeDtypeStruct((rows, 128), F32),
        in_specs=[VM],
        out_specs=VM,
        scratch_shapes=[
            pltpu.VMEM((8, rows, 128), F32),
            pltpu.VMEM((reps, rows, 128), F32),
            block,
            pltpu.SemaphoreType.DMA((2, 7)),
            pltpu.SemaphoreType.DMA((2, reps - 1)),
        ],
        compiler_params=params(collective_id),
        cost_estimate=link_cost(10),
    )(padded)
    return summed.reshape(-1)[:size]


def column_blocks(weight, owners, subs):
    rows, columns = weight.shape
    blocked = weight.reshape(rows, owners, subs, columns // (owners * subs))
    mine = lax.dynamic_index_in_dim(blocked, lax.axis_index("sub"), axis=2, keepdims=False)
    return jnp.swapaxes(mine, 0, 1)


def regroup_columns(weights, owners, subs):
    blocks = jnp.concatenate([column_blocks(w, owners, subs) for w in weights], axis=-1)
    moved = lax.all_to_all(blocks, "fsdp", split_axis=0, concat_axis=0, tiled=True)
    return moved.reshape(-1, moved.shape[-1])


def row_block(weight, subs):
    rows = weight.shape[0] // subs
    return lax.dynamic_slice_in_dim(weight, lax.axis_index("sub") * rows, rows, axis=0)


def gather_tokens(block):
    return lax.all_gather(block, ("sub", "fsdp"), axis=0, tiled=True)


def scatter_tokens(partial):
    return lax.psum_scatter(partial, ("sub", "fsdp"), scatter_dimension=0, tiled=True)


def sum_planes(term):
    return lax.psum_scatter(term, "rep", scatter_dimension=0, tiled=True)


def spread_planes(piece):
    rep, subs = lax.axis_size("rep"), lax.axis_size("sub")
    spread = lax.all_gather(piece, ("rep", "sub"), axis=0, tiled=False)
    return spread.reshape((rep, subs) + piece.shape)


def owner_major(term):
    owners, rep = lax.axis_size("fsdp"), lax.axis_size("rep")
    rows, columns = term.shape
    blocked = jnp.swapaxes(term.reshape(owners, rep, rows // (owners * rep), columns), 0, 1)
    return blocked.reshape(rows, columns)


def to_owners(piece):
    blocked = piece.reshape(lax.axis_size("fsdp"), -1, piece.shape[1])
    return lax.all_to_all(blocked, "fsdp", split_axis=0, concat_axis=0, tiled=True)


def place_columns(spread):
    reps, subs, owners, rows, columns = spread.shape
    part = jnp.transpose(spread, (0, 3, 2, 1, 4))
    return part.reshape(reps * rows, owners * subs * columns).astype(F32)


def shards(
    kernels,
    hidden_in,
    segment_ids,
    valid_mask,
    cotangent,
    norm_attn,
    w_query,
    w_key,
    w_value,
    w_output,
    norm_mlp,
    w_gate,
    w_up,
    w_down,
):
    owners, subs, reps = lax.axis_size("fsdp"), lax.axis_size("sub"), lax.axis_size("rep")
    members = owners * subs
    length, width = hidden_in.shape[1:]
    tokens = members * length
    q_width, k_width = GROUPS * HD, HD

    def gathered(blocks, collective_id, jobs=()):
        if kernels:
            outs = list(gather_plane(blocks, collective_id, jobs, reps))
        else:
            outs = [gather_tokens(block) for block in blocks]
        return [o.reshape(tokens, -1) for o in outs[: len(blocks)]] + outs[len(blocks) :]

    def scattered(xs, w, turned, collective_id, jobs=()):
        if kernels:
            return product_scatter(xs, w, turned, collective_id, jobs, reps)
        x = jnp.concatenate(xs, axis=1)
        product = contract_cols(x, w) if turned else dot_f32(x, row_block(w, subs))
        return [scatter_tokens(product.astype(BF16)).astype(F32)]

    codes = segment_ids * 2 + valid_mask
    gains = jnp.stack([norm_attn, norm_mlp])
    result_grad = cotangent[0].astype(F32)
    mlp_out_low = (RESIDUAL_SCALE * result_grad).astype(BF16)
    if kernels:
        quarter = quarter_columns(w_gate, w_up, reps, 0)
        gate_up = lax.all_gather(quarter, "rep", axis=1, tiled=True).reshape(width, -1)
        hidden_tied = after(hidden_in[0], quarter)
        hidden_low, codes, gains, heads_all = start_plane(
            hidden_tied, codes, gains, w_query, w_key, w_value, 1
        )
        hidden_low = hidden_low.reshape(tokens, width)
        codes = codes.reshape(members, length)
        gains = jnp.swapaxes(gains, 0, 1).reshape(2, width)
        heads_all = heads_all.reshape(width, -1)
    else:
        gains = lax.all_gather(gains, "fsdp", axis=1, tiled=True)
        codes = gather_tokens(codes)
        hidden_low = gather_tokens(hidden_in[0])
        qkv = regroup_columns((w_query, w_key, w_value), owners, subs)
        gate_up = regroup_columns((w_gate, w_up), owners, subs)
    gain_attn = gains[0].astype(F32)
    gain_mlp = gains[1].astype(F32)
    ff = gate_up.shape[1] // 2

    if kernels:
        tables = turn_tables(length)
        attn_branch, normed_one, heads, attended, mlp_out_grad = attend(
            hidden_low.reshape(members, length, width), gain_attn[None], heads_all, tables, codes,
            mlp_out_low, w_output, 9,
        )
        normed_one = normed_one.reshape(tokens, width)
        mlp_out_grad = mlp_out_grad.reshape(tokens, width)
        attended = attended.reshape(tokens, q_width)
        heads_all = after(heads_all, normed_one)
        core_at = lax.axis_index("sub") * HD
        key_cols = lax.dynamic_slice_in_dim(heads_all, q_width + core_at, HD, axis=1)
        value_cols = lax.dynamic_slice_in_dim(heads_all, q_width + 2 * HD + core_at, HD, axis=1)
        qkv = jnp.concatenate([heads_all[:, :q_width], key_cols, value_cols], axis=1)
    else:
        cos_table, sin_table = rope_tables(length, HD)
        hidden_all = hidden_low.astype(F32)
        normed_one = (hidden_all * row_scale(hidden_all) * gain_attn).astype(BF16)
        projected = dot_f32(normed_one, qkv)
        cos_heads = cos_table[None, :, None, :]
        sin_heads = sin_table[None, :, None, :]
        per_seq = projected.reshape(members, length, GROUPS + 2, HD)
        queries = rotate(per_seq[:, :, :GROUPS], cos_heads, sin_heads).astype(BF16)
        keys = rotate(per_seq[:, :, GROUPS : GROUPS + 1], cos_heads, sin_heads).astype(BF16)[:, :, 0]
        values = per_seq[:, :, GROUPS + 1].astype(BF16)

        segments, validity = codes // 2, codes % 2
        row_index = jnp.arange(length, dtype=jnp.int32)[:, None]
        col_index = jnp.arange(length, dtype=jnp.int32)[None, :]
        allowed = (
            (segments[:, :, None] == segments[:, None, :])
            & (col_index <= row_index)
            & ((validity[:, None, :] == 1) | (col_index == row_index))
        )[:, None]
        scores = jnp.einsum("stgd,sud->sgtu", queries, keys, preferred_element_type=F32) * SCORE_SCALE
        scores = jnp.where(allowed, scores, MASKED_SCORE)
        shifted = jnp.exp(scores - jnp.max(scores, axis=-1, keepdims=True))
        probs = shifted / jnp.sum(shifted, axis=-1, keepdims=True)
        probs_low = probs.astype(BF16)
        attended = jnp.einsum("sgtu,sud->stgd", probs_low, values, preferred_element_type=F32)
        attended = attended.reshape(tokens, q_width).astype(BF16)
    if not kernels:
        (attn_branch,) = scattered([attended], w_output, False, 2)

    hidden = hidden_in[0].astype(F32)
    scale_one = row_scale(hidden)
    unit_one = hidden * scale_one
    middle = hidden + RESIDUAL_SCALE * attn_branch
    scale_two = row_scale(middle)
    unit_two = middle * scale_two
    normed_own = (unit_two * gain_mlp).astype(BF16)
    if kernels:
        normed_two, gate_up_proj, mixed_act, down_w_grad = mlp_plane(
            normed_own, gate_up, mlp_out_grad.reshape(members, length, width), 3
        )
        normed_two = normed_two.reshape(tokens, width)
    else:
        normed_two, mlp_out_grad = gathered([normed_own, mlp_out_low], 3)
        gate_up_proj = dot_f32(normed_two, gate_up)
    gate_proj, up_proj = gate_up_proj[:, :ff], gate_up_proj[:, ff:]
    sigma = jax.nn.sigmoid(gate_proj)
    silu_gate = gate_proj * sigma
    if not kernels:
        mixed_act = (silu_gate * up_proj).astype(BF16)
        down_w_grad = contract_rows(mixed_act, mlp_out_grad).astype(BF16)
    down_w_piece = sum_planes(down_w_grad)
    mixed_grad = contract_cols(after(mlp_out_grad, down_w_grad), row_block(w_down, subs))
    slope = sigma * (1.0 + gate_proj * (1.0 - sigma))
    gate_grad = (mixed_grad * up_proj * slope).astype(BF16)
    up_grad = (mixed_grad * silu_gate).astype(BF16)
    gate_w_grad = contract_rows(normed_two, gate_grad).astype(BF16)
    up_w_grad = contract_rows(normed_two, up_grad).astype(BF16)
    gate_sum = sum_planes(owner_major(gate_w_grad))
    gate_up_grad = [after(gate_grad, gate_w_grad, up_w_grad), up_grad]
    (normed_two_grad,) = scattered(gate_up_grad, gate_up, True, 4)
    gain_mlp_grad, middle_part = norm_backward(normed_two_grad, scale_two, unit_two, gain_mlp)
    middle_grad = result_grad + middle_part

    attn_out_low = (RESIDUAL_SCALE * middle_grad).astype(BF16)
    passed = [KeepJob(down_w_piece)] if kernels else []
    attn_out_grad, *passed = gathered([attn_out_low], 5, passed)
    down_spread = spread_planes(passed[0] if kernels else down_w_piece)
    if kernels:
        qkv_grad, output_w_grad = attend_back(
            attn_out_grad.reshape(members, length, width), row_block(w_output, subs), heads,
            attended.reshape(members, length, q_width), tables, codes,
        )
        qkv_grad = qkv_grad.reshape(tokens, q_width + 2 * k_width)
    else:
        attended_grad = contract_cols(attn_out_grad, row_block(w_output, subs)).astype(BF16)
        output_w_grad = contract_rows(attended, attn_out_grad).astype(BF16)
        heads_grad = attended_grad.reshape(members, length, GROUPS, HD)
        prob_grad = jnp.einsum("stgd,sud->sgtu", heads_grad, values, preferred_element_type=F32)
        row_dot = jnp.sum(probs * prob_grad, axis=-1, keepdims=True)
        score_grad = (probs * (prob_grad - row_dot)).astype(BF16)
        query_grad = (
            jnp.einsum("sgtu,sud->stgd", score_grad, keys, preferred_element_type=F32) * SCORE_SCALE
        )
        key_grad = (
            jnp.einsum("sgtu,stgd->sud", score_grad, queries, preferred_element_type=F32) * SCORE_SCALE
        )
        value_grad = jnp.einsum("sgtu,stgd->sud", probs_low, heads_grad, preferred_element_type=F32)
        qkv_grad = jnp.concatenate(
            [
                rotate(query_grad, cos_heads, -sin_heads),
                rotate(key_grad[:, :, None], cos_heads, -sin_heads),
                value_grad[:, :, None],
            ],
            axis=2,
        )
        qkv_grad = qkv_grad.reshape(tokens, q_width + 2 * k_width).astype(BF16)
    qkv_tied = after(qkv_grad, output_w_grad)
    gate_job = [KeepJob(gate_sum)] if kernels else []
    normed_one_grad, *gate_kept = scattered([qkv_tied], qkv, True, 6, gate_job)
    qkv_grad = after(qkv_grad, normed_one_grad)
    qkv_w_grad = contract_rows(normed_one, qkv_grad).astype(BF16)
    gain_attn_grad, hidden_part = norm_backward(normed_one_grad, scale_one, unit_one, gain_attn)
    input_grad = (middle_grad + hidden_part).astype(BF16)

    mixed_tied = after(mixed_act, normed_one_grad, qkv_w_grad, down_spread)
    last_jobs = []
    if kernels:
        up_job = SumJob(
            [up_w_grad, qkv_w_grad], 4, 4, reps,
            {1: range(4), 2: range(4, 8), 3: range(8, 12), 4: range(12, 17)},
        )
        output_job = SumJob([output_w_grad], 1, 2, reps, {4: range(3)})
        last_jobs = [up_job, output_job, ExchangeJob(gate_kept[0])]
        last_jobs += [HandJob(up_job, reps, 4), HandJob(output_job, reps, 2)]
    mlp_branch, *last = scattered([mixed_tied], w_down, False, 7, last_jobs)
    result = middle + RESIDUAL_SCALE * mlp_branch

    validity_own = valid_mask[0].astype(F32)[:, None]
    squares = [
        jnp.sum(tensor * tensor * validity_own)
        for tensor in (hidden, middle, result, attn_branch, mlp_branch)
    ]
    tally = jnp.concatenate(
        [gain_attn_grad, gain_mlp_grad, jnp.stack(squares + [jnp.sum(validity_own)])]
    )
    tally = tally_all(tally, reps, 8) if kernels else lax.psum(tally, ("rep", "sub", "fsdp"))
    part = width // owners
    start = lax.axis_index("fsdp") * part
    gain_attn_out = lax.dynamic_slice_in_dim(tally, start, part)
    gain_mlp_out = lax.dynamic_slice_in_dim(tally, width + start, part)
    statistics = jnp.sqrt(tally[2 * width : 2 * width + 5] / (tally[2 * width + 5] * width))

    if kernels:
        gate_piece, up_handed, output_handed = last
        gate_spread = spread_planes(gate_piece)
        down_out = cast_rows(down_spread)
        output_out = cast_rows(output_handed.reshape((2, 2) + output_handed.shape[3:]))
        gate_out, up_out = cast_columns(gate_spread, ff), cast_columns(up_handed, ff)
        query_out, key_out, value_out = cast_heads(up_handed, ff)
    else:
        down_out, output_out = (
            jnp.swapaxes(s, 0, 1).reshape(-1, width).astype(F32)
            for s in (down_spread, spread_planes(sum_planes(output_w_grad)))
        )
        gate_spread, up_spread, qkv_spread = (
            spread_planes(to_owners(g))
            for g in (
                gate_sum,
                sum_planes(owner_major(up_w_grad)),
                sum_planes(owner_major(qkv_w_grad)),
            )
        )
        gate_out, up_out = place_columns(gate_spread), place_columns(up_spread)
        query_out = place_columns(qkv_spread[..., :q_width])
        key_out = place_columns(qkv_spread[..., q_width : q_width + k_width])
        value_out = place_columns(qkv_spread[..., q_width + k_width :])
    return (
        result.astype(BF16)[None],
        input_grad[None],
        gain_attn_out,
        query_out,
        key_out,
        value_out,
        output_out,
        gain_mlp_out,
        gate_out,
        up_out,
        down_out,
        statistics,
    )


def solution(mesh):
    fsdp = mesh.shape["fsdp"]
    subs = max(1, KV // fsdp)
    rep = mesh.shape["dp"] // subs
    kernels = fsdp == 4 and subs == 2 and rep >= 3
    plane_mesh = Mesh(mesh.devices.reshape(rep, subs, fsdp), ("rep", "sub", "fsdp"))
    batch = ("rep", "sub", "fsdp")
    return jax.shard_map(
        functools.partial(shards, kernels),
        mesh=plane_mesh,
        in_specs=(
            P(batch, None, None),
            P(batch, None),
            P(batch, None),
            P(batch, None, None),
            P("fsdp"),
            P("fsdp", None),
            P("fsdp", None),
            P("fsdp", None),
            P("fsdp", None),
            P("fsdp"),
            P("fsdp", None),
            P("fsdp", None),
            P("fsdp", None),
        ),
        out_specs=(
            P(batch, None, None),
            P(batch, None, None),
            P("fsdp"),
            P("fsdp", None),
            P("fsdp", None),
            P("fsdp", None),
            P("fsdp", None),
            P("fsdp"),
            P("fsdp", None),
            P("fsdp", None),
            P("fsdp", None),
            P(),
        ),
        check_vma=False,
    )
```

```python
import functools

import jax
import jax.numpy as jnp
import numpy as np
from jax import lax
from jax.experimental import pallas as pl
from jax.experimental.pallas import tpu as pltpu
from jax.sharding import Mesh
from jax.sharding import PartitionSpec as P

H = 32
KV = 8
HD = 64
GROUPS = H // KV

EPSILON = 1e-05
RESIDUAL_SCALE = 0.22
SCORE_SCALE = 1.0 / 64.0
MASKED_SCORE = -1e30
ROPE_BASE = 10000000.0

BF16 = jnp.bfloat16
F32 = jnp.float32
MESH = pl.DeviceIdType.MESH
SCALE = 3_300_000
HBM = pl.BlockSpec(memory_space=pltpu.HBM)
VM = pl.BlockSpec(memory_space=pltpu.VMEM)


def rope_tables(length, head_size):
    half_size = head_size // 2
    frequency = ROPE_BASE ** (-(jnp.arange(half_size, dtype=F32) * 2.0 / head_size))
    angles = jnp.arange(length, dtype=F32)[:, None] * frequency[None, :]
    return (jnp.cos(angles), jnp.sin(angles))


def turn_tables(length):
    half = HD // 2
    frequency = (ROPE_BASE ** (-2.0 * np.arange(half) / HD)).astype(np.float32)
    angles = np.arange(length, dtype=np.float32)[:, None] * frequency[None, :]
    plain = np.zeros((length, HD))
    angles = np.concatenate([angles] * (2 * (GROUPS + 1)) + [plain], axis=1).astype(np.float64)
    return jnp.asarray(np.cos(angles), F32), jnp.asarray(np.sin(angles), F32)


def rotate(tensor, cos_table, sin_table):
    half_size = tensor.shape[-1] // 2
    front_half = tensor[..., :half_size]
    back_half = tensor[..., half_size:]
    return jnp.concatenate(
        [
            front_half * cos_table - back_half * sin_table,
            back_half * cos_table + front_half * sin_table,
        ],
        axis=-1,
    )


def dot_f32(left, right):
    return jnp.dot(left, right, preferred_element_type=F32)


def contract_rows(left, right):
    return jnp.einsum("sa,sb->ab", left, right, preferred_element_type=F32)


def contract_cols(left, right):
    return jnp.einsum("sb,ab->sa", left, right, preferred_element_type=F32)


def row_scale(source):
    return lax.rsqrt(jnp.mean(source * source, axis=-1, keepdims=True) + EPSILON)


def norm_backward(grad_norm, scale_row, unit_rows, gain):
    gain_grad = jnp.sum(grad_norm * unit_rows, axis=0)
    scaled = grad_norm * gain
    source_grad = scale_row * (
        scaled - unit_rows * jnp.mean(scaled * unit_rows, axis=-1, keepdims=True)
    )
    return (gain_grad, source_grad)


def after(value, *others):
    return lax.optimization_barrier((value,) + others)[0]


def plane_position():
    rep, core, own = lax.axis_index("rep"), lax.axis_index("sub"), lax.axis_index("fsdp")
    row, col = own // 2, own % 2
    across = row * 2 + (1 - col)
    down = (1 - row) * 2 + col
    corner = (1 - row) * 2 + (1 - col)
    return rep, core, own, across, down, corner


def meet(devices):
    barrier = pltpu.get_barrier_semaphore()
    for device in devices:
        pl.semaphore_signal(barrier, inc=1, device_id=device, device_id_type=MESH)
    pl.semaphore_wait(barrier, len(devices))


def params(collective_id, megabytes=16):
    return pltpu.CompilerParams(
        collective_id=collective_id, has_side_effects=True, vmem_limit_bytes=megabytes << 20
    )


def link_cost(microseconds, flops=0):
    return pl.CostEstimate(
        flops=0, bytes_accessed=int(microseconds * SCALE), transcendentals=0
    )


class Sender:
    def __init__(self, send_sems, recv_sems):
        self.send_sems, self.recv_sems, self.copies = send_sems, recv_sems, []

    def send(self, src, dst, device):
        copy = self.make(src, dst, device)
        copy.start()
        return copy

    def make(self, src, dst, device):
        index = len(self.copies)
        copy = pltpu.make_async_remote_copy(
            src_ref=src,
            dst_ref=dst,
            send_sem=self.send_sems.at[index],
            recv_sem=self.recv_sems.at[index],
            device_id=device,
            device_id_type=MESH,
        )
        self.copies.append(copy)
        return copy

    def finish(self):
        for copy in self.copies:
            copy.wait_send()


class Bounce:
    def __init__(self, src, dst, room, sems):
        self.fetch = pltpu.make_async_copy(src, room, sems.at[0])
        self.store = pltpu.make_async_copy(room, dst, sems.at[1])

    def start(self):
        self.fetch.start()

    def turn(self):
        self.fetch.wait()
        self.store.start()

    def wait(self):
        self.store.wait()


class Gather:
    def __init__(self, sender, x_ref, out_ref, local_sem, place):
        rep, core, own, across, down, corner = place
        to_across, to_down, to_core = (rep, core, across), (rep, core, down), (rep, 1 - core, own)
        half = x_ref.shape[0] // 2
        low, high, whole = pl.ds(0, half), pl.ds(half, half), pl.ds(0, 2 * half)
        base = core * 4

        def first(rows, device):
            return sender.make(x_ref.at[rows], out_ref.at[base + own, rows], device)

        def forward(block, rows, device):
            ref = out_ref.at[base + block, rows]
            return sender.make(ref, ref, device)

        self.across_low, self.down_high = first(low, to_across), first(high, to_down)
        self.across_high, self.down_low = first(high, to_across), first(low, to_down)
        self.corner_low = forward(across, low, to_down)
        self.corner_high = forward(down, high, to_across)
        self.swap_own = first(whole, to_core)
        self.swap_near = [
            forward(across, low, to_core),
            forward(down, high, to_core),
            forward(across, high, to_core),
            forward(down, low, to_core),
        ]
        self.swap_corner = [forward(corner, low, to_core), forward(corner, high, to_core)]
        self.mine = pltpu.make_async_copy(x_ref, out_ref.at[base + own], local_sem)

    def begin(self):
        for copy in (self.across_low, self.down_high, self.across_high, self.down_low):
            copy.start()
        self.swap_own.start()
        self.mine.start()

    def relay(self):
        self.relay_first()
        self.relay_second()

    def relay_first(self):
        self.across_low.wait_recv()
        self.corner_low.start()
        self.swap_near[0].start()
        self.down_high.wait_recv()
        self.corner_high.start()
        self.swap_near[1].start()

    def relay_second(self):
        self.across_high.wait_recv()
        self.swap_near[2].start()
        self.down_low.wait_recv()
        self.swap_near[3].start()

    def finish(self):
        self.pass_corner()
        self.arrive()

    def pass_corner(self):
        self.corner_low.wait_recv()
        self.swap_corner[0].start()
        self.corner_high.wait_recv()
        self.swap_corner[1].start()

    def arrive(self):
        for swap in [self.swap_own] + self.swap_near + self.swap_corner:
            swap.wait_recv()
        self.mine.wait()


class ExchangeJob:
    climbs = False
    corner = True

    def __init__(self, source):
        self.rows = source.shape[0] // 4
        shape = (self.rows, source.shape[1])
        self.arrays = [source]
        self.outs = [jax.ShapeDtypeStruct((4,) + shape, BF16)]
        self.scratch = [pltpu.SemaphoreType.DMA((3,))] * 2
        self.scratch += [pltpu.VMEM(shape, BF16), pltpu.SemaphoreType.DMA((2,))]

    def open(self, arrays, outs, scratch, place):
        self.source, self.out, self.place = arrays[0], outs[0], place
        own = place[2]
        self.sems = scratch[:2]
        self.keep = Bounce(self.part(own), self.out.at[own], scratch[2], scratch[3])

    def part(self, block):
        return self.source.at[pl.ds(pl.multiple_of(block * self.rows, 16), self.rows)]

    def stage(self, n):
        rep, core, own, across, down, corner = self.place
        if n == 0:
            self.keep.start()
            self.sender = Sender(*self.sems)
            for peer in (corner, across, down):
                self.sender.send(self.part(peer), self.out.at[own], (rep, core, peer))
        if n == 1:
            self.keep.turn()
        if n == 6:
            for copy in self.sender.copies:
                copy.wait()
            self.keep.wait()


class KeepJob:
    climbs = False
    corner = False

    def __init__(self, source):
        self.arrays = [source]
        self.outs = [jax.ShapeDtypeStruct(source.shape, BF16)]
        self.scratch = [pltpu.VMEM(source.shape, BF16), pltpu.SemaphoreType.DMA((2,))]

    def open(self, arrays, outs, scratch, place):
        self.keep = Bounce(arrays[0], outs[0], *scratch)

    def stage(self, n):
        if n == 0:
            self.keep.start()
        if n == 1:
            self.keep.turn()
        if n == 6:
            self.keep.wait()


def column_place(place, reps):
    rep, core, own = place[:3]
    above, below = ((rep + 1) % reps, core, own), ((rep + reps - 1) % reps, core, own)
    up = (rep == 0, rep == reps - 1, above, below)
    down = (rep == reps - 1, rep == 0, below, above)
    return (up, down)


def skewed(rep, reps, count, act, i):
    for low in (True, False):
        near = 0 if low else 1

        @pl.when((rep * 2 < reps) == low)
        def _(near=near):
            if i < count:
                act(near, i)
            if i >= 1:
                act(1 - near, i - 1)


class SumJob:
    climbs = True

    def __init__(self, sources, blocks, cuts, reps, steps):
        self.blocks, self.cuts, self.reps, self.steps = blocks, cuts, reps, steps
        self.arrays = sources
        self.corner = blocks > 1
        rows = sources[0].shape[0]
        self.span = rows // blocks
        self.half = self.span // 2
        self.size = self.half // cuts
        self.widths = [source.shape[1] for source in sources]
        wide = sum(self.widths)
        self.shape = (2, blocks, self.half, wide)
        self.outs = []
        self.count = blocks * cuts
        sems = pltpu.SemaphoreType.DMA((2, self.count))
        self.scratch = [
            pltpu.VMEM(self.shape, BF16),
            pltpu.VMEM(self.shape, BF16),
            pltpu.VMEM(self.shape, BF16),
            pltpu.SemaphoreType.DMA((2, blocks, len(sources))),
        ] + [sems] * 5

    def open(self, arrays, outs, scratch, place):
        self.sources = arrays
        self.held, self.landed, self.fin, self.load_sems = scratch[:4]
        self.chain_sems, self.give_sems, self.keep_sems = scratch[4:6], scratch[6:8], scratch[8]
        self.rep, self.core, self.own = place[:3]
        self.ways = column_place(place, self.reps)
        for k in range(self.blocks):
            for way in range(2):
                for load in self.loads(way, k):
                    load.start()

    def block(self, k):
        return (self.own + k) % self.blocks

    def loads(self, way, k):
        copies = []
        at = 0
        for n, (source, width) in enumerate(zip(self.sources, self.widths)):
            start = pl.multiple_of(self.block(k) * self.span + way * self.half, 16)
            src = source.at[pl.ds(start, self.half)]
            dst = self.held.at[way, k, :, pl.ds(at, width)]
            copies.append(pltpu.make_async_copy(src, dst, self.load_sems.at[way, k, n]))
            at += width
        return copies

    def rows(self, i):
        return i // self.cuts, pl.ds(i % self.cuts * self.size, self.size)

    def chain(self, way, i):
        k, rows = self.rows(i)
        return pltpu.make_async_remote_copy(
            src_ref=self.held.at[way, k, rows],
            dst_ref=self.landed.at[way, k, rows],
            send_sem=self.chain_sems[0].at[way, i],
            recv_sem=self.chain_sems[1].at[way, i],
            device_id=self.ways[way][2],
            device_id_type=MESH,
        )

    def give(self, way, i):
        k, rows = self.rows(i)
        return pltpu.make_async_remote_copy(
            src_ref=self.held.at[way, k, rows],
            dst_ref=self.fin.at[way, self.own, rows],
            send_sem=self.give_sems[0].at[way, i],
            recv_sem=self.give_sems[1].at[way, i],
            device_id=(self.rep, self.core, self.block(k)),
            device_id_type=MESH,
        )

    def keep(self, way, i):
        k, rows = self.rows(i)
        own = self.own if self.blocks > 1 else 0
        src, dst = self.held.at[way, k, rows], self.fin.at[way, own, rows]
        return pltpu.make_async_copy(src, dst, self.keep_sems.at[way, i])

    def loaded(self, way, i):
        if i % self.cuts == 0:
            for load in self.loads(way, i // self.cuts):
                load.wait()

    def prime(self):
        for way in range(2):

            @pl.when(self.ways[way][0])
            def _(way=way):
                for i in range(self.count):
                    self.loaded(way, i)
                    self.chain(way, i).start()

    def add(self, way, i):
        first, last = self.ways[way][:2]
        k, rows = self.rows(i)

        @pl.when(jnp.logical_not(first))
        def _():
            self.loaded(way, i)
            self.chain(way, i).wait_recv()
            self.held[way, k, rows] = self.held[way, k, rows] + self.landed[way, k, rows]

            @pl.when(jnp.logical_not(last))
            def _():
                self.chain(way, i).start()

            @pl.when(last)
            def _():
                if k == 0:
                    self.keep(way, i).start()
                else:
                    self.give(way, i).start()

    def step(self, i):
        skewed(self.rep, self.reps, self.count, self.add, i)

    def stage(self, n):
        if n == 0:
            self.prime()
        if n in self.steps:
            for i in self.steps[n]:
                self.step(i)
        if n == 7:
            for way in range(2):
                last = self.ways[way][1]
                for i in range(self.count):

                    @pl.when(jnp.logical_not(last))
                    def _(way=way, i=i):
                        self.chain(way, i).wait_send()

                    @pl.when(last)
                    def _(way=way, i=i):
                        if i // self.cuts == 0:
                            self.keep(way, i).wait()
                        else:
                            self.give(way, i).wait()


class HandJob:
    climbs = True

    def __init__(self, sums, reps, cuts):
        self.sums, self.arrays = sums, []
        shape = sums.shape
        self.reps, self.cuts, self.size = reps, cuts, shape[2] // cuts
        self.count = shape[1] * cuts
        self.corner = False
        self.outs = [jax.ShapeDtypeStruct((2, 2) + shape[1:], BF16)]
        self.scratch = [pltpu.SemaphoreType.DMA((2, self.count))] * 5

    def open(self, arrays, outs, scratch, place):
        self.out = outs[0]
        self.hand_sems, self.side_sems, self.keep_sems = scratch[:2], scratch[2:4], scratch[4]
        self.rep, self.core, self.own = place[:3]
        self.ways = column_place(place, self.reps)

    def rows(self, j):
        return j // self.cuts, pl.ds(j % self.cuts * self.size, self.size)

    def place(self, way, j):
        block, rows = self.rows(j)
        return self.out.at[way, self.core, block, rows]

    def remote(self, src, way, j, sems, device):
        return pltpu.make_async_remote_copy(
            src_ref=src,
            dst_ref=self.place(way, j),
            send_sem=sems[0].at[way, j],
            recv_sem=sems[1].at[way, j],
            device_id=device,
            device_id_type=MESH,
        )

    def beside(self):
        return (self.rep, 1 - self.core, self.own)

    def begin(self):
        fin = self.sums.fin
        for j in range(self.count):
            for way in range(2):

                @pl.when(self.ways[way][1])
                def _(way=way, j=j):
                    block, rows = self.rows(j)
                    src = fin.at[way, block, rows]
                    self.remote(src, way, j, self.hand_sems, self.ways[way][3]).start()
                    self.remote(src, way, j, self.side_sems, self.beside()).start()
                    dst = self.place(way, j)
                    pltpu.make_async_copy(src, dst, self.keep_sems.at[way, j]).start()

    def hand(self, way, j):
        first, last = self.ways[way][:2]

        @pl.when(jnp.logical_not(last))
        def _():
            ref = self.place(way, j)
            hand = self.remote(ref, way, j, self.hand_sems, self.ways[way][3])
            hand.wait_recv()

            @pl.when(jnp.logical_not(first))
            def _():
                hand.start()

            self.remote(ref, way, j, self.side_sems, self.beside()).start()

    def pass_on(self):
        for j in range(self.count + 1):
            skewed(self.rep, self.reps, self.count, lambda w, i: self.hand(1 - w, i), j)

    def close(self):
        for j in range(self.count):
            for way in range(2):
                first, last = self.ways[way][:2]
                ref = self.place(way, j)
                self.remote(ref, way, j, self.side_sems, self.beside()).wait()

                @pl.when(jnp.logical_not(first))
                def _(way=way, j=j, ref=ref):
                    self.remote(ref, way, j, self.hand_sems, self.ways[way][3]).wait_send()

                @pl.when(last)
                def _(way=way, j=j, ref=ref):
                    pltpu.make_async_copy(ref, ref, self.keep_sems.at[way, j]).wait()

    def stage(self, n):
        if n == 7:
            self.begin()
        if n == 8:
            self.pass_on()
        if n == 9:
            self.close()


class Jobs:
    def __init__(self, jobs, reps):
        self.jobs, self.reps = jobs, reps
        self.arrays = [a for job in jobs for a in job.arrays]
        self.out_shapes = [o for job in jobs for o in job.outs]
        self.scratch = [x for job in jobs for x in job.scratch]

    def greet(self, place):
        rep, core, own, across, down, corner = place
        devices = [(rep, core, across), (rep, core, down), (rep, 1 - core, own)]
        if any(job.climbs for job in self.jobs):
            devices += [((rep + 1) % self.reps, core, own)]
            devices += [((rep + self.reps - 1) % self.reps, core, own)]
        if any(job.corner for job in self.jobs):
            devices.append((rep, core, corner))
        meet(devices)

    def open(self, arrays, outs, scratch, place):
        arrays, outs, scratch = list(arrays), list(outs), list(scratch)

        def take(refs, count):
            taken = refs[:count]
            del refs[:count]
            return taken

        for job in self.jobs:
            mine = [take(arrays, len(job.arrays)), take(outs, len(job.outs))]
            job.open(*mine, take(scratch, len(job.scratch)), place)

    def stage(self, n):
        for job in self.jobs:
            job.stage(n)


def gather_kernel(count, jobs, *refs):
    arrays, outs = len(jobs.arrays), len(jobs.out_shapes)
    xs, job_arrays = refs[:count], refs[count : count + arrays]
    refs = refs[count + arrays :]
    x_outs, job_outs = refs[:count], refs[count : count + outs]
    refs = refs[count + outs :]
    local_sems, send_sems, recv_sems = refs[:3]
    place = plane_position()
    jobs.greet(place)
    sender = Sender(send_sems, recv_sems)
    moves = [
        Gather(sender, x, out, local_sems.at[i], place)
        for i, (x, out) in enumerate(zip(xs, x_outs))
    ]
    for move in moves:
        move.begin()
    jobs.open(job_arrays, job_outs, refs[3:], place)
    jobs.stage(0)
    jobs.stage(1)
    for move in moves:
        move.relay()
    jobs.stage(5)
    for move in moves:
        move.finish()
    sender.finish()
    for n in (6, 7, 8, 9):
        jobs.stage(n)


def gather_plane(blocks, collective_id, jobs=(), reps=1):
    count = len(blocks)
    jobs = Jobs(jobs, reps)
    return pl.pallas_call(
        functools.partial(gather_kernel, count, jobs),
        out_shape=[jax.ShapeDtypeStruct((8,) + x.shape, x.dtype) for x in blocks]
        + jobs.out_shapes,
        in_specs=[VM] * count + [HBM] * len(jobs.arrays),
        out_specs=[HBM] * (count + len(jobs.out_shapes)),
        scratch_shapes=[
            pltpu.SemaphoreType.DMA((count,)),
            pltpu.SemaphoreType.DMA((13 * count,)),
            pltpu.SemaphoreType.DMA((13 * count,)),
        ]
        + jobs.scratch,
        compiler_params=params(collective_id, 60),
        cost_estimate=link_cost(40 * count),
    )(*blocks, *jobs.arrays)


def column_source(ref, rows, block, width):
    return ref.at[rows, pl.ds(pl.multiple_of(block * width, width), width)]


def quarter_kernel(gate_ref, up_ref, out_ref, room, local_sems, send_sems, recv_sems):
    rep, core, own, across, down, corner = plane_position()
    peers = (corner, across, down)
    meet([(rep, core, peer) for peer in peers])
    rows = out_ref.shape[1]
    width = out_ref.shape[2] // 2
    mine = pl.ds(pl.multiple_of(rep * rows, rows), rows)
    sender = Sender(send_sems, recv_sems)
    local = []
    for k, ref in enumerate((gate_ref, up_ref)):
        columns = pl.ds(k * width, width)
        target = out_ref.at[own, :, columns]
        source = column_source(ref, mine, own * 2 + core, width)
        copy = Bounce(source, target, room.at[:, columns], local_sems.at[k])
        copy.start()
        local.append(copy)
        for peer in peers:
            source = column_source(ref, mine, peer * 2 + core, width)
            sender.send(source, target, (rep, core, peer))
    for copy in local:
        copy.turn()
    for copy in sender.copies:
        copy.wait_recv()
    sender.finish()
    for copy in local:
        copy.wait()


def quarter_columns(w_gate, w_up, reps, collective_id):
    rows, columns = w_gate.shape
    shape = (rows // reps, columns // 4)
    return pl.pallas_call(
        quarter_kernel,
        out_shape=jax.ShapeDtypeStruct((4,) + shape, BF16),
        in_specs=[HBM] * 2,
        out_specs=HBM,
        scratch_shapes=[
            pltpu.VMEM(shape, BF16),
            pltpu.SemaphoreType.DMA((2, 2)),
            pltpu.SemaphoreType.DMA((6,)),
            pltpu.SemaphoreType.DMA((6,)),
        ],
        compiler_params=params(collective_id, 60),
        cost_estimate=link_cost(25),
    )(w_gate, w_up)


def start_kernel(
    x_ref, code_ref, gain_ref, q_ref, k_ref, v_ref, x_out, code_out, gain_out, heads_out,
    room, bounce_sems, local_sems, send_sems, recv_sems,
):
    place = plane_position()
    rep, core, own, across, down, corner = place
    peers = (corner, across, down)
    others = [(rep, core, peer) for peer in peers] + [(rep, 1 - core, peer) for peer in peers]
    others.append((rep, 1 - core, own))
    meet(others)
    sender = Sender(send_sems, recv_sems)
    move = Gather(sender, x_ref, x_out, local_sems.at[0], place)
    direct = [sender.make(gain_ref, gain_out.at[own], (rep, core, peer)) for peer in peers]
    slot = code_out.at[core * 4 + own]
    direct += [sender.make(code_ref, slot, device) for device in others]
    whole = pl.ds(0, q_ref.shape[0])
    q_wide, pair = GROUPS * HD, 2 * HD

    def fetch(ref, at, width, blocks):
        columns = pl.ds(at, width)
        target = heads_out.at[own, :, columns]
        source = column_source(ref, whole, blocks[0], width)
        bounced = Bounce(source, target, room.at[:, columns], bounce_sems.at[min(at, 1)])
        sends = []
        for block, peer in zip(blocks[1:], peers):
            source = column_source(ref, whole, block, width)
            sends.append(sender.make(source, target, (rep, core, peer)))
        return bounced, sends

    def swap(at):
        columns = pl.ds(at, pair)
        copies = [sender.make(room.at[:, columns], heads_out.at[own, :, columns], others[-1])]
        for peer in peers:
            ref = heads_out.at[peer, :, columns]
            copies.append(sender.make(ref, ref, others[-1]))
        return copies

    q_kept, q_sends = fetch(q_ref, 0, q_wide, [block * 2 + core for block in (own,) + peers])
    direct += q_sends
    first = len(sender.copies)
    sides = []
    for ref, at in ((k_ref, q_wide), (v_ref, q_wide + pair)):
        kept, sends = fetch(ref, at, pair, (own,) + peers)
        swaps = swap(at)
        del sender.copies[first + len(sends) :]
        sides.append((kept, sends, swaps, swap(2 * q_wide + pair - at)))
        del sender.copies[first:]
    local = [
        pltpu.make_async_copy(gain_ref, gain_out.at[own], local_sems.at[1]),
        pltpu.make_async_copy(code_ref, slot, local_sems.at[2]),
    ]
    move.begin()
    for copy in direct + local + [q_kept]:
        copy.start()
    for side, (kept, sends, swaps, _) in enumerate(sides):

        @pl.when(core == side)
        def _(kept=kept, sends=sends, swaps=swaps):
            for copy in [kept] + sends:
                copy.start()
            kept.turn()
            swaps[0].start()

    q_kept.turn()
    move.relay()
    for side, (kept, sends, swaps, _) in enumerate(sides):

        @pl.when(core == side)
        def _(kept=kept, sends=sends, swaps=swaps):
            for copy, passed in zip(sends, swaps[1:]):
                copy.wait_recv()
                passed.start()

    move.finish()
    for copy in direct:
        copy.wait_recv()
    for side, (kept, sends, swaps, arrivals) in enumerate(sides):

        @pl.when(core == side)
        def _(kept=kept, sends=sends, swaps=swaps, arrivals=arrivals):
            for copy in arrivals:
                copy.wait_recv()
            for copy in sends + swaps:
                copy.wait_send()
            kept.wait()

    sender.finish()
    for copy in local + [q_kept]:
        copy.wait()


def start_plane(hidden, codes, gains, w_query, w_key, w_value, collective_id):
    heads = (w_query.shape[0], (GROUPS + 4) * HD)
    shapes = [
        ((8,) + hidden.shape, BF16),
        ((8,) + codes.shape, jnp.int32),
        ((4,) + gains.shape, BF16),
        ((4,) + heads, BF16),
    ]
    return pl.pallas_call(
        start_kernel,
        out_shape=[jax.ShapeDtypeStruct(s, d) for s, d in shapes],
        in_specs=[VM] * 3 + [HBM] * 3,
        out_specs=[HBM] * 4,
        scratch_shapes=[
            pltpu.VMEM(heads, BF16),
            pltpu.SemaphoreType.DMA((2, 2)),
            pltpu.SemaphoreType.DMA((3,)),
            pltpu.SemaphoreType.DMA((40,)),
            pltpu.SemaphoreType.DMA((40,)),
        ],
        compiler_params=params(collective_id, 60),
        cost_estimate=link_cost(60),
    )(hidden, codes, gains, w_query, w_key, w_value)


def mlp_kernel(
    x_ref, w_hbm, grad_hbm, x_out, product_out, act_out, down_out,
    x_all, w_ref, product, act, grad, total, down,
    w_sems, grad_sems, store_sems, down_sems, local_sem, send_sems, recv_sems,
):
    place = plane_position()
    rep, core, own, across, down_at, corner = place
    rows = x_ref.shape[0]
    ff = act.shape[2]
    tile, depth = 512, 256
    tiles = ff // tile
    here, there = core * 4, (1 - core) * 4
    order = [here + own, there + own, here + across, here + down_at]
    order += [there + across, there + down_at, here + corner, there + corner]
    loads = []
    for t in range(tiles):
        for k in range(2):
            columns = pl.ds(k * ff + t * tile, tile)
            load = pltpu.make_async_copy(w_hbm.at[:, columns], w_ref.at[:, columns], w_sems.at[t, k])
            load.start()
            loads.append(load)
    grads = [
        pltpu.make_async_copy(grad_hbm.at[block], grad.at[n % 2], grad_sems.at[n])
        for n, block in enumerate(order)
    ]
    grads[0].start()
    grads[1].start()
    meet([(rep, core, across), (rep, core, down_at), (rep, 1 - core, own)])
    sender = Sender(send_sems, recv_sems)
    move = Gather(sender, x_ref, x_all, local_sem, place)
    move.begin()
    pending, finals = [], []

    def piece(x, slot, at):
        gate = dot_f32(x, w_ref[:, pl.ds(at, tile)])
        up = dot_f32(x, w_ref[:, pl.ds(ff + at, tile)])
        product[slot, :, pl.ds(at, tile)] = gate
        product[slot, :, pl.ds(ff + at, tile)] = up
        act[slot, :, pl.ds(at, tile)] = (gate * jax.nn.sigmoid(gate) * up).astype(BF16)

    def compute(n):
        block, slot = order[n], n % 2
        if n >= 2:
            for store in pending[n - 2][:2]:
                store.wait()
        for t in range(tiles):
            if n == 0:
                loads[2 * t].wait()
                loads[2 * t + 1].wait()
            piece(x_all[block], slot, t * tile)
        mine = pl.ds(pl.multiple_of(block * rows, rows), rows)
        stores = [
            pltpu.make_async_copy(product.at[slot], product_out.at[mine], store_sems.at[n, 0]),
            pltpu.make_async_copy(act.at[slot], act_out.at[mine], store_sems.at[n, 1]),
            pltpu.make_async_copy(x_all.at[block], x_out.at[block], store_sems.at[n, 2]),
        ]
        for store in stores:
            store.start()
        pending.append(stores)

    def weigh(n):
        slot = n % 2
        grads[n].wait()

        def term(at):
            return lax.dot_general(
                act[slot, :, pl.ds(at, depth)], grad[slot], (((0,), (0,)), ((), ())),
                preferred_element_type=F32,
            )

        if n == 7:
            for r in range(ff // depth):
                at = pl.ds(r * depth, depth)
                down[at] = (total[at] + term(r * depth)).astype(BF16)
                final = pltpu.make_async_copy(down.at[at], down_out.at[at], down_sems.at[r])
                final.start()
                finals.append(final)
        else:

            @pl.loop(0, ff // depth)
            def _(r):
                start = pl.multiple_of(r * depth, depth)
                at = pl.ds(start, depth)
                total[at] = term(start) if n == 0 else total[at] + term(start)

        if n + 2 < 8:
            grads[n + 2].start()

    move.mine.wait()
    compute(0)
    move.swap_own.wait_recv()
    compute(1)
    move.relay_first()
    weigh(0)
    weigh(1)
    move.relay_second()
    compute(2)
    compute(3)
    for swap in move.swap_near:
        swap.wait_recv()
    weigh(2)
    compute(4)
    move.pass_corner()
    weigh(3)
    compute(5)
    weigh(4)
    compute(6)
    weigh(5)
    for swap in move.swap_corner:
        swap.wait_recv()
    compute(7)
    weigh(6)
    weigh(7)
    for k, stores in enumerate(pending):
        for store in stores if k >= 6 else stores[2:]:
            store.wait()
    for final in finals:
        final.wait()
    sender.finish()


def mlp_plane(x, w, grad, collective_id):
    rows, width = x.shape
    wide = w.shape[1]
    ff = wide // 2
    return pl.pallas_call(
        mlp_kernel,
        out_shape=[
            jax.ShapeDtypeStruct((8, rows, width), BF16),
            jax.ShapeDtypeStruct((8 * rows, wide), F32),
            jax.ShapeDtypeStruct((8 * rows, ff), BF16),
            jax.ShapeDtypeStruct((ff, width), BF16),
        ],
        in_specs=[VM, HBM, HBM],
        out_specs=[HBM] * 4,
        scratch_shapes=[
            pltpu.VMEM((8, rows, width), BF16),
            pltpu.VMEM((width, wide), BF16),
            pltpu.VMEM((2, rows, wide), F32),
            pltpu.VMEM((2, rows, ff), BF16),
            pltpu.VMEM((2, rows, width), BF16),
            pltpu.VMEM((ff, width), F32),
            pltpu.VMEM((ff, width), BF16),
            pltpu.SemaphoreType.DMA((ff // 512, 2)),
            pltpu.SemaphoreType.DMA((8,)),
            pltpu.SemaphoreType.DMA((8, 3)),
            pltpu.SemaphoreType.DMA((ff // 256,)),
            pltpu.SemaphoreType.DMA,
            pltpu.SemaphoreType.DMA((13,)),
            pltpu.SemaphoreType.DMA((13,)),
        ],
        compiler_params=params(collective_id, 60),
        cost_estimate=link_cost(50),
    )(x, w, grad)


def product_scatter_kernel(turned, count, jobs, *refs):
    arrays, outs = len(jobs.arrays), len(jobs.out_shapes)
    x_hbm, w_hbm, job_arrays = refs[:count], refs[count], refs[count + 1 : count + 1 + arrays]
    refs = refs[count + 1 + arrays :]
    out_ref, job_outs = refs[0], refs[1 : 1 + outs]
    refs = refs[1 + outs :]
    x_refs, w_ref = refs[:count], refs[count]
    (
        swap, held, from_core, from_across, from_down, last_across, last_down,
        x_sems, w_sems, core_send, core_recv, send_sems, recv_sems,
    ) = refs[count + 1 : count + 14]
    place = plane_position()
    rep, core, own, across, down, corner = place
    to_across, to_down, to_core = (rep, core, across), (rep, core, down), (rep, 1 - core, own)
    _, rows, wide = held.shape
    depth = x_refs[0].shape[1]
    tile = 512
    tiles = wide // tile
    half = rows // 2
    low, high = pl.ds(0, half), pl.ds(half, half)
    order = []
    for block in (corner, across, down, own):
        order += [(1 - core) * 4 + block, core * 4 + block]

    def rows_of(block):
        return pl.ds(pl.multiple_of(block * rows, rows), rows)

    x_loads = [
        [
            pltpu.make_async_copy(
                x_hbm[i].at[rows_of(block)], x_refs[i].at[rows_of(block)], x_sems.at[i, n]
            )
            for i in range(count)
        ]
        for n, block in enumerate(order)
    ]
    w_loads = []
    for t in range(tiles):
        columns = pl.ds(t * tile, tile)
        if turned:
            src, dst = w_hbm.at[columns], w_ref.at[columns]
        else:
            kept = pl.ds(pl.multiple_of(core * depth, depth), depth)
            src, dst = w_hbm.at[kept, columns], w_ref.at[:, columns]
        w_loads.append(pltpu.make_async_copy(src, dst, w_sems.at[t]))
    for load in x_loads[0]:
        load.start()
    for load in w_loads:
        load.start()
    for loads in x_loads[1:]:
        for load in loads:
            load.start()
    jobs.open(job_arrays, job_outs, refs[count + 14 :], place)
    jobs.greet(place)
    jobs.stage(0)

    def product(dst, mine, columns):
        total = None
        for i in range(count):
            x = x_refs[i][mine, :]
            if turned:
                w = w_ref[columns, pl.ds(i * depth, depth)]
                part = lax.dot_general(
                    x, w, (((1,), (1,)), ((), ())), preferred_element_type=F32
                )
            else:
                part = dot_f32(x, w_ref[:, columns])
            total = part if total is None else total + part
        dst[:, columns] = total.astype(BF16)

    def fill(dst, n):
        for load in x_loads[n]:
            load.wait()
        mine = rows_of(order[n])
        if n == 0:
            for t in range(tiles):
                w_loads[t].wait()
                product(dst, mine, pl.ds(t * tile, tile))
        else:

            @pl.loop(0, tiles)
            def _(t):
                product(dst, mine, pl.ds(pl.multiple_of(t * tile, tile), tile))

    swaps = Sender(core_send, core_recv)
    sender = Sender(send_sems, recv_sems)
    sent = {}
    for k in range(4):
        fill(swap.at[k], 2 * k)
        swaps.send(swap.at[k], from_core.at[k], to_core)
        fill(held.at[k], 2 * k + 1)
        swaps.copies[k].wait_recv()
        held[k] = held[k] + from_core[k]
        if k == 0:
            sent[0] = sender.send(held.at[0, low], from_across.at[0], to_across)
            sent[1] = sender.send(held.at[0, high], from_down.at[0], to_down)
        if k == 1:
            sent[2] = sender.send(held.at[1, low], from_across.at[1], to_across)
        if k == 2:
            sent[3] = sender.send(held.at[2, high], from_down.at[1], to_down)
        jobs.stage(1 + k)
    sent[0].wait_recv()
    held[2, low] = held[2, low] + from_across[0]
    to_last = sender.send(held.at[2, low], last_down, to_down)
    sent[1].wait_recv()
    held[1, high] = held[1, high] + from_down[0]
    across_last = sender.send(held.at[1, high], last_across, to_across)
    jobs.stage(5)
    sent[2].wait_recv()
    sent[3].wait_recv()
    to_last.wait_recv()
    out_ref[low] = (
        held[3, low].astype(F32) + from_across[1].astype(F32) + last_down[...].astype(F32)
    )
    across_last.wait_recv()
    out_ref[high] = (
        held[3, high].astype(F32) + from_down[1].astype(F32) + last_across[...].astype(F32)
    )
    swaps.finish()
    sender.finish()
    for n in (6, 7, 8, 9):
        jobs.stage(n)


def product_scatter(xs, w, turned, collective_id, jobs=(), reps=1):
    count = len(xs)
    jobs = Jobs(jobs, reps)
    tokens, depth = xs[0].shape
    rows = tokens // 8
    wide = w.shape[0] if turned else w.shape[1]
    half = rows // 2
    return pl.pallas_call(
        functools.partial(product_scatter_kernel, turned, count, jobs),
        out_shape=[jax.ShapeDtypeStruct((rows, wide), F32)] + jobs.out_shapes,
        in_specs=[HBM] * (count + 1 + len(jobs.arrays)),
        out_specs=[VM] + [HBM] * len(jobs.out_shapes),
        scratch_shapes=[pltpu.VMEM((tokens, depth), BF16)] * count
        + [
            pltpu.VMEM((wide, depth * count) if turned else (depth, wide), BF16),
            pltpu.VMEM((4, rows, wide), BF16),
            pltpu.VMEM((4, rows, wide), BF16),
            pltpu.VMEM((4, rows, wide), BF16),
            pltpu.VMEM((2, half, wide), BF16),
            pltpu.VMEM((2, half, wide), BF16),
            pltpu.VMEM((half, wide), BF16),
            pltpu.VMEM((half, wide), BF16),
            pltpu.SemaphoreType.DMA((count, 8)),
            pltpu.SemaphoreType.DMA((wide // 512,)),
            pltpu.SemaphoreType.DMA((4,)),
            pltpu.SemaphoreType.DMA((4,)),
            pltpu.SemaphoreType.DMA((6,)),
            pltpu.SemaphoreType.DMA((6,)),
        ]
        + jobs.scratch,
        compiler_params=params(collective_id, 60),
        cost_estimate=link_cost(44, 2 * tokens * depth * count * wide),
    )(*xs, w, *jobs.arrays)


def turn(value, cos_ref, sin_ref, back):
    wide = value.shape[1]
    lanes = lax.broadcasted_iota(jnp.int32, value.shape, 1)
    front = lax.rem(lanes, HD) < HD // 2
    ahead = pltpu.roll(value, wide - HD // 2, 1)
    behind = pltpu.roll(value, HD // 2, 1)
    swapped = jnp.where(front, -ahead, behind) * sin_ref[...]
    turned = value * cos_ref[...]
    return turned - swapped if back else turned + swapped


def allowed_pairs(row_ref, col_ref):
    keys, queries = row_ref[...], col_ref[...]
    length = keys.shape[1]
    row_index = lax.broadcasted_iota(jnp.int32, (length, length), 0)
    col_index = lax.broadcasted_iota(jnp.int32, (length, length), 1)
    same = lax.shift_right_logical(keys, 1) == lax.shift_right_logical(queries, 1)
    valid = jnp.bitwise_and(keys, 1) == 1
    return same & (col_index <= row_index) & (valid | (col_index == row_index))


def head_probs(query, keys, allowed):
    scores = lax.dot_general(
        query, keys, (((1,), (1,)), ((), ())), preferred_element_type=F32
    )
    scores = jnp.where(allowed, scores * SCORE_SCALE, MASKED_SCORE)
    shifted = jnp.exp(scores - jnp.max(scores, axis=-1, keepdims=True))
    return shifted / jnp.sum(shifted, axis=-1, keepdims=True)


def attend_kernel(
    x_hbm, gain_ref, w_ref, cos_ref, sin_ref, row_ref, col_ref, cot_ref, out_w_hbm,
    out_ref, normed_hbm, heads_hbm, attended_hbm, cot_out,
    x_buf, normed, heads_buf, attended, out_w, parts, from_core, from_across, from_down,
    last_across, last_down, x_sems, w_sem, store_sems, local_sem,
    core_send, core_recv, send_sems, recv_sems, cot_send, cot_recv,
):
    place = plane_position()
    rep, core, own, across, down, corner = place
    row, col = own // 2, own % 2
    to_across, to_down, to_core = (rep, core, across), (rep, core, down), (rep, 1 - core, own)
    length, wide = out_ref.shape
    half = length // 2
    low, high = pl.ds(0, half), pl.ds(half, half)
    depth = out_w.shape[0]
    tile = 512

    def block_of(n):
        k = n // 2
        far_row = row + (k + 1) % 2 * (1 - 2 * row)
        far_col = col + (1 - k // 2) * (1 - 2 * col)
        near = n % 2
        return (near * core + (1 - near) * (1 - core)) * 4 + far_row * 2 + far_col

    def fetch(n):
        slot = n % 2
        return pltpu.make_async_copy(x_hbm.at[block_of(n)], x_buf.at[slot], x_sems.at[slot])

    def stores(n):
        slot, block = n % 2, block_of(n)
        pairs = ((normed, normed_hbm), (heads_buf, heads_hbm), (attended, attended_hbm))
        return [
            pltpu.make_async_copy(src.at[slot], dst.at[block], store_sems.at[slot, i])
            for i, (src, dst) in enumerate(pairs)
        ]

    def swap(k):
        return pltpu.make_async_remote_copy(
            src_ref=parts.at[0, k],
            dst_ref=from_core.at[k],
            send_sem=core_send.at[k],
            recv_sem=core_recv.at[k],
            device_id=to_core,
            device_id_type=MESH,
        )

    rows_kept = pl.ds(pl.multiple_of(core * depth, depth), depth)
    out_w_load = pltpu.make_async_copy(out_w_hbm.at[rows_kept], out_w, w_sem)
    out_w_load.start()
    fetch(0).start()
    meet([to_across, to_down, to_core])
    cot_sender = Sender(cot_send, cot_recv)
    move = Gather(cot_sender, cot_ref, cot_out, local_sem, place)
    move.begin()
    sender = Sender(send_sems, recv_sems)
    sent = [
        sender.make(parts.at[1, 0, low], from_across.at[0], to_across),
        sender.make(parts.at[1, 0, high], from_down.at[0], to_down),
        sender.make(parts.at[1, 1, low], from_across.at[1], to_across),
        sender.make(parts.at[1, 2, high], from_down.at[1], to_down),
        sender.make(parts.at[1, 2, low], last_down, to_down),
        sender.make(parts.at[1, 1, high], last_across, to_across),
    ]
    out_w_load.wait()

    @pl.loop(0, 8)
    def _(n):
        slot, k = n % 2, n // 2
        block = block_of(n)
        fetch(n).wait()

        @pl.when(n < 7)
        def _():
            fetch(n + 1).start()

        @pl.when(n >= 2)
        def _():
            for store in stores(n - 2):
                store.wait()

        @pl.when(n == 3)
        def _():
            move.relay_first()

        @pl.when(n == 5)
        def _():
            move.relay_second()

        @pl.loop(0, length // 32)
        def _(t):
            rows = pl.ds(pl.multiple_of(t * 32, 32), 32)
            x = x_buf[slot, rows].astype(F32)
            normed[slot, rows] = (x * row_scale(x) * gain_ref[...]).astype(BF16)

        projected = dot_f32(normed[slot], w_ref[...])
        keys_at, values_at = GROUPS * HD, (GROUPS + 2) * HD
        pieces = [projected[:, :keys_at]]
        for at in (keys_at, values_at):
            mine, other = projected[:, at : at + HD], projected[:, at + HD : at + 2 * HD]
            pieces.append(jnp.where(core == 0, mine, other))
        heads = turn(jnp.concatenate(pieces, axis=1), cos_ref, sin_ref, False).astype(BF16)
        heads_buf[slot] = heads
        allowed = allowed_pairs(row_ref.at[block], col_ref.at[block])
        keys = heads[:, GROUPS * HD : (GROUPS + 1) * HD]
        values = heads[:, (GROUPS + 1) * HD :]
        outs = []
        for h in range(GROUPS):
            probs = head_probs(heads[:, h * HD : (h + 1) * HD], keys, allowed)
            outs.append(dot_f32(probs.astype(BF16), values))
        attended[slot] = jnp.concatenate(outs, axis=1).astype(BF16)
        for store in stores(n):
            store.start()

        @pl.loop(0, wide // tile)
        def _(t):
            columns = pl.ds(pl.multiple_of(t * tile, tile), tile)
            parts[slot, k, :, columns] = dot_f32(attended[slot], out_w[:, columns]).astype(BF16)

        @pl.when(slot == 0)
        def _():
            swap(k).start()

        @pl.when(slot == 1)
        def _():
            swap(k).wait_recv()
            parts[1, k] = parts[1, k] + from_core[k]

        @pl.when(n == 1)
        def _():
            sent[0].start()
            sent[1].start()

        @pl.when(n == 3)
        def _():
            sent[2].start()

        @pl.when(n == 5)
        def _():
            sent[3].start()

    sent[0].wait_recv()
    parts[1, 2, low] = parts[1, 2, low] + from_across[0]
    sent[4].start()
    sent[1].wait_recv()
    parts[1, 1, high] = parts[1, 1, high] + from_down[0]
    sent[5].start()
    move.pass_corner()
    sent[2].wait_recv()
    sent[3].wait_recv()
    sent[4].wait_recv()
    out_ref[low] = (
        parts[1, 3, low].astype(F32) + from_across[1].astype(F32) + last_down[...].astype(F32)
    )
    sent[5].wait_recv()
    out_ref[high] = (
        parts[1, 3, high].astype(F32) + from_down[1].astype(F32) + last_across[...].astype(F32)
    )
    move.arrive()
    cot_sender.finish()
    for k in range(4):
        swap(k).wait_send()
    sender.finish()
    for n in (6, 7):
        for store in stores(n):
            store.wait()


def attend(hidden, gain, qkv, tables, codes, cotangent, w_output, collective_id):
    members, length, width = hidden.shape
    wide, q_wide = (GROUPS + 2) * HD, GROUPS * HD
    half = length // 2
    three = [(length, width), (length, wide), (length, q_wide)]
    return pl.pallas_call(
        attend_kernel,
        out_shape=[jax.ShapeDtypeStruct((length, width), F32)]
        + [jax.ShapeDtypeStruct((members,) + shape, BF16) for shape in three]
        + [jax.ShapeDtypeStruct((8,) + cotangent.shape, BF16)],
        in_specs=[HBM] + [VM] * 7 + [HBM],
        out_specs=[VM] + [HBM] * 4,
        scratch_shapes=[pltpu.VMEM((2, length, width), BF16)]
        + [pltpu.VMEM((2,) + shape, BF16) for shape in three]
        + [
            pltpu.VMEM((q_wide, width), BF16),
            pltpu.VMEM((2, 4, length, width), BF16),
            pltpu.VMEM((4, length, width), BF16),
            pltpu.VMEM((2, half, width), BF16),
            pltpu.VMEM((2, half, width), BF16),
            pltpu.VMEM((half, width), BF16),
            pltpu.VMEM((half, width), BF16),
            pltpu.SemaphoreType.DMA((2,)),
            pltpu.SemaphoreType.DMA,
            pltpu.SemaphoreType.DMA((2, 3)),
            pltpu.SemaphoreType.DMA,
            pltpu.SemaphoreType.DMA((4,)),
            pltpu.SemaphoreType.DMA((4,)),
            pltpu.SemaphoreType.DMA((6,)),
            pltpu.SemaphoreType.DMA((6,)),
            pltpu.SemaphoreType.DMA((13,)),
            pltpu.SemaphoreType.DMA((13,)),
        ],
        compiler_params=params(collective_id, 60),
        cost_estimate=link_cost(70),
    )(
        hidden, gain, qkv, *tables, codes[:, None, :], codes[:, :, None], cotangent, w_output
    )


def attend_back_kernel(
    out_grad_ref, w_ref, heads_ref, attended_ref, cos_ref, sin_ref, row_ref, col_ref,
    grad_ref, w_grad_ref, total,
):
    at = pl.program_id(0)
    out_grad = out_grad_ref[0]
    heads = heads_ref[0]
    attended_grad = lax.dot_general(
        out_grad, w_ref[...], (((1,), (1,)), ((), ())), preferred_element_type=F32
    ).astype(BF16)
    term = lax.dot_general(
        attended_ref[0], out_grad, (((0,), (0,)), ((), ())), preferred_element_type=F32
    )

    @pl.when(at == 0)
    def _():
        total[...] = term

    @pl.when(at > 0)
    def _():
        total[...] = total[...] + term

    @pl.when(at == pl.num_programs(0) - 1)
    def _():
        w_grad_ref[...] = total[...].astype(BF16)

    allowed = allowed_pairs(row_ref.at[0], col_ref.at[0])
    keys = heads[:, GROUPS * HD : (GROUPS + 1) * HD]
    values = heads[:, (GROUPS + 1) * HD :]
    grads = []
    key_grad, value_grad = None, None
    for h in range(GROUPS):
        lanes = slice(h * HD, (h + 1) * HD)
        query, head_grad = heads[:, lanes], attended_grad[:, lanes]
        probs = head_probs(query, keys, allowed)
        prob_grad = lax.dot_general(
            head_grad, values, (((1,), (1,)), ((), ())), preferred_element_type=F32
        )
        row_dot = jnp.sum(probs * prob_grad, axis=-1, keepdims=True)
        score_grad = (probs * (prob_grad - row_dot)).astype(BF16)
        grads.append(dot_f32(score_grad, keys) * SCORE_SCALE)
        key_part = lax.dot_general(
            score_grad, query, (((0,), (0,)), ((), ())), preferred_element_type=F32
        )
        value_part = lax.dot_general(
            probs.astype(BF16), head_grad, (((0,), (0,)), ((), ())), preferred_element_type=F32
        )
        key_grad = key_part if key_grad is None else key_grad + key_part
        value_grad = value_part if value_grad is None else value_grad + value_part
    grads += [key_grad * SCORE_SCALE, value_grad]
    grad_ref[0] = turn(jnp.concatenate(grads, axis=1), cos_ref, sin_ref, True).astype(BF16)


def attend_back(out_grad, out_rows, heads, attended, tables, codes):
    members, length, width = out_grad.shape
    wide, q_wide = heads.shape[2], attended.shape[2]

    def one(columns):
        return pl.BlockSpec((1, length, columns), lambda i: (i, 0, 0))

    def fixed(*shape):
        return pl.BlockSpec(shape, lambda i: (0,) * len(shape))

    return pl.pallas_call(
        attend_back_kernel,
        grid=(members,),
        out_shape=[
            jax.ShapeDtypeStruct((members, length, wide), BF16),
            jax.ShapeDtypeStruct((q_wide, width), BF16),
        ],
        in_specs=[
            one(width), fixed(q_wide, width), one(wide), one(q_wide), fixed(length, wide),
            fixed(length, wide), pl.BlockSpec((1, 1, length), lambda i: (i, 0, 0)), one(1),
        ],
        out_specs=[one(wide), fixed(q_wide, width)],
        scratch_shapes=[pltpu.VMEM((q_wide, width), F32)],
        compiler_params=pltpu.CompilerParams(vmem_limit_bytes=48 << 20),
        cost_estimate=link_cost(25),
    )(out_grad, out_rows, heads, attended, *tables, codes[:, None, :], codes[:, :, None])


def cast_rows_kernel(x_ref, out_ref):
    out_ref[...] = x_ref[0, 0].astype(F32)


def cast_rows(spread):
    reps, subs, rows, columns = spread.shape
    return pl.pallas_call(
        cast_rows_kernel,
        grid=(subs, reps),
        out_shape=jax.ShapeDtypeStruct((reps * subs * rows, columns), F32),
        in_specs=[pl.BlockSpec((1, 1, rows, columns), lambda s, r: (r, s, 0, 0))],
        out_specs=pl.BlockSpec((rows, columns), lambda s, r: (s * reps + r, 0)),
        cost_estimate=link_cost(8),
    )(spread)


def cast_columns_kernel(x_ref, out_ref):
    _, subs, owners, _, columns = x_ref.shape
    for j in range(owners):
        for s in range(subs):
            at = (j * subs + s) * columns
            out_ref[:, at : at + columns] = x_ref[0, s, j].astype(F32)


def cast_columns(handed, columns):
    parts, subs, owners, rows, _ = handed.shape
    wide = owners * subs * columns
    cuts = max(1, rows // 64)
    block = (1, subs, owners, rows // cuts, columns)
    return pl.pallas_call(
        cast_columns_kernel,
        grid=(parts, cuts),
        out_shape=jax.ShapeDtypeStruct((parts * rows, wide), F32),
        in_specs=[pl.BlockSpec(block, lambda r, h: (r, 0, 0, h, 0))],
        out_specs=pl.BlockSpec((rows // cuts, wide), lambda r, h: (r * cuts + h, 0)),
        compiler_params=pltpu.CompilerParams(vmem_limit_bytes=48 << 20),
        cost_estimate=link_cost(8),
    )(handed)


def cast_heads_kernel(q_ref, kv_ref, q_out, k_out, v_out):
    _, subs, owners, _, columns = q_ref.shape
    for j in range(owners):
        for s in range(subs):
            at = (j * subs + s) * columns
            q_out[:, at : at + columns] = q_ref[0, s, j].astype(F32)
        pair = [kv_ref[0, s, j].astype(F32) for s in range(subs)]
        wide = HD * subs
        at = j * wide
        k_out[:, at : at + wide] = jnp.concatenate([p[:, :HD] for p in pair], axis=1)
        v_out[:, at : at + wide] = jnp.concatenate([p[:, HD:] for p in pair], axis=1)


def cast_heads(handed, skip):
    parts, subs, owners, rows, _ = handed.shape
    q_wide, k_wide = GROUPS * HD, 2 * HD
    members = owners * subs

    def source(wide, at):
        return pl.BlockSpec((1, subs, owners, rows, wide), lambda r: (r, 0, 0, 0, at // wide))

    def shape(wide):
        return jax.ShapeDtypeStruct((parts * rows, wide), F32)

    widths = (members * q_wide, members * HD, members * HD)
    return pl.pallas_call(
        cast_heads_kernel,
        grid=(parts,),
        out_shape=[shape(w) for w in widths],
        in_specs=[source(q_wide, skip), source(k_wide, skip + q_wide)],
        out_specs=[pl.BlockSpec((rows, w), lambda r: (r, 0)) for w in widths],
        compiler_params=pltpu.CompilerParams(vmem_limit_bytes=48 << 20),
        cost_estimate=link_cost(5),
    )(handed, handed)


def tally_kernel(x_ref, out_ref, plane, planes, total, sems, plane_sems):
    rep, core, own, _, _, _ = plane_position()
    reps = planes.shape[0]
    mates = [(c, j) for c in range(2) for j in range(4)][1:]
    others = [(rep, (core + c) % 2, (own + j) % 4) for c, j in mates]
    above = [((rep + r) % reps, core, own) for r in range(1, reps)]
    meet(others + above)
    sender = Sender(sems.at[0], sems.at[1])
    for device in others:
        sender.send(x_ref, plane.at[core * 4 + own], device)
    plane[core * 4 + own] = x_ref[...]
    for copy in sender.copies:
        copy.wait_recv()
    mine = plane[0]
    for k in range(1, 8):
        mine = mine + plane[k]
    total[...] = mine
    climber = Sender(plane_sems.at[0], plane_sems.at[1])
    for device in above:
        climber.send(total, planes.at[rep], device)
    planes[rep] = mine
    for copy in climber.copies:
        copy.wait_recv()
    whole = planes[0]
    for k in range(1, reps):
        whole = whole + planes[k]
    out_ref[...] = whole
    sender.finish()
    climber.finish()


def tally_all(values, reps, collective_id):
    size = values.shape[0]
    rows = -(-size // 1024) * 8
    padded = jnp.pad(values, (0, rows * 128 - size)).reshape(rows, 128)
    block = pltpu.VMEM((rows, 128), F32)
    summed = pl.pallas_call(
        tally_kernel,
        out_shape=jax.ShapeDtypeStruct((rows, 128), F32),
        in_specs=[VM],
        out_specs=VM,
        scratch_shapes=[
            pltpu.VMEM((8, rows, 128), F32),
            pltpu.VMEM((reps, rows, 128), F32),
            block,
            pltpu.SemaphoreType.DMA((2, 7)),
            pltpu.SemaphoreType.DMA((2, reps - 1)),
        ],
        compiler_params=params(collective_id),
        cost_estimate=link_cost(10),
    )(padded)
    return summed.reshape(-1)[:size]


def column_blocks(weight, owners, subs):
    rows, columns = weight.shape
    blocked = weight.reshape(rows, owners, subs, columns // (owners * subs))
    mine = lax.dynamic_index_in_dim(blocked, lax.axis_index("sub"), axis=2, keepdims=False)
    return jnp.swapaxes(mine, 0, 1)


def regroup_columns(weights, owners, subs):
    blocks = jnp.concatenate([column_blocks(w, owners, subs) for w in weights], axis=-1)
    moved = lax.all_to_all(blocks, "fsdp", split_axis=0, concat_axis=0, tiled=True)
    return moved.reshape(-1, moved.shape[-1])


def row_block(weight, subs):
    rows = weight.shape[0] // subs
    return lax.dynamic_slice_in_dim(weight, lax.axis_index("sub") * rows, rows, axis=0)


def gather_tokens(block):
    return lax.all_gather(block, ("sub", "fsdp"), axis=0, tiled=True)


def scatter_tokens(partial):
    return lax.psum_scatter(partial, ("sub", "fsdp"), scatter_dimension=0, tiled=True)


def sum_planes(term):
    return lax.psum_scatter(term, "rep", scatter_dimension=0, tiled=True)


def spread_planes(piece):
    rep, subs = lax.axis_size("rep"), lax.axis_size("sub")
    spread = lax.all_gather(piece, ("rep", "sub"), axis=0, tiled=False)
    return spread.reshape((rep, subs) + piece.shape)


def owner_major(term):
    owners, rep = lax.axis_size("fsdp"), lax.axis_size("rep")
    rows, columns = term.shape
    blocked = jnp.swapaxes(term.reshape(owners, rep, rows // (owners * rep), columns), 0, 1)
    return blocked.reshape(rows, columns)


def to_owners(piece):
    blocked = piece.reshape(lax.axis_size("fsdp"), -1, piece.shape[1])
    return lax.all_to_all(blocked, "fsdp", split_axis=0, concat_axis=0, tiled=True)


def place_columns(spread):
    reps, subs, owners, rows, columns = spread.shape
    part = jnp.transpose(spread, (0, 3, 2, 1, 4))
    return part.reshape(reps * rows, owners * subs * columns).astype(F32)


def shards(
    kernels,
    hidden_in,
    segment_ids,
    valid_mask,
    cotangent,
    norm_attn,
    w_query,
    w_key,
    w_value,
    w_output,
    norm_mlp,
    w_gate,
    w_up,
    w_down,
):
    owners, subs, reps = lax.axis_size("fsdp"), lax.axis_size("sub"), lax.axis_size("rep")
    members = owners * subs
    length, width = hidden_in.shape[1:]
    tokens = members * length
    q_width, k_width = GROUPS * HD, HD

    def gathered(blocks, collective_id, jobs=()):
        if kernels:
            outs = list(gather_plane(blocks, collective_id, jobs, reps))
        else:
            outs = [gather_tokens(block) for block in blocks]
        return [o.reshape(tokens, -1) for o in outs[: len(blocks)]] + outs[len(blocks) :]

    def scattered(xs, w, turned, collective_id, jobs=()):
        if kernels:
            return product_scatter(xs, w, turned, collective_id, jobs, reps)
        x = jnp.concatenate(xs, axis=1)
        product = contract_cols(x, w) if turned else dot_f32(x, row_block(w, subs))
        return [scatter_tokens(product.astype(BF16)).astype(F32)]

    codes = segment_ids * 2 + valid_mask
    gains = jnp.stack([norm_attn, norm_mlp])
    result_grad = cotangent[0].astype(F32)
    mlp_out_low = (RESIDUAL_SCALE * result_grad).astype(BF16)
    if kernels:
        quarter = quarter_columns(w_gate, w_up, reps, 0)
        gate_up = lax.all_gather(quarter, "rep", axis=1, tiled=True).reshape(width, -1)
        hidden_tied = after(hidden_in[0], quarter)
        hidden_low, codes, gains, heads_all = start_plane(
            hidden_tied, codes, gains, w_query, w_key, w_value, 1
        )
        hidden_low = hidden_low.reshape(tokens, width)
        codes = codes.reshape(members, length)
        gains = jnp.swapaxes(gains, 0, 1).reshape(2, width)
        heads_all = heads_all.reshape(width, -1)
    else:
        gains = lax.all_gather(gains, "fsdp", axis=1, tiled=True)
        codes = gather_tokens(codes)
        hidden_low = gather_tokens(hidden_in[0])
        qkv = regroup_columns((w_query, w_key, w_value), owners, subs)
        gate_up = regroup_columns((w_gate, w_up), owners, subs)
    gain_attn = gains[0].astype(F32)
    gain_mlp = gains[1].astype(F32)
    ff = gate_up.shape[1] // 2

    if kernels:
        tables = turn_tables(length)
        attn_branch, normed_one, heads, attended, mlp_out_grad = attend(
            hidden_low.reshape(members, length, width), gain_attn[None], heads_all, tables, codes,
            mlp_out_low, w_output, 9,
        )
        normed_one = normed_one.reshape(tokens, width)
        mlp_out_grad = mlp_out_grad.reshape(tokens, width)
        attended = attended.reshape(tokens, q_width)
        heads_all = after(heads_all, normed_one)
        core_at = lax.axis_index("sub") * HD
        key_cols = lax.dynamic_slice_in_dim(heads_all, q_width + core_at, HD, axis=1)
        value_cols = lax.dynamic_slice_in_dim(heads_all, q_width + 2 * HD + core_at, HD, axis=1)
        qkv = jnp.concatenate([heads_all[:, :q_width], key_cols, value_cols], axis=1)
    else:
        cos_table, sin_table = rope_tables(length, HD)
        hidden_all = hidden_low.astype(F32)
        normed_one = (hidden_all * row_scale(hidden_all) * gain_attn).astype(BF16)
        projected = dot_f32(normed_one, qkv)
        cos_heads = cos_table[None, :, None, :]
        sin_heads = sin_table[None, :, None, :]
        per_seq = projected.reshape(members, length, GROUPS + 2, HD)
        queries = rotate(per_seq[:, :, :GROUPS], cos_heads, sin_heads).astype(BF16)
        keys = rotate(per_seq[:, :, GROUPS : GROUPS + 1], cos_heads, sin_heads).astype(BF16)[:, :, 0]
        values = per_seq[:, :, GROUPS + 1].astype(BF16)

        segments, validity = codes // 2, codes % 2
        row_index = jnp.arange(length, dtype=jnp.int32)[:, None]
        col_index = jnp.arange(length, dtype=jnp.int32)[None, :]
        allowed = (
            (segments[:, :, None] == segments[:, None, :])
            & (col_index <= row_index)
            & ((validity[:, None, :] == 1) | (col_index == row_index))
        )[:, None]
        scores = jnp.einsum("stgd,sud->sgtu", queries, keys, preferred_element_type=F32) * SCORE_SCALE
        scores = jnp.where(allowed, scores, MASKED_SCORE)
        shifted = jnp.exp(scores - jnp.max(scores, axis=-1, keepdims=True))
        probs = shifted / jnp.sum(shifted, axis=-1, keepdims=True)
        probs_low = probs.astype(BF16)
        attended = jnp.einsum("sgtu,sud->stgd", probs_low, values, preferred_element_type=F32)
        attended = attended.reshape(tokens, q_width).astype(BF16)
    if not kernels:
        (attn_branch,) = scattered([attended], w_output, False, 2)

    hidden = hidden_in[0].astype(F32)
    scale_one = row_scale(hidden)
    unit_one = hidden * scale_one
    middle = hidden + RESIDUAL_SCALE * attn_branch
    scale_two = row_scale(middle)
    unit_two = middle * scale_two
    normed_own = (unit_two * gain_mlp).astype(BF16)
    if kernels:
        normed_two, gate_up_proj, mixed_act, down_w_grad = mlp_plane(
            normed_own, gate_up, mlp_out_grad.reshape(members, length, width), 3
        )
        normed_two = normed_two.reshape(tokens, width)
    else:
        normed_two, mlp_out_grad = gathered([normed_own, mlp_out_low], 3)
        gate_up_proj = dot_f32(normed_two, gate_up)
    gate_proj, up_proj = gate_up_proj[:, :ff], gate_up_proj[:, ff:]
    sigma = jax.nn.sigmoid(gate_proj)
    silu_gate = gate_proj * sigma
    if not kernels:
        mixed_act = (silu_gate * up_proj).astype(BF16)
        down_w_grad = contract_rows(mixed_act, mlp_out_grad).astype(BF16)
    down_w_piece = sum_planes(down_w_grad)
    mixed_grad = contract_cols(after(mlp_out_grad, down_w_grad), row_block(w_down, subs))
    slope = sigma * (1.0 + gate_proj * (1.0 - sigma))
    gate_grad = (mixed_grad * up_proj * slope).astype(BF16)
    up_grad = (mixed_grad * silu_gate).astype(BF16)
    gate_w_grad = contract_rows(normed_two, gate_grad).astype(BF16)
    up_w_grad = contract_rows(normed_two, up_grad).astype(BF16)
    gate_sum = sum_planes(owner_major(gate_w_grad))
    gate_up_grad = [after(gate_grad, gate_w_grad, up_w_grad), up_grad]
    (normed_two_grad,) = scattered(gate_up_grad, gate_up, True, 4)
    gain_mlp_grad, middle_part = norm_backward(normed_two_grad, scale_two, unit_two, gain_mlp)
    middle_grad = result_grad + middle_part

    attn_out_low = (RESIDUAL_SCALE * middle_grad).astype(BF16)
    passed = [KeepJob(down_w_piece)] if kernels else []
    attn_out_grad, *passed = gathered([attn_out_low], 5, passed)
    down_spread = spread_planes(passed[0] if kernels else down_w_piece)
    if kernels:
        qkv_grad, output_w_grad = attend_back(
            attn_out_grad.reshape(members, length, width), row_block(w_output, subs), heads,
            attended.reshape(members, length, q_width), tables, codes,
        )
        qkv_grad = qkv_grad.reshape(tokens, q_width + 2 * k_width)
    else:
        attended_grad = contract_cols(attn_out_grad, row_block(w_output, subs)).astype(BF16)
        output_w_grad = contract_rows(attended, attn_out_grad).astype(BF16)
        heads_grad = attended_grad.reshape(members, length, GROUPS, HD)
        prob_grad = jnp.einsum("stgd,sud->sgtu", heads_grad, values, preferred_element_type=F32)
        row_dot = jnp.sum(probs * prob_grad, axis=-1, keepdims=True)
        score_grad = (probs * (prob_grad - row_dot)).astype(BF16)
        query_grad = (
            jnp.einsum("sgtu,sud->stgd", score_grad, keys, preferred_element_type=F32) * SCORE_SCALE
        )
        key_grad = (
            jnp.einsum("sgtu,stgd->sud", score_grad, queries, preferred_element_type=F32) * SCORE_SCALE
        )
        value_grad = jnp.einsum("sgtu,stgd->sud", probs_low, heads_grad, preferred_element_type=F32)
        qkv_grad = jnp.concatenate(
            [
                rotate(query_grad, cos_heads, -sin_heads),
                rotate(key_grad[:, :, None], cos_heads, -sin_heads),
                value_grad[:, :, None],
            ],
            axis=2,
        )
        qkv_grad = qkv_grad.reshape(tokens, q_width + 2 * k_width).astype(BF16)
    qkv_tied = after(qkv_grad, output_w_grad)
    gate_job = [KeepJob(gate_sum)] if kernels else []
    normed_one_grad, *gate_kept = scattered([qkv_tied], qkv, True, 6, gate_job)
    qkv_grad = after(qkv_grad, normed_one_grad)
    qkv_w_grad = contract_rows(normed_one, qkv_grad).astype(BF16)
    gain_attn_grad, hidden_part = norm_backward(normed_one_grad, scale_one, unit_one, gain_attn)
    input_grad = (middle_grad + hidden_part).astype(BF16)

    mixed_tied = after(mixed_act, normed_one_grad, qkv_w_grad, down_spread)
    last_jobs = []
    if kernels:
        up_job = SumJob(
            [up_w_grad, qkv_w_grad], 4, 4, reps,
            {1: range(4), 2: range(4, 8), 3: range(8, 12), 4: range(12, 17)},
        )
        output_job = SumJob([output_w_grad], 1, 2, reps, {4: range(3)})
        last_jobs = [up_job, output_job, ExchangeJob(gate_kept[0])]
        last_jobs += [HandJob(up_job, reps, 4), HandJob(output_job, reps, 2)]
    mlp_branch, *last = scattered([mixed_tied], w_down, False, 7, last_jobs)
    result = middle + RESIDUAL_SCALE * mlp_branch

    validity_own = valid_mask[0].astype(F32)[:, None]
    squares = [
        jnp.sum(tensor * tensor * validity_own)
        for tensor in (hidden, middle, result, attn_branch, mlp_branch)
    ]
    tally = jnp.concatenate(
        [gain_attn_grad, gain_mlp_grad, jnp.stack(squares + [jnp.sum(validity_own)])]
    )
    tally = tally_all(tally, reps, 8) if kernels else lax.psum(tally, ("rep", "sub", "fsdp"))
    part = width // owners
    start = lax.axis_index("fsdp") * part
    gain_attn_out = lax.dynamic_slice_in_dim(tally, start, part)
    gain_mlp_out = lax.dynamic_slice_in_dim(tally, width + start, part)
    statistics = jnp.sqrt(tally[2 * width : 2 * width + 5] / (tally[2 * width + 5] * width))

    if kernels:
        gate_piece, up_handed, output_handed = last
        gate_spread = spread_planes(gate_piece)
        down_out = cast_rows(down_spread)
        output_out = cast_rows(output_handed.reshape((2, 2) + output_handed.shape[3:]))
        gate_out, up_out = cast_columns(gate_spread, ff), cast_columns(up_handed, ff)
        query_out, key_out, value_out = cast_heads(up_handed, ff)
    else:
        down_out, output_out = (
            jnp.swapaxes(s, 0, 1).reshape(-1, width).astype(F32)
            for s in (down_spread, spread_planes(sum_planes(output_w_grad)))
        )
        gate_spread, up_spread, qkv_spread = (
            spread_planes(to_owners(g))
            for g in (
                gate_sum,
                sum_planes(owner_major(up_w_grad)),
                sum_planes(owner_major(qkv_w_grad)),
            )
        )
        gate_out, up_out = place_columns(gate_spread), place_columns(up_spread)
        query_out = place_columns(qkv_spread[..., :q_width])
        key_out = place_columns(qkv_spread[..., q_width : q_width + k_width])
        value_out = place_columns(qkv_spread[..., q_width + k_width :])
    return (
        result.astype(BF16)[None],
        input_grad[None],
        gain_attn_out,
        query_out,
        key_out,
        value_out,
        output_out,
        gain_mlp_out,
        gate_out,
        up_out,
        down_out,
        statistics,
    )


def solution(mesh):
    fsdp = mesh.shape["fsdp"]
    subs = max(1, KV // fsdp)
    rep = mesh.shape["dp"] // subs
    kernels = fsdp == 4 and subs == 2 and rep >= 3
    plane_mesh = Mesh(mesh.devices.reshape(rep, subs, fsdp), ("rep", "sub", "fsdp"))
    batch = ("rep", "sub", "fsdp")
    return jax.shard_map(
        functools.partial(shards, kernels),
        mesh=plane_mesh,
        in_specs=(
            P(batch, None, None),
            P(batch, None),
            P(batch, None),
            P(batch, None, None),
            P("fsdp"),
            P("fsdp", None),
            P("fsdp", None),
            P("fsdp", None),
            P("fsdp", None),
            P("fsdp"),
            P("fsdp", None),
            P("fsdp", None),
            P("fsdp", None),
        ),
        out_specs=(
            P(batch, None, None),
            P(batch, None, None),
            P("fsdp"),
            P("fsdp", None),
            P("fsdp", None),
            P("fsdp", None),
            P("fsdp", None),
            P("fsdp"),
            P("fsdp", None),
            P("fsdp", None),
            P("fsdp", None),
            P(),
        ),
        check_vma=False,
    )
```
